128 devices in a mesh: ctx: 16 (over x_lo, z, core), head: 8 (over x_hi, y).
Axes of the slice: x: 4 (x_hi: 2, x_lo: 2; x = x_hi * 2 + x_lo), y: 4, z: 4, core: 2. Of those that a mesh axis runs over, the one named last changes fastest.
Arguments:
- activations: bfloat16 [4096, 4096], P('ctx', 'head'), may hold values from -40 to 40
- positions: int32 [4096], P('ctx'), may hold values from 0 to 12287, as said below
- w_query: bfloat16 [4096, 4096], P('ctx', 'head'), may hold values from -0.09375 to 0.09375
- w_key: bfloat16 [4096, 4096], P('ctx', 'head'), may hold values from -0.09375 to 0.09375
- w_value: bfloat16 [4096, 4096], P('ctx', 'head'), may hold values from -0.09375 to 0.09375
- conv_kernel: float32 [32, 66], P('head'), may hold values from -0.6 to 0.6
- head_mix: float32 [32, 4], P('head'), may hold values from -0.45 to 1.45
- out_gain: float32 [4096], P('head'), may hold values from 0.1 to 1.9
- w_out: bfloat16 [4096, 4096], P('head', 'ctx'), may hold values from -0.09375 to 0.09375
Outputs:
- attended: bfloat16 [4096, 4096], P('ctx', 'head')
The draws below stay inside these ranges and needn't reach their ends.
Inputs may be any that keep to these rules, and one draw needn't show every extreme that they name: `positions`: strictly increasing along the tokens; the first token's is 0 and the last token's is 12287.
All inputs are finite; a program needn't handle non-finite values.
Results may differ from the reference program's by a relative error of at most 0.018.
Values may be sent and summed in bfloat16 or wider, within the bound.
A program may use at most 128 MiB of HBM per device.

```python
import math
import jax
import jax.numpy as jnp
from jax import lax

D = 4096
HEADS = 32
HD = 128
GROUP = 4
CQ = 6
CK = 11
KB = 512
TOKEN_COUNT = 4096


def draw_activations(key, part):
    key_base = jax.random.fold_in(key, 0)
    values = jnp.clip(jax.random.normal(key_base, (TOKEN_COUNT, D), jnp.float32), -5.0, 5.0)
    return values.astype(jnp.bfloat16)


def draw_positions(key, part):
    steps_drawn = jax.random.randint(key, (TOKEN_COUNT,), 1, 4)
    walked = (jnp.cumsum(steps_drawn) - 1).astype(jnp.int32)
    walked = walked.at[0].set(0)
    return walked.at[TOKEN_COUNT - 1].set(3 * TOKEN_COUNT - 1)


def draw_head_mix(key, part):
    diagonal = ((jnp.arange(HEADS) % GROUP)[:, None] == jnp.arange(GROUP)[None, :]).astype(jnp.float32)
    noise = jax.random.uniform(key, (HEADS, GROUP), jnp.float32, -0.3, 0.3)
    return diagonal + noise


def block_levels(own_key, shape, pieces, least, high):
    loudness, own = 1.0, jax.random.fold_in(own_key, 6)
    for position, parts in pieces:
        draws = jnp.exp(jax.random.uniform(jax.random.fold_in(own, position), (parts,), jnp.float32, least / len(pieces), high / len(pieces)))
        loudness = loudness * jnp.repeat(draws, shape[position] // parts).reshape([-1 if axis == position else 1 for axis in range(len(shape))])
    return loudness


def gaussian(own_key, extent, scale, bound, shards=(), held_as=jnp.bfloat16):
    drawn = scale * jax.random.normal(own_key, extent, jnp.float32)
    if shards:
        drawn = drawn * block_levels(own_key, extent, shards, -0.22, 0.18)
    return jnp.clip(drawn, -bound, bound).astype(held_as)


def setup_inputs(seed: int = 0) -> dict:
    splits = jax.random.split(jax.random.key(seed), 10)
    activations = draw_activations(jax.random.fold_in(splits[9], 71), 0)
    positions = draw_positions(jax.random.fold_in(splits[9], 71), 0)
    w_query = gaussian(splits[2], (D, HEADS * HD), D ** -0.5, 0.09375, ((0, 16), (1, 8)))
    w_key = gaussian(splits[3], (D, HEADS * HD), D ** -0.5, 0.09375, ((0, 16), (1, 8)))
    w_value = gaussian(splits[4], (D, HEADS * HD), D ** -0.5, 0.09375, ((0, 16), (1, 8)))
    conv_kernel = gaussian(splits[5], (HEADS, CQ * CK), 0.15, 0.6, ((0, 8),), jnp.float32)
    head_mix = draw_head_mix(jax.random.fold_in(splits[9], 71), 0)
    out_gain = jnp.clip(1.0 + 0.18 * jax.random.normal(splits[7], (HEADS * HD,), jnp.float32), 0.1, 1.9)
    w_out = gaussian(splits[8], (HEADS * HD, D), (HEADS * HD) ** -0.5, 0.09375, ((0, 8), (1, 16)))
    return dict(activations=activations, positions=positions, w_query=w_query, w_key=w_key, w_value=w_value, conv_kernel=conv_kernel, head_mix=head_mix, out_gain=out_gain, w_out=w_out)


def rope(projected, positions):
    row_count = projected.shape[0]
    head_count = projected.shape[1] // HD
    shaped = projected.reshape(row_count, head_count, HD)
    half_size = HD // 2
    exponents = jnp.arange(half_size, dtype=jnp.float32) * (2.0 / HD)
    inverse = jnp.exp(-exponents * math.log(500000.0))
    angle = (positions.astype(jnp.float32) * 0.25)[:, None, None] * inverse[None, None, :]
    cosine = jnp.cos(angle)
    sine = jnp.sin(angle)
    lower_half = shaped[..., :half_size]
    upper_half = shaped[..., half_size:]
    rotated_rows = jnp.concatenate([lower_half * cosine - upper_half * sine, upper_half * cosine + lower_half * sine], -1)
    return rotated_rows.reshape(row_count, head_count * HD)

def convolve(masked, kernel, row_count, col_count):
    summed = jnp.zeros((masked.shape[0], row_count, col_count), jnp.float32)
    for lag_q in range(CQ):
        for lag_k in range(CK):
            weight = kernel[:, lag_q * CK + lag_k][:, None, None]
            window = masked[:, CQ - 1 - lag_q:CQ - 1 - lag_q + row_count, CK - 1 - lag_k:CK - 1 - lag_k + col_count]
            summed = summed + weight * window
    return summed

def reference(activations, positions, w_query, w_key, w_value, conv_kernel, head_mix, out_gain, w_out):
    length = TOKEN_COUNT
    groups = HEADS // GROUP
    scale = 1.0 / math.sqrt(HD)
    query = rope(jnp.dot(activations, w_query, preferred_element_type=jnp.float32), positions).astype(jnp.bfloat16)
    key = rope(jnp.dot(activations, w_key, preferred_element_type=jnp.float32), positions).astype(jnp.bfloat16)
    value = jnp.dot(activations, w_value, preferred_element_type=jnp.float32).astype(jnp.bfloat16)
    query_groups = query.reshape(length, groups, GROUP, HD).transpose(1, 0, 2, 3)
    query_groups = jnp.pad(query_groups, ((0, 0), (CQ - 1, 0), (0, 0), (0, 0)))
    key_groups = key.reshape(length, groups, GROUP, HD).transpose(1, 0, 2, 3)
    key_groups = jnp.pad(key_groups, ((0, 0), (CK // 2, CK // 2), (0, 0), (0, 0)))
    value_groups = value.reshape(length, groups, GROUP, HD).transpose(1, 0, 2, 3)
    kernels = conv_kernel.reshape(groups, GROUP, CQ * CK)
    mixes = head_mix.reshape(groups, GROUP, GROUP)

    def one_group(packed):
        query_pad, key_pad, value_cluster, kernel, mixing = packed

        def one_block(start):
            query_ext = lax.dynamic_slice_in_dim(query_pad, start, KB + CQ - 1, 0)
            scores = jnp.einsum('rhd,khd->hrk', query_ext.astype(jnp.float32), key_pad.astype(jnp.float32)) * scale
            prow = start - (CQ - 1) + jnp.arange(KB + CQ - 1, dtype=jnp.int32)
            kcol = jnp.arange(length + CK - 1, dtype=jnp.int32) - CK // 2
            valid = (kcol[None, :] <= prow[:, None]) & (prow[:, None] >= 0)
            masked = jnp.where(valid[None], scores, 0.0)
            conv = convolve(masked, kernel, KB, length)
            irow = start + jnp.arange(KB, dtype=jnp.int32)
            jcol = jnp.arange(length, dtype=jnp.int32)
            logits = jnp.where((jcol[None, :] <= irow[:, None])[None], conv, -jnp.inf)
            probs = jax.nn.softmax(logits, axis=-1)
            mixed_scores = jnp.einsum('ab,bik->aik', mixing, probs).astype(jnp.bfloat16)
            return jnp.einsum('gup,pgb->ugb', mixed_scores.astype(jnp.float32), value_cluster.astype(jnp.float32))
        starts = jnp.arange(length // KB, dtype=jnp.int32) * KB
        return lax.map(one_block, starts)
    outputs = lax.map(one_group, (query_groups, key_groups, value_groups, kernels, mixes))
    head_output = outputs.transpose(1, 2, 0, 3, 4).reshape(length, HEADS, HD)
    rms = jnp.sqrt(lax.optimization_barrier(jnp.mean(head_output * head_output, axis=-1, keepdims=True)) + 1e-05)
    normed = (head_output / rms * out_gain.reshape(HEADS, HD)).astype(jnp.bfloat16).reshape(length, HEADS * HD)
    return jnp.dot(normed, w_out, preferred_element_type=jnp.float32).astype(jnp.bfloat16)
```

```python
import math

import jax
import jax.numpy as jnp
from jax import lax
from jax.experimental import pallas as pl
from jax.experimental.pallas import tpu as pltpu
from jax.sharding import PartitionSpec as P

HD = 128
GROUP = 4
CQ = 6
CK = 11
KB = 512
ROWS = 256
TOKENS = 4096
FRONT = 256
BAND = 10


def passed_along(value, axis, steps):
    count = lax.axis_size(axis)
    leading, last = (max(0, -steps), min(count, count - steps))
    return lax.ppermute(value, axis, [(source, source + steps) for source in range(leading, last)])


def rope(projected, positions):
    row_count = projected.shape[0]
    head_count = projected.shape[1] // HD
    shaped = projected.reshape(row_count, head_count, HD)
    half_size = HD // 2
    exponents = jnp.arange(half_size, dtype=jnp.float32) * (2.0 / HD)
    inverse = jnp.exp(-exponents * math.log(500000.0))
    angle = (positions.astype(jnp.float32) * 0.25)[:, None, None] * inverse[None, None, :]
    cosine = jnp.cos(angle)
    sine = jnp.sin(angle)
    lower_half = shaped[..., :half_size]
    upper_half = shaped[..., half_size:]
    rotated_rows = jnp.concatenate(
        [lower_half * cosine - upper_half * sine, upper_half * cosine + lower_half * sine], -1
    )
    return rotated_rows.reshape(row_count, head_count * HD)


def add_rows(left, piece):
    return jnp.dot(left, piece, preferred_element_type=jnp.float32)


def dot_nt(left, right):
    return lax.dot_general(
        left, right, (((1,), (1,)), ((), ())), preferred_element_type=jnp.float32
    )


def attend_kernel(
    place_ref, kern_ref, mix_ref, q_ref, k_ref, v_ref, gain_ref, o_ref,
    q32, k32, qt, kc, lg, band, acc, tail,
):
    place = place_ref[0]
    r0 = place * ROWS
    blocks = lax.div(place + 2, 2)
    scale = 1.0 / math.sqrt(HD)

    def weight(h, a, c):
        return kern_ref[h, a * CK + c] * scale

    for h in range(GROUP):
        cols = slice(h * HD, (h + 1) * HD)
        q32[h] = q_ref[:, cols].astype(jnp.float32)
        k32[h, :FRONT] = jnp.zeros((FRONT, HD), jnp.float32)
        k32[h, pl.ds(pl.multiple_of(FRONT + blocks * KB, 8), 8)] = jnp.zeros((8, HD), jnp.float32)

    def widen(b, _):
        for h in range(GROUP):
            rows = pl.ds(pl.multiple_of(b * KB, KB), KB)
            dest = pl.ds(pl.multiple_of(FRONT + b * KB, FRONT), KB)
            k32[h, dest] = k_ref[rows, h * HD : (h + 1) * HD].astype(jnp.float32)
        return 0

    lax.fori_loop(0, blocks, widen, 0)

    for h in range(GROUP):

        def mix_lags(r, _, h=h):
            view = q32.at[h, pl.ds(pl.multiple_of(r * 16, 16), 24)]
            lags = [view[8 - a : 24 - a] for a in range(CQ)]
            for c in range(CK):
                total = weight(h, 0, c) * lags[0]
                for a in range(1, CQ):
                    total = total + weight(h, a, c) * lags[a]
                qt[h, pl.ds(pl.multiple_of(r * 16, 16), 16), c * HD : (c + 1) * HD] = total.astype(
                    jnp.bfloat16
                )
            return 0

        lax.fori_loop(0, ROWS // 16, mix_lags, 0)

    def block_logits(b, _):
        for h in range(GROUP):
            slot = h % 2
            view = k32.at[h, pl.ds(pl.multiple_of(FRONT - 8 + b * KB, 8), KB + 16)]
            for c in range(CK):
                start = 8 + CK // 2 - c
                kc[slot, :, c * HD : (c + 1) * HD] = view[start : start + KB].astype(jnp.bfloat16)
            lg[h, :, pl.ds(pl.multiple_of(HD + b * KB, HD), KB)] = dot_nt(qt[h], kc[slot])
        return 0

    lax.fori_loop(0, blocks, block_logits, 0)

    for s in range(2):
        for h in range(GROUP):
            queries = q32[h, s * HD : s * HD + HD + 8].astype(jnp.bfloat16)
            keys = k32[h, pl.ds(pl.multiple_of(FRONT - HD + r0 + s * HD, HD), 2 * HD)]
            scores = dot_nt(queries, keys.astype(jnp.bfloat16))
            apart = (
                lax.broadcasted_iota(jnp.int32, scores.shape, 0)
                - lax.broadcasted_iota(jnp.int32, scores.shape, 1)
                + (HD - 8)
            )
            kept = jnp.where((apart >= 0) & (apart <= 24), scores, 0.0)
            band[s * GROUP + h, 0] = kept[:, :HD]
            band[s * GROUP + h, 1] = kept[:, HD:]

    row_in = lax.broadcasted_iota(jnp.int32, (8, HD), 0)
    col_in = lax.broadcasted_iota(jnp.int32, (8, HD), 1)

    def taps(h, lags, width):
        total = None
        for c in range(CK):
            part = weight(h, 0, c) * lags[0]
            for a in range(1, CQ):
                part = part + weight(h, a, c) * lags[a]
            shift = (c - CK // 2) % width
            part = pltpu.roll(part, shift, 1) if shift else part
            total = part if total is None else total + part
        return total

    for s in range(2):
        for h in range(GROUP):
            here = pl.ds(pl.multiple_of(HD + r0 + s * HD, HD), HD)
            prior = pl.ds(pl.multiple_of(r0 + s * HD, HD), HD)

            for k in range(2):
                lags = [
                    jnp.concatenate(
                        [
                            band[s * GROUP + h, t, 8 * k + 8 - a : 8 * k + 16 - a]
                            for t in range(2)
                        ],
                        1,
                    )
                    for a in range(CQ)
                ]
                direct = taps(h, lags, 2 * HD)
                rows = slice(s * HD + 8 * k, s * HD + 8 * k + 8)
                apart = 8 * k + row_in - col_in
                lg[h, rows, prior] = jnp.where(
                    apart + HD >= BAND, lg[h, rows, prior], direct[:, :HD]
                )
                lg[h, rows, here] = jnp.where(
                    apart >= BAND,
                    lg[h, rows, here],
                    jnp.where(apart >= 0, direct[:, HD:], -jnp.inf),
                )

            def one_tile(k, _, s=s, h=h, here=here):
                view = band.at[s * GROUP + h, 1, pl.ds(pl.multiple_of(8 * k, 8), 16)]
                direct = taps(h, [view[8 - a : 16 - a] for a in range(CQ)], HD)
                rows = pl.ds(pl.multiple_of(s * HD + 8 * k, 8), 8)
                apart = 8 * k + row_in - col_in
                lg[h, rows, here] = jnp.where(
                    apart >= BAND,
                    lg[h, rows, here],
                    jnp.where(apart >= 0, direct, -jnp.inf),
                )
                return 0

            lax.fori_loop(2, HD // 8, one_tile, 0)

    for h in range(GROUP):
        lg[h, :HD, pl.ds(pl.multiple_of(2 * HD + r0, HD), HD)] = jnp.full(
            (HD, HD), -jnp.inf, jnp.float32
        )

    @pl.when(lax.rem(place, 2) == 0)
    def _():
        for h in range(GROUP):
            lg[h, :, pl.ds(pl.multiple_of(3 * HD + r0, HD), ROWS)] = jnp.full(
                (ROWS, ROWS), -jnp.inf, jnp.float32
            )

    for g in range(GROUP):

        def peak_of(b, peak, g=g):
            block = lg[g, :, pl.ds(pl.multiple_of(HD + b * KB, HD), KB)]
            for t in range(KB // HD):
                peak = jnp.maximum(peak, block[:, t * HD : (t + 1) * HD])
            return peak

        peak = lax.fori_loop(0, blocks, peak_of, jnp.full((ROWS, HD), -jnp.inf, jnp.float32))
        peak = jnp.max(peak, axis=1, keepdims=True)

        def weigh(b, mass, g=g, peak=peak):
            block = lg[g, :, pl.ds(pl.multiple_of(HD + b * KB, HD), KB)]
            probs = jnp.exp(block - peak)
            for t in range(KB // HD):
                mass = mass + probs[:, t * HD : (t + 1) * HD]
            values = v_ref[pl.ds(pl.multiple_of(b * KB, KB), KB), :]
            piece = jnp.dot(probs.astype(jnp.bfloat16), values, preferred_element_type=jnp.float32)

            @pl.when(b == 0)
            def _():
                acc[g] = piece

            @pl.when(b > 0)
            def _():
                acc[g] = acc[g] + piece

            return mass

        mass = lax.fori_loop(0, blocks, weigh, jnp.zeros((ROWS, HD), jnp.float32))
        tail[g] = jnp.broadcast_to(1.0 / jnp.sum(mass, axis=1, keepdims=True), (ROWS, HD))

    for h in range(GROUP):
        cols = slice(h * HD, (h + 1) * HD)
        total = mix_ref[h, 0] * (acc[0, :, cols] * tail[0])
        for g in range(1, GROUP):
            total = total + mix_ref[h, g] * (acc[g, :, cols] * tail[g])
        rms = jnp.sqrt(jnp.mean(total * total, axis=1, keepdims=True) + 1e-05)
        o_ref[:, cols] = (total / rms * gain_ref[:, cols]).astype(jnp.bfloat16)


def attend(place, query_ext, keys, values, kernel, mixing, gain):
    smem = pl.BlockSpec(memory_space=pltpu.SMEM)
    vmem = pl.BlockSpec(memory_space=pltpu.VMEM)
    return pl.pallas_call(
        attend_kernel,
        out_shape=jax.ShapeDtypeStruct((ROWS, GROUP * HD), jnp.bfloat16),
        in_specs=[smem, smem, smem, vmem, vmem, vmem, vmem],
        out_specs=vmem,
        scratch_shapes=[
            pltpu.VMEM((GROUP, ROWS + 8, HD), jnp.float32),
            pltpu.VMEM((GROUP, FRONT + TOKENS + 16, HD), jnp.float32),
            pltpu.VMEM((GROUP, ROWS, CK * HD), jnp.bfloat16),
            pltpu.VMEM((2, KB, CK * HD), jnp.bfloat16),
            pltpu.VMEM((GROUP, ROWS, HD + TOKENS), jnp.float32),
            pltpu.VMEM((2 * GROUP, 2, HD + 8, HD), jnp.float32),
            pltpu.VMEM((GROUP, ROWS, GROUP * HD), jnp.float32),
            pltpu.VMEM((GROUP, ROWS, HD), jnp.float32),
        ],
        compiler_params=pltpu.CompilerParams(vmem_limit_bytes=62 * 1024 * 1024),
        name="attend",
    )(place, kernel, mixing, query_ext, keys, values, gain)


def per_device(
    activations, positions, w_query, w_key, w_value, conv_kernel, head_mix, out_gain, w_out
):
    row_count = activations.shape[0]
    ctx_place = lax.axis_index("ctx")
    features = lax.all_gather(activations, "head", axis=1, tiled=True)
    key_proj = add_rows(features, lax.all_gather(w_key, "ctx", axis=0, tiled=True))
    key = rope(key_proj, positions).astype(jnp.bfloat16)
    value_proj = add_rows(features, lax.all_gather(w_value, "ctx", axis=0, tiled=True))
    value = value_proj.astype(jnp.bfloat16)
    query_proj = add_rows(features, lax.all_gather(w_query, "ctx", axis=0, tiled=True))
    query = rope(query_proj, positions).astype(jnp.bfloat16)
    keys_all = lax.all_gather(key, "ctx", axis=0, tiled=True)
    values_all = lax.all_gather(value, "ctx", axis=0, tiled=True)
    rim_rows = passed_along(query[row_count - 8 :], "ctx", 1)
    query_ext = jnp.concatenate([rim_rows, query], 0)
    normed = attend(
        ctx_place.astype(jnp.int32).reshape(1),
        query_ext,
        keys_all,
        values_all,
        conv_kernel,
        head_mix,
        out_gain.reshape(1, -1),
    )
    partial_out = jnp.dot(
        normed, lax.all_gather(w_out, "ctx", axis=1, tiled=True), preferred_element_type=jnp.float32
    )
    return lax.psum_scatter(
        partial_out.astype(jnp.bfloat16), "head", scatter_dimension=1, tiled=True
    )


def solution(mesh):
    return jax.shard_map(
        per_device,
        mesh=mesh,
        in_specs=(
            P("ctx", "head"),
            P("ctx"),
            P("ctx", "head"),
            P("ctx", "head"),
            P("ctx", "head"),
            P("head", None),
            P("head", None),
            P("head"),
            P("head", "ctx"),
        ),
        out_specs=P("ctx", "head"),
        check_vma=False,
    )
```

```python
import math

import jax
import jax.numpy as jnp
from jax import lax
from jax.experimental import pallas as pl
from jax.experimental.pallas import tpu as pltpu
from jax.sharding import PartitionSpec as P

HD = 128
GROUP = 4
CQ = 6
CK = 11
KB = 512
ROWS = 256
TOKENS = 4096
FRONT = 256
BAND = 10


MESH = pl.DeviceIdType.MESH


class Places:
    def __init__(self):
        self.ctx = lax.axis_index("ctx")
        self.head = lax.axis_index("head")
        self.col = lax.div(self.ctx, 8)
        self.z = lax.rem(lax.div(self.ctx, 2), 4)
        self.core = lax.rem(self.ctx, 2)
        self.y = lax.rem(self.head, 4)
        self.far = lax.div(self.head, 4)

    def ctx_at(self, flip_col=False, dz=0, flip_core=False):
        col = 1 - self.col if flip_col else self.col
        core = 1 - self.core if flip_core else self.core
        return col * 8 + lax.rem(self.z + dz + 4, 4) * 2 + core

    def head_at(self, flip=False, dy=0):
        far = 1 - self.far if flip else self.far
        return far * 4 + lax.rem(self.y + dy + 4, 4)


def greet(targets):
    barrier = pltpu.get_barrier_semaphore()
    for target in targets:
        pl.semaphore_signal(barrier, inc=1, device_id=target, device_id_type=MESH)
    pl.semaphore_wait(barrier, len(targets))


class Gather:
    def __init__(self, at, own, buf, rows, send, recv):
        self.at, self.own, self.buf, self.rows, self.send, self.recv = at, own, buf, rows, send, recv
        self.sib = {"ctx": at.ctx_at(flip_core=True)}
        self.xn = {"ctx": at.ctx_at(flip_col=True)}
        self.up = {"ctx": at.ctx_at(dz=1)}
        self.down = {"ctx": at.ctx_at(dz=-1)}
        self.sent = []

    def slot(self, index, half=None):
        size = self.rows if half is None else self.rows // 2
        first = index * self.rows + (size if half == 1 else 0)
        return self.buf.at[pl.ds(pl.multiple_of(first, size), size), :]

    def put(self, event, target, src, dst):
        copy = pltpu.make_async_remote_copy(
            src_ref=src, dst_ref=dst, send_sem=self.send.at[event], recv_sem=self.recv.at[event],
            device_id=target, device_id_type=MESH,
        )
        copy.start()
        self.sent.append(copy)

    def pass_on(self, event, target, index, half=None):
        piece = self.slot(index, half)
        self.put(event, target, piece, piece)

    def arrive(self, event, index, half=None):
        piece = self.slot(index, half)
        pltpu.make_async_remote_copy(
            src_ref=piece, dst_ref=piece, send_sem=self.send.at[event],
            recv_sem=self.recv.at[event], device_id=self.sib, device_id_type=MESH,
        ).wait_recv()

    def first(self):
        dst = self.slot(self.at.ctx)
        self.put(2, self.up, self.own, dst)
        self.put(3, self.down, self.own, dst)
        self.put(1, self.xn, self.own, dst)
        self.put(0, self.sib, self.own, dst)

    def second(self):
        at = self.at
        index = at.ctx_at(flip_col=True)
        self.arrive(1, index)
        self.pass_on(4, self.up, index)
        self.pass_on(5, self.down, index)
        self.pass_on(9, self.sib, index)
        index = at.ctx_at(dz=-1)
        self.arrive(2, index)
        self.pass_on(6, self.up, index, 0)
        self.pass_on(10, self.sib, index)
        index = at.ctx_at(dz=1)
        self.arrive(3, index)
        self.pass_on(7, self.down, index, 1)
        self.pass_on(11, self.sib, index)

    def third(self):
        at = self.at
        index = at.ctx_at(dz=2)
        self.arrive(6, index, 0)
        self.arrive(7, index, 1)
        self.pass_on(8, self.xn, index)
        self.pass_on(14, self.sib, index)
        for event, dz, on in ((4, -1, 12), (5, 1, 13)):
            index = at.ctx_at(flip_col=True, dz=dz)
            self.arrive(event, index)
            self.pass_on(on, self.sib, index)

    def last(self):
        at = self.at
        index = at.ctx_at(flip_col=True, dz=2)
        self.arrive(8, index)
        self.pass_on(15, self.sib, index)

    def whole(self):
        at = self.at
        for event, flip_col, dz in (
            (0, False, 0), (9, True, 0), (10, False, -1), (11, False, 1),
            (12, True, -1), (13, True, 1), (14, False, 2), (15, True, 2),
        ):
            self.arrive(event, at.ctx_at(flip_col=flip_col, dz=dz, flip_core=True))

    def close(self):
        for copy in self.sent:
            copy.wait_send()


class Features:
    def __init__(self, at, own, buf, send, recv):
        self.at, self.own, self.buf, self.send, self.recv = at, own, buf, send, recv
        self.partner = {"head": at.head_at(flip=True)}
        self.up = {"head": at.head_at(dy=1)}
        self.down = {"head": at.head_at(dy=-1)}
        self.sent = []

    def slot(self, index, half=None):
        cols = pl.ds(pl.multiple_of(index * 512, 512), 512)
        if half is None:
            return self.buf.at[:, cols]
        return self.buf.at[pl.ds(half * (ROWS // 2), ROWS // 2), cols]

    put, pass_on = Gather.put, Gather.pass_on

    def arrive(self, event, index, half=None):
        piece = self.slot(index, half)
        pltpu.make_async_remote_copy(
            src_ref=piece, dst_ref=piece, send_sem=self.send.at[event],
            recv_sem=self.recv.at[event], device_id=self.partner, device_id_type=MESH,
        ).wait_recv()

    def first(self):
        dst = self.slot(self.at.head)
        self.put(0, self.partner, self.own, dst)
        self.put(1, self.up, self.own, dst)
        self.put(2, self.down, self.own, dst)

    def second(self):
        at = self.at
        index = at.head_at(flip=True)
        self.arrive(0, index)
        self.pass_on(3, self.up, index)
        self.pass_on(4, self.down, index)
        index = at.head_at(dy=-1)
        self.arrive(1, index)
        self.pass_on(5, self.up, index, 0)
        index = at.head_at(dy=1)
        self.arrive(2, index)
        self.pass_on(6, self.down, index, 1)

    def third(self):
        at = self.at
        index = at.head_at(flip=True, dy=-1)
        self.arrive(3, index)
        self.pass_on(7, self.up, index, 0)
        index = at.head_at(flip=True, dy=1)
        self.arrive(4, index)
        self.pass_on(8, self.down, index, 1)

    def whole(self):
        at = self.at
        for event, flip in ((5, False), (7, True)):
            index = at.head_at(flip=flip, dy=2)
            self.arrive(event, index, 0)
            self.arrive(event + 1, index, 1)

    close = Gather.close


def project_kernel(
    x_ref, wk_ref, wv_ref, wq_ref, wo_ref, cos_ref, sin_ref,
    q_out, rim_out, k_out, v_out, wo_out,
    x_buf, w_bufs, made, send, recv, x_send, x_recv, here, rim_sems,
):
    at = Places()
    after = {"ctx": lax.rem(at.ctx + 1, 16)}
    greet(
        [{"ctx": at.ctx_at(flip_core=True)}, {"ctx": at.ctx_at(flip_col=True)}]
        + [{"ctx": at.ctx_at(dz=1)}, {"ctx": at.ctx_at(dz=-1)}]
        + [{"head": at.head_at(dy=1)}, {"head": at.head_at(dy=-1)}, {"head": at.head_at(flip=True)}]
        + [after, {"ctx": lax.rem(at.ctx + 15, 16)}]
    )

    def gather(t, own, buf, rows):
        return Gather(at, own, buf, rows, send.at[t], recv.at[t])

    feats = Features(at, x_ref, x_buf, x_send, x_recv)
    wk = gather(0, wk_ref, w_bufs.at[0], ROWS)
    wv = gather(1, wv_ref, w_bufs.at[1], ROWS)
    wq = gather(2, wq_ref, w_bufs.at[2], ROWS)
    own_slot = pl.ds(pl.multiple_of(at.ctx * ROWS, ROWS), ROWS)
    keys = gather(3, k_out.at[own_slot], k_out, ROWS)
    values = gather(4, v_out.at[own_slot], v_out, ROWS)
    wo = gather(5, wo_ref, wo_out, 2 * ROWS)

    wk.first()
    feats.first()
    own = [
        pltpu.make_async_copy(x_ref, feats.slot(at.head), here.at[0]),
        pltpu.make_async_copy(wk_ref, wk.slot(at.ctx), here.at[1]),
        pltpu.make_async_copy(wv_ref, wv.slot(at.ctx), here.at[2]),
        pltpu.make_async_copy(wq_ref, wq.slot(at.ctx), here.at[3]),
        pltpu.make_async_copy(wo_ref, wo.slot(at.ctx), here.at[4]),
    ]
    for copy in own:
        copy.start()

    def project(t):
        return jnp.dot(x_buf[...], w_bufs[t], preferred_element_type=jnp.float32)

    def rotate(projected):
        turned = []
        for h in range(GROUP):
            part = projected[:, h * HD : (h + 1) * HD]
            turned.append(part * cos_ref[...] + pltpu.roll(part, HD // 2, 1) * sin_ref[...])
        return jnp.concatenate(turned, 1)

    def keep(index, value, dst):
        made[index] = value.astype(jnp.bfloat16)
        copy = pltpu.make_async_copy(made.at[index], dst, here.at[5 + index])
        copy.start()
        copy.wait()

    wk.second()
    feats.second()
    wv.first()
    wk.third()
    feats.third()
    wv.second()
    wq.first()
    wk.last()
    for copy in own:
        copy.wait()
    feats.whole()
    wk.whole()
    keep(0, rotate(project(0)), k_out.at[own_slot])
    wv.third()
    wq.second()
    keys.first()
    wv.last()
    wv.whole()
    keep(1, project(1), v_out.at[own_slot])
    wq.third()
    keys.second()
    values.first()
    wq.last()
    wq.whole()
    keep(2, rotate(project(2)), q_out)
    rim = pltpu.make_async_remote_copy(
        src_ref=q_out.at[pl.ds(ROWS - 16, 16)], dst_ref=rim_out,
        send_sem=rim_sems.at[0], recv_sem=rim_sems.at[1], device_id=after, device_id_type=MESH,
    )
    rim.start()
    keys.third()
    values.second()
    wo.first()
    keys.last()
    values.third()
    wo.second()
    values.last()
    wo.third()
    wo.last()
    keys.whole()
    values.whole()
    wo.whole()
    rim.wait()
    for each in (feats, wk, wv, wq, keys, values, wo):
        each.close()


def project(x, wk, wv, wq, wo, cosine, sine):
    any_ref = pl.BlockSpec(memory_space=pl.ANY)
    vmem = pl.BlockSpec(memory_space=pltpu.VMEM)
    width = GROUP * HD
    shape = lambda *dims: jax.ShapeDtypeStruct(dims, jnp.bfloat16)
    return pl.pallas_call(
        project_kernel,
        out_shape=(
            shape(ROWS, width), shape(16, width), shape(TOKENS, width), shape(TOKENS, width),
            shape(16 * width, ROWS),
        ),
        in_specs=[any_ref] * 5 + [vmem] * 2,
        out_specs=(any_ref,) * 5,
        scratch_shapes=[
            pltpu.VMEM((ROWS, TOKENS), jnp.bfloat16),
            pltpu.VMEM((3, TOKENS, width), jnp.bfloat16),
            pltpu.VMEM((3, ROWS, width), jnp.bfloat16),
            pltpu.SemaphoreType.DMA((6, 16)),
            pltpu.SemaphoreType.DMA((6, 16)),
            pltpu.SemaphoreType.DMA((9,)),
            pltpu.SemaphoreType.DMA((9,)),
            pltpu.SemaphoreType.DMA((8,)),
            pltpu.SemaphoreType.DMA((2,)),
        ],
        compiler_params=pltpu.CompilerParams(
            collective_id=1, has_side_effects=True, vmem_limit_bytes=40 * 1024 * 1024
        ),
        name="project",
    )(x, wk, wv, wq, wo, cosine, sine)


def reduce_kernel(p_ref, o_ref, up_half, down_half, up_full, down_full, up_sum, down_sum, give, got, send, recv):
    at = Places()
    up = {"head": at.head_at(dy=1)}
    down = {"head": at.head_at(dy=-1)}
    partner = {"head": at.head_at(flip=True)}
    greet([up, down, partner])
    half = ROWS // 2
    top, low = pl.ds(0, half), pl.ds(half, half)
    y_up = lax.rem(at.y + 1, 4)
    y_down = lax.rem(at.y + 3, 4)
    y_far = lax.rem(at.y + 2, 4)

    def copy(event, target, src, dst):
        made = pltpu.make_async_remote_copy(
            src_ref=src, dst_ref=dst, send_sem=send.at[event], recv_sem=recv.at[event],
            device_id=target, device_id_type=MESH,
        )
        made.start()
        return made

    c0 = copy(0, up, p_ref.at[y_far, :, top], up_half)
    c1 = copy(1, down, p_ref.at[y_far, :, low], down_half)

    def add(left, right):
        return (left.astype(jnp.float32) + right.astype(jnp.float32)).astype(jnp.bfloat16)

    up_sum[:, low] = p_ref[y_up, :, low]
    down_sum[:, top] = p_ref[y_down, :, top]
    c0.wait_recv()
    up_sum[:, top] = add(p_ref[y_up, :, top], up_half[...])
    c2 = copy(2, up, up_sum, up_full)
    c1.wait_recv()
    down_sum[:, low] = add(p_ref[y_down, :, low], down_half[...])
    c3 = copy(3, down, down_sum, down_full)
    c2.wait_recv()
    c3.wait_recv()

    def total(far):
        return (
            p_ref[at.y, far].astype(jnp.float32)
            + up_full[far].astype(jnp.float32)
            + down_full[far].astype(jnp.float32)
        )

    give[...] = total(1 - at.far).astype(jnp.bfloat16)
    c4 = copy(4, partner, give, got)
    mine = total(at.far)
    c4.wait_recv()
    o_ref[...] = (mine + got[...].astype(jnp.float32)).astype(jnp.bfloat16)
    for made in (c0, c1, c2, c3, c4):
        made.wait_send()


def reduce_over_head(partial):
    vmem = pl.BlockSpec(memory_space=pltpu.VMEM)
    width = GROUP * HD
    buf = lambda *dims: pltpu.VMEM(dims, jnp.bfloat16)
    return pl.pallas_call(
        reduce_kernel,
        out_shape=jax.ShapeDtypeStruct((ROWS, width), jnp.bfloat16),
        in_specs=[vmem],
        out_specs=vmem,
        scratch_shapes=[
            buf(2, ROWS // 2, width), buf(2, ROWS // 2, width),
            buf(2, ROWS, width), buf(2, ROWS, width), buf(2, ROWS, width), buf(2, ROWS, width),
            buf(ROWS, width), buf(ROWS, width),
            pltpu.SemaphoreType.DMA((5,)),
            pltpu.SemaphoreType.DMA((5,)),
        ],
        compiler_params=pltpu.CompilerParams(
            collective_id=2, has_side_effects=True, vmem_limit_bytes=32 * 1024 * 1024
        ),
        name="reduce_over_head",
    )(partial)


def dot_nt(left, right):
    return lax.dot_general(
        left, right, (((1,), (1,)), ((), ())), preferred_element_type=jnp.float32
    )


def attend_kernel(
    place_ref, kern_ref, mix_ref, q_ref, rim_ref, k_ref, v_ref, wo_ref, gain_ref, o_ref,
    normed, q32, k32, qt, kc, lg, band, acc, tail,
):
    place = place_ref[0]
    r0 = place * ROWS
    blocks = lax.div(place + 2, 2)
    scale = 1.0 / math.sqrt(HD)

    def weight(h, a, c):
        return kern_ref[h, a * CK + c] * scale

    for h in range(GROUP):
        cols = slice(h * HD, (h + 1) * HD)
        q32[h, 8:] = q_ref[:, cols].astype(jnp.float32)
        rim = rim_ref[:, cols].astype(jnp.float32)[8:]
        q32[h, :8] = jnp.where(place > 0, rim, 0.0)
        k32[h, :FRONT] = jnp.zeros((FRONT, HD), jnp.float32)
        k32[h, pl.ds(pl.multiple_of(FRONT + blocks * KB, 8), 8)] = jnp.zeros((8, HD), jnp.float32)

    def widen(b, _):
        for h in range(GROUP):
            rows = pl.ds(pl.multiple_of(b * KB, KB), KB)
            dest = pl.ds(pl.multiple_of(FRONT + b * KB, FRONT), KB)
            k32[h, dest] = k_ref[rows, h * HD : (h + 1) * HD].astype(jnp.float32)
        return 0

    lax.fori_loop(0, blocks, widen, 0)

    for h in range(GROUP):

        def mix_lags(r, _, h=h):
            view = q32.at[h, pl.ds(pl.multiple_of(r * 16, 16), 24)]
            lags = [view[8 - a : 24 - a] for a in range(CQ)]
            for c in range(CK):
                total = weight(h, 0, c) * lags[0]
                for a in range(1, CQ):
                    total = total + weight(h, a, c) * lags[a]
                qt[h, pl.ds(pl.multiple_of(r * 16, 16), 16), c * HD : (c + 1) * HD] = total.astype(
                    jnp.bfloat16
                )
            return 0

        lax.fori_loop(0, ROWS // 16, mix_lags, 0)

    def block_logits(b, _):
        for h in range(GROUP):
            slot = h % 2
            view = k32.at[h, pl.ds(pl.multiple_of(FRONT - 8 + b * KB, 8), KB + 16)]
            for c in range(CK):
                start = 8 + CK // 2 - c
                kc[slot, :, c * HD : (c + 1) * HD] = view[start : start + KB].astype(jnp.bfloat16)
            lg[h, :, pl.ds(pl.multiple_of(HD + b * KB, HD), KB)] = dot_nt(qt[h], kc[slot])
        return 0

    lax.fori_loop(0, blocks, block_logits, 0)

    for s in range(2):
        for h in range(GROUP):
            queries = q32[h, s * HD : s * HD + HD + 8].astype(jnp.bfloat16)
            keys = k32[h, pl.ds(pl.multiple_of(FRONT - HD + r0 + s * HD, HD), 2 * HD)]
            scores = dot_nt(queries, keys.astype(jnp.bfloat16))
            apart = (
                lax.broadcasted_iota(jnp.int32, scores.shape, 0)
                - lax.broadcasted_iota(jnp.int32, scores.shape, 1)
                + (HD - 8)
            )
            kept = jnp.where((apart >= 0) & (apart <= 24), scores, 0.0)
            band[s * GROUP + h, 0] = kept[:, :HD]
            band[s * GROUP + h, 1] = kept[:, HD:]

    row_in = lax.broadcasted_iota(jnp.int32, (8, HD), 0)
    col_in = lax.broadcasted_iota(jnp.int32, (8, HD), 1)

    def taps(h, lags, width):
        total = None
        for c in range(CK):
            part = weight(h, 0, c) * lags[0]
            for a in range(1, CQ):
                part = part + weight(h, a, c) * lags[a]
            shift = (c - CK // 2) % width
            part = pltpu.roll(part, shift, 1) if shift else part
            total = part if total is None else total + part
        return total

    for s in range(2):
        for h in range(GROUP):
            here = pl.ds(pl.multiple_of(HD + r0 + s * HD, HD), HD)
            prior = pl.ds(pl.multiple_of(r0 + s * HD, HD), HD)

            for k in range(2):
                lags = [
                    jnp.concatenate(
                        [
                            band[s * GROUP + h, t, 8 * k + 8 - a : 8 * k + 16 - a]
                            for t in range(2)
                        ],
                        1,
                    )
                    for a in range(CQ)
                ]
                direct = taps(h, lags, 2 * HD)
                rows = slice(s * HD + 8 * k, s * HD + 8 * k + 8)
                apart = 8 * k + row_in - col_in
                lg[h, rows, prior] = jnp.where(
                    apart + HD >= BAND, lg[h, rows, prior], direct[:, :HD]
                )
                lg[h, rows, here] = jnp.where(
                    apart >= BAND,
                    lg[h, rows, here],
                    jnp.where(apart >= 0, direct[:, HD:], -jnp.inf),
                )

            def one_tile(k, _, s=s, h=h, here=here):
                view = band.at[s * GROUP + h, 1, pl.ds(pl.multiple_of(8 * k, 8), 16)]
                direct = taps(h, [view[8 - a : 16 - a] for a in range(CQ)], HD)
                rows = pl.ds(pl.multiple_of(s * HD + 8 * k, 8), 8)
                apart = 8 * k + row_in - col_in
                lg[h, rows, here] = jnp.where(
                    apart >= BAND,
                    lg[h, rows, here],
                    jnp.where(apart >= 0, direct, -jnp.inf),
                )
                return 0

            lax.fori_loop(2, HD // 8, one_tile, 0)

    for h in range(GROUP):
        lg[h, :HD, pl.ds(pl.multiple_of(2 * HD + r0, HD), HD)] = jnp.full(
            (HD, HD), -jnp.inf, jnp.float32
        )

    @pl.when(lax.rem(place, 2) == 0)
    def _():
        for h in range(GROUP):
            lg[h, :, pl.ds(pl.multiple_of(3 * HD + r0, HD), ROWS)] = jnp.full(
                (ROWS, ROWS), -jnp.inf, jnp.float32
            )

    for g in range(GROUP):

        def peak_of(b, peak, g=g):
            block = lg[g, :, pl.ds(pl.multiple_of(HD + b * KB, HD), KB)]
            for t in range(KB // HD):
                peak = jnp.maximum(peak, block[:, t * HD : (t + 1) * HD])
            return peak

        peak = lax.fori_loop(0, blocks, peak_of, jnp.full((ROWS, HD), -jnp.inf, jnp.float32))
        peak = jnp.max(peak, axis=1, keepdims=True)

        def weigh(b, mass, g=g, peak=peak):
            block = lg[g, :, pl.ds(pl.multiple_of(HD + b * KB, HD), KB)]
            probs = jnp.exp(block - peak)
            for t in range(KB // HD):
                mass = mass + probs[:, t * HD : (t + 1) * HD]
            values = v_ref[pl.ds(pl.multiple_of(b * KB, KB), KB), :]
            piece = jnp.dot(probs.astype(jnp.bfloat16), values, preferred_element_type=jnp.float32)

            @pl.when(b == 0)
            def _():
                acc[g] = piece

            @pl.when(b > 0)
            def _():
                acc[g] = acc[g] + piece

            return mass

        mass = lax.fori_loop(0, blocks, weigh, jnp.zeros((ROWS, HD), jnp.float32))
        tail[g] = jnp.broadcast_to(1.0 / jnp.sum(mass, axis=1, keepdims=True), (ROWS, HD))

    for h in range(GROUP):
        cols = slice(h * HD, (h + 1) * HD)
        total = mix_ref[h, 0] * (acc[0, :, cols] * tail[0])
        for g in range(1, GROUP):
            total = total + mix_ref[h, g] * (acc[g, :, cols] * tail[g])
        rms = jnp.sqrt(jnp.mean(total * total, axis=1, keepdims=True) + 1e-05)
        normed[:, cols] = (total / rms * gain_ref[:, cols]).astype(jnp.bfloat16)

    width = GROUP * HD

    def out_block(b, _):
        rows = pl.ds(pl.multiple_of(b * width, width), width)
        piece = jnp.dot(normed[...], wo_ref[rows], preferred_element_type=jnp.float32)
        far, y, part = lax.div(b, 8), lax.rem(lax.div(b, 2), 4), lax.rem(b, 2)
        o_ref[y, far, :, pl.ds(pl.multiple_of(part * ROWS, ROWS), ROWS)] = piece.astype(jnp.bfloat16)
        return 0

    lax.fori_loop(0, 16, out_block, 0)


def attend(place, query, rim, keys, values, wo, kernel, mixing, gain):
    smem = pl.BlockSpec(memory_space=pltpu.SMEM)
    vmem = pl.BlockSpec(memory_space=pltpu.VMEM)
    return pl.pallas_call(
        attend_kernel,
        out_shape=jax.ShapeDtypeStruct((4, 2, ROWS, GROUP * HD), jnp.bfloat16),
        in_specs=[smem, smem, smem, vmem, vmem, vmem, vmem, vmem, vmem],
        out_specs=vmem,
        scratch_shapes=[
            pltpu.VMEM((ROWS, GROUP * HD), jnp.bfloat16),
            pltpu.VMEM((GROUP, ROWS + 8, HD), jnp.float32),
            pltpu.VMEM((GROUP, FRONT + TOKENS + 16, HD), jnp.float32),
            pltpu.VMEM((GROUP, ROWS, CK * HD), jnp.bfloat16),
            pltpu.VMEM((2, KB, CK * HD), jnp.bfloat16),
            pltpu.VMEM((GROUP, ROWS, HD + TOKENS), jnp.float32),
            pltpu.VMEM((2 * GROUP, 2, HD + 8, HD), jnp.float32),
            pltpu.VMEM((GROUP, ROWS, GROUP * HD), jnp.float32),
            pltpu.VMEM((GROUP, ROWS, HD), jnp.float32),
        ],
        compiler_params=pltpu.CompilerParams(vmem_limit_bytes=62 * 1024 * 1024),
        name="attend",
    )(place, kernel, mixing, query, rim, keys, values, wo, gain)


def per_device(
    activations, positions, w_query, w_key, w_value, conv_kernel, head_mix, out_gain, w_out
):
    exponents = jnp.arange(HD // 2, dtype=jnp.float32) * (2.0 / HD)
    inverse = jnp.exp(-exponents * math.log(500000.0))
    angle = (positions.astype(jnp.float32) * 0.25)[:, None] * inverse[None, :]
    cosine = jnp.cos(angle)
    sine = jnp.sin(angle)
    query, rim, keys, values, wo = project(
        activations, w_key, w_value, w_query, w_out,
        jnp.concatenate([cosine, cosine], 1), jnp.concatenate([-sine, sine], 1),
    )
    partial = attend(
        lax.axis_index("ctx").astype(jnp.int32).reshape(1),
        query, rim, keys, values, wo, conv_kernel, head_mix, out_gain.reshape(1, -1),
    )
    return reduce_over_head(partial)


def solution(mesh):
    return jax.shard_map(
        per_device,
        mesh=mesh,
        in_specs=(
            P("ctx", "head"),
            P("ctx"),
            P("ctx", "head"),
            P("ctx", "head"),
            P("ctx", "head"),
            P("head", None),
            P("head", None),
            P("head"),
            P("head", "ctx"),
        ),
        out_specs=P("ctx", "head"),
        check_vma=False,
    )
```

```python
import math

import jax
import jax.numpy as jnp
from jax import lax
from jax.experimental import pallas as pl
from jax.experimental.pallas import tpu as pltpu
from jax.sharding import PartitionSpec as P

HD = 128
GROUP = 4
CQ = 6
CK = 11
KB = 512
ROWS = 256
TOKENS = 4096
HALF = 128
BAND = 10


MESH = pl.DeviceIdType.MESH


class Places:
    def __init__(self):
        self.ctx = lax.axis_index("ctx")
        self.head = lax.axis_index("head")
        self.col = lax.div(self.ctx, 8)
        self.z = lax.rem(lax.div(self.ctx, 2), 4)
        self.core = lax.rem(self.ctx, 2)
        self.y = lax.rem(self.head, 4)
        self.far = lax.div(self.head, 4)

    def ctx_at(self, flip_col=False, dz=0, flip_core=False):
        col = 1 - self.col if flip_col else self.col
        core = 1 - self.core if flip_core else self.core
        return col * 8 + lax.rem(self.z + dz + 4, 4) * 2 + core

    def head_at(self, flip=False, dy=0):
        far = 1 - self.far if flip else self.far
        return far * 4 + lax.rem(self.y + dy + 4, 4)


def greet(targets):
    barrier = pltpu.get_barrier_semaphore()
    for target in targets:
        pl.semaphore_signal(barrier, inc=1, device_id=target, device_id_type=MESH)
    pl.semaphore_wait(barrier, len(targets))


class Gather:
    def __init__(self, at, own, buf, rows, send, recv, base=0):
        self.at, self.own, self.buf, self.rows, self.send, self.recv = at, own, buf, rows, send, recv
        self.base = base
        self.sib = {"ctx": at.ctx_at(flip_core=True)}
        self.xn = {"ctx": at.ctx_at(flip_col=True)}
        self.up = {"ctx": at.ctx_at(dz=1)}
        self.down = {"ctx": at.ctx_at(dz=-1)}

    def slot(self, index, half=None):
        size = self.rows if half is None else self.rows // 2
        first = self.base + index * self.rows + (size if half == 1 else 0)
        return self.buf.at[pl.ds(pl.multiple_of(first, 128), size), :]

    def put(self, event, target, src, dst):
        copy = pltpu.make_async_remote_copy(
            src_ref=src, dst_ref=dst, send_sem=self.send.at[event], recv_sem=self.recv.at[event],
            device_id=target, device_id_type=MESH,
        )
        copy.start()

    def pass_on(self, event, target, index, half=None):
        piece = self.slot(index, half)
        self.put(event, target, piece, piece)

    def arrive(self, event, index, half=None):
        piece = self.slot(index, half)
        pltpu.make_async_remote_copy(
            src_ref=piece, dst_ref=piece, send_sem=self.send.at[event],
            recv_sem=self.recv.at[event], device_id=self.sib, device_id_type=MESH,
        ).wait_recv()

    def first(self):
        dst = self.slot(self.at.ctx)
        self.put(2, self.up, self.own, dst)
        self.put(3, self.down, self.own, dst)
        self.put(1, self.xn, self.own, dst)
        self.put(0, self.sib, self.own, dst)

    def second(self):
        at = self.at
        index = at.ctx_at(flip_col=True)
        self.arrive(1, index)
        self.pass_on(4, self.up, index)
        self.pass_on(5, self.down, index)
        self.pass_on(9, self.sib, index)
        index = at.ctx_at(dz=-1)
        self.arrive(2, index)
        self.pass_on(6, self.up, index, 0)
        self.pass_on(10, self.sib, index)
        index = at.ctx_at(dz=1)
        self.arrive(3, index)
        self.pass_on(7, self.down, index, 1)
        self.pass_on(11, self.sib, index)

    def third(self):
        at = self.at
        index = at.ctx_at(dz=2)
        self.arrive(6, index, 0)
        self.arrive(7, index, 1)
        self.pass_on(8, self.xn, index)
        self.pass_on(14, self.sib, index)
        for event, dz, on in ((4, -1, 12), (5, 1, 13)):
            index = at.ctx_at(flip_col=True, dz=dz)
            self.arrive(event, index)
            self.pass_on(on, self.sib, index)

    def last(self):
        at = self.at
        index = at.ctx_at(flip_col=True, dz=2)
        self.arrive(8, index)
        self.pass_on(15, self.sib, index)

    def whole(self):
        at = self.at
        for event, flip_col, dz in (
            (0, False, 0), (9, True, 0), (10, False, -1), (11, False, 1),
            (12, True, -1), (13, True, 1), (14, False, 2), (15, True, 2),
        ):
            self.arrive(event, at.ctx_at(flip_col=flip_col, dz=dz, flip_core=True))

    halves = (6, 7)
    events = 16

    def close(self):
        for event in range(self.events):
            piece = self.slot(0, 0 if event in self.halves else None)
            pltpu.make_async_remote_copy(
                src_ref=piece, dst_ref=piece, send_sem=self.send.at[event],
                recv_sem=self.recv.at[event], device_id=self.sib, device_id_type=MESH,
            ).wait_send()


class Features:
    def __init__(self, at, own, buf, send, recv):
        self.at, self.own, self.buf, self.send, self.recv = at, own, buf, send, recv
        self.partner = self.sib = {"head": at.head_at(flip=True)}
        self.up = {"head": at.head_at(dy=1)}
        self.down = {"head": at.head_at(dy=-1)}

    def slot(self, index, half=None):
        cols = pl.ds(pl.multiple_of(index * 512, 512), 512)
        if half is None:
            return self.buf.at[:, cols]
        return self.buf.at[pl.ds(half * (ROWS // 2), ROWS // 2), cols]

    put, pass_on = Gather.put, Gather.pass_on

    def arrive(self, event, index, half=None):
        piece = self.slot(index, half)
        pltpu.make_async_remote_copy(
            src_ref=piece, dst_ref=piece, send_sem=self.send.at[event],
            recv_sem=self.recv.at[event], device_id=self.partner, device_id_type=MESH,
        ).wait_recv()

    def first(self):
        dst = self.slot(self.at.head)
        self.put(0, self.partner, self.own, dst)
        self.put(1, self.up, self.own, dst)
        self.put(2, self.down, self.own, dst)

    def second(self):
        at = self.at
        index = at.head_at(flip=True)
        self.arrive(0, index)
        self.pass_on(3, self.up, index)
        self.pass_on(4, self.down, index)
        index = at.head_at(dy=-1)
        self.arrive(1, index)
        self.pass_on(5, self.up, index, 0)
        index = at.head_at(dy=1)
        self.arrive(2, index)
        self.pass_on(6, self.down, index, 1)

    def third(self):
        at = self.at
        index = at.head_at(flip=True, dy=-1)
        self.arrive(3, index)
        self.pass_on(7, self.up, index, 0)
        index = at.head_at(flip=True, dy=1)
        self.arrive(4, index)
        self.pass_on(8, self.down, index, 1)

    def whole(self):
        at = self.at
        for event, flip in ((5, False), (7, True)):
            index = at.head_at(flip=flip, dy=2)
            self.arrive(event, index, 0)
            self.arrive(event + 1, index, 1)

    halves = (5, 6, 7, 8)
    events = 9
    close = Gather.close


def dot_nt(left, right):
    return lax.dot_general(
        left, right, (((1,), (1,)), ((), ())), preferred_element_type=jnp.float32
    )


def layer_kernel(
    x_ref, wk_ref, wv_ref, wq_ref, wo_ref, kern_ref, mix_ref, cos_ref, sin_ref, gain_ref, o_ref,
    x_buf, wk_buf, wq_buf, wv_buf, k_buf, v_buf, wo_buf, made, qx, rim_in,
    q32, k32, qt, kc, lg, band, ps, acc, mass, peaks, normed, part,
    y_half, y_sum, y_full, give, got,
    send, recv, x_send, x_recv, here, rim_sems, r_send, r_recv,
):
    at = Places()
    place = at.ctx
    r0 = place * ROWS
    blocks = lax.div(place + 2, 2)
    scale = 1.0 / math.sqrt(HD)
    after = {"ctx": lax.rem(at.ctx + 1, 16)}
    greet(
        [{"ctx": at.ctx_at(flip_core=True)}, {"ctx": at.ctx_at(flip_col=True)}]
        + [{"ctx": at.ctx_at(dz=1)}, {"ctx": at.ctx_at(dz=-1)}]
        + [{"head": at.head_at(dy=1)}, {"head": at.head_at(dy=-1)}, {"head": at.head_at(flip=True)}]
        + [after, {"ctx": lax.rem(at.ctx + 15, 16)}]
    )

    def gather(t, own, buf, rows, base=0):
        return Gather(at, own, buf, rows, send.at[t], recv.at[t], base)

    feats = Features(at, x_ref, x_buf, x_send, x_recv)
    wk = gather(0, wk_ref, wk_buf, ROWS)
    wv = gather(1, wv_ref, wv_buf, ROWS)
    wq = gather(2, wq_ref, wq_buf, ROWS)
    keys = gather(3, None, k_buf, ROWS, HD)
    values = gather(4, None, v_buf, ROWS)
    wo = gather(5, wo_ref, wo_buf, 2 * ROWS)
    keys.own = keys.slot(at.ctx)
    values.own = values.slot(at.ctx)

    wk.first()
    feats.first()
    own = [
        pltpu.make_async_copy(x_ref, feats.slot(at.head), here.at[0]),
        pltpu.make_async_copy(wk_ref, wk.slot(at.ctx), here.at[1]),
        pltpu.make_async_copy(wq_ref, wq.slot(at.ctx), here.at[3]),
        pltpu.make_async_copy(wv_ref, wv.slot(at.ctx), here.at[2]),
        pltpu.make_async_copy(wo_ref, wo.slot(at.ctx), here.at[4]),
    ]
    for copy in own:
        copy.start()
    k_buf[:HD] = jnp.zeros((HD, GROUP * HD), jnp.bfloat16)
    k_buf[HD + TOKENS :] = jnp.zeros((16, GROUP * HD), jnp.bfloat16)

    def project(buf):
        return jnp.dot(x_buf[...], buf[...], preferred_element_type=jnp.float32)

    def rotate(projected):
        turned = []
        for h in range(GROUP):
            piece = projected[:, h * HD : (h + 1) * HD]
            turned.append(piece * cos_ref[...] + pltpu.roll(piece, HD // 2, 1) * sin_ref[...])
        return jnp.concatenate(turned, 1)

    def keep(index, value, dst):
        made[index] = value.astype(jnp.bfloat16)
        copy = pltpu.make_async_copy(made.at[index], dst, here.at[5 + index])
        copy.start()
        copy.wait()

    wk.second()
    feats.second()
    wq.first()
    wk.third()
    feats.third()
    wq.second()
    wk.last()
    for copy in own:
        copy.wait()
    feats.whole()
    wk.whole()
    keep(0, rotate(project(wk_buf)), keys.slot(at.ctx))
    keys.first()
    wv.first()
    wq.third()
    wq.last()
    keys.second()
    wq.whole()
    keep(2, rotate(project(wq_buf)), qx.at[pl.ds(16, ROWS)])
    rim = pltpu.make_async_remote_copy(
        src_ref=qx.at[pl.ds(ROWS, 16)], dst_ref=rim_in,
        send_sem=rim_sems.at[0], recv_sem=rim_sems.at[1], device_id=after, device_id_type=MESH,
    )
    rim.start()
    wv.second()
    keys.third()
    rim.wait()
    qx[:16] = jnp.where(place > 0, rim_in[...], jnp.zeros_like(rim_in))
    for h in range(GROUP):
        q32[h] = qx[:, h * HD : (h + 1) * HD].astype(jnp.float32)[8:] * scale

    def mix_lags(r, _):
        for h in range(GROUP):
            view = q32.at[h, pl.ds(pl.multiple_of(r * 16, 16), 24)]
            lags = [view[8 - a : 24 - a] for a in range(CQ)]
            for c in range(CK):
                total = kern_ref[h, c] * lags[0]
                for a in range(1, CQ):
                    total = total + kern_ref[h, a * CK + c] * lags[a]
                qt[h, pl.ds(pl.multiple_of(r * 16, 16), 16), c * HD : (c + 1) * HD] = total.astype(
                    jnp.bfloat16
                )
        return 0

    lax.fori_loop(0, ROWS // 16, mix_lags, 0)
    keys.last()
    keys.whole()

    def value_step():
        wv.last()
        wv.whole()
        keep(1, project(wv_buf), values.slot(at.ctx))
        values.first()
        wo.first()

    steps = {1: [wv.third], 3: [value_step], 5: [values.second], 7: [wo.second, values.third]}

    def block_logits(b, _):
        for when, actions in steps.items():

            @pl.when(b == when)
            def _(actions=actions):
                for action in actions:
                    action()

        @pl.when(b < blocks)
        def _():
            for h in range(GROUP):
                rows = k_buf[pl.ds(pl.multiple_of(HD - 16 + b * KB, 16), KB + 32), h * HD : (h + 1) * HD]
                k32[h] = rows.astype(jnp.float32)
                for c in range(CK):
                    start = 16 + CK // 2 - c
                    kc[h % 2, :, c * HD : (c + 1) * HD] = k32[h, start : start + KB].astype(jnp.bfloat16)
                lg[h, :, pl.ds(pl.multiple_of(HD + b * KB, HD), KB)] = dot_nt(qt[h], kc[h % 2])

        return 0

    lax.fori_loop(0, 8, block_logits, 0)

    for s in range(2):
        for h in range(GROUP):
            cols = slice(h * HD, (h + 1) * HD)
            near = k_buf[pl.ds(pl.multiple_of(r0 + s * HD, HD), 2 * HD), cols]
            scores = dot_nt(qx[s * HD : s * HD + HD + 16, cols], near)[8:] * scale
            apart = (
                lax.broadcasted_iota(jnp.int32, scores.shape, 0)
                - lax.broadcasted_iota(jnp.int32, scores.shape, 1)
                + (HD - 8)
            )
            kept = jnp.where((apart >= 0) & (apart <= 24), scores, 0.0)
            band[s * GROUP + h, 0] = kept[:, :HD]
            band[s * GROUP + h, 1] = kept[:, HD:]

    row_in = lax.broadcasted_iota(jnp.int32, (8, HD), 0)
    col_in = lax.broadcasted_iota(jnp.int32, (8, HD), 1)

    def taps(h, lags, width):
        total = None
        for c in range(CK):
            piece = kern_ref[h, c] * lags[0]
            for a in range(1, CQ):
                piece = piece + kern_ref[h, a * CK + c] * lags[a]
            shift = (c - CK // 2) % width
            piece = pltpu.roll(piece, shift, 1) if shift else piece
            total = piece if total is None else total + piece
        return total

    def two_tiles(k, _):
        for s in range(2):
            here_cols = pl.ds(pl.multiple_of(HD + r0 + s * HD, HD), HD)
            prior = pl.ds(pl.multiple_of(r0 + s * HD, HD), HD)
            for h in range(GROUP):
                views = [
                    band.at[s * GROUP + h, t, pl.ds(pl.multiple_of(8 * k, 8), 16)] for t in range(2)
                ]
                lags = [
                    jnp.concatenate([view[8 - a : 16 - a] for view in views], 1) for a in range(CQ)
                ]
                direct = taps(h, lags, 2 * HD)
                rows = pl.ds(pl.multiple_of(s * HD + 8 * k, 8), 8)
                apart = 8 * k + row_in - col_in
                lg[h, rows, prior] = jnp.where(
                    apart + HD >= BAND, lg[h, rows, prior], direct[:, :HD]
                )
                lg[h, rows, here_cols] = jnp.where(
                    apart >= BAND,
                    lg[h, rows, here_cols],
                    jnp.where(apart >= 0, direct[:, HD:], -jnp.inf),
                )
        return 0

    def one_tile(k, _):
        for s in range(2):
            here_cols = pl.ds(pl.multiple_of(HD + r0 + s * HD, HD), HD)
            for h in range(GROUP):
                view = band.at[s * GROUP + h, 1, pl.ds(pl.multiple_of(8 * k, 8), 16)]
                direct = taps(h, [view[8 - a : 16 - a] for a in range(CQ)], HD)
                rows = pl.ds(pl.multiple_of(s * HD + 8 * k, 8), 8)
                apart = 8 * k + row_in - col_in
                lg[h, rows, here_cols] = jnp.where(
                    apart >= BAND,
                    lg[h, rows, here_cols],
                    jnp.where(apart >= 0, direct, -jnp.inf),
                )
        return 0

    lax.fori_loop(0, 2, two_tiles, 0)
    lax.fori_loop(2, HD // 8, one_tile, 0)
    for h in range(GROUP):
        lg[h, :HD, pl.ds(pl.multiple_of(2 * HD + r0, HD), HD)] = jnp.full(
            (HD, HD), -jnp.inf, jnp.float32
        )

    @pl.when(lax.rem(place, 2) == 0)
    def _():
        for h in range(GROUP):
            lg[h, :, pl.ds(pl.multiple_of(3 * HD + r0, HD), ROWS)] = jnp.full(
                (ROWS, ROWS), -jnp.inf, jnp.float32
            )

    for g in range(GROUP):

        def peak_of(b, peak, g=g):
            block = lg[g, :, pl.ds(pl.multiple_of(HD + b * KB, HD), KB)]
            for t in range(KB // HD):
                peak = jnp.maximum(peak, block[:, t * HD : (t + 1) * HD])
            return peak

        peak = lax.fori_loop(0, blocks, peak_of, jnp.full((ROWS, HD), -jnp.inf, jnp.float32))
        peaks[g] = jnp.broadcast_to(jnp.max(peak, axis=1, keepdims=True), (ROWS, HD))

    values.last()
    wo.third()
    values.whole()

    up = {"head": at.head_at(dy=1)}
    down = {"head": at.head_at(dy=-1)}
    partner = {"head": at.head_at(flip=True)}
    quarter = HALF // 2
    y_up, y_down, y_far = (lax.rem(at.y + d, 4) for d in (1, 3, 2))

    def ring_copy(r, event):
        top, low = pl.ds(0, quarter), pl.ds(quarter, quarter)
        target, src, dst = (
            (up, part.at[r, y_far, :, top], y_half.at[r, 0]),
            (down, part.at[r, y_far, :, low], y_half.at[r, 1]),
            (up, y_sum.at[r, 0], y_full.at[r, 0]),
            (down, y_sum.at[r, 1], y_full.at[r, 1]),
            (partner, give.at[r], got.at[r]),
        )[event]
        return pltpu.make_async_remote_copy(
            src_ref=src, dst_ref=dst, send_sem=r_send.at[r, event], recv_sem=r_recv.at[r, event],
            device_id=target, device_id_type=MESH,
        )

    def add(left, right):
        return (left.astype(jnp.float32) + right.astype(jnp.float32)).astype(jnp.bfloat16)

    def ring_first(r):
        ring_copy(r, 0).start()
        ring_copy(r, 1).start()
        y_sum[r, 0, :, quarter:] = part[r, y_up, :, quarter:]
        y_sum[r, 1, :, :quarter] = part[r, y_down, :, :quarter]

    def ring_second(r):
        ring_copy(r, 0).wait_recv()
        y_sum[r, 0, :, :quarter] = add(part[r, y_up, :, :quarter], y_half[r, 0])
        ring_copy(r, 2).start()
        ring_copy(r, 1).wait_recv()
        y_sum[r, 1, :, quarter:] = add(part[r, y_down, :, quarter:], y_half[r, 1])
        ring_copy(r, 3).start()

    def ring_total(r, far):
        return (
            part[r, at.y, far].astype(jnp.float32)
            + y_full[r, 0, far].astype(jnp.float32)
            + y_full[r, 1, far].astype(jnp.float32)
        )

    def ring_third(r):
        ring_copy(r, 2).wait_recv()
        ring_copy(r, 3).wait_recv()
        give[r] = ring_total(r, 1 - at.far).astype(jnp.bfloat16)
        ring_copy(r, 4).start()

    def ring_last(r):
        mine = ring_total(r, at.far)
        ring_copy(r, 4).wait_recv()
        total = mine + got[r].astype(jnp.float32)
        o_ref[r * HALF : (r + 1) * HALF] = total.astype(jnp.bfloat16)

    for r in range(2):
        rows = slice(r * HALF, (r + 1) * HALF)
        acc[...] = jnp.zeros_like(acc)
        mass[...] = jnp.zeros_like(mass)

        def weigh(b, _, r=r, rows=rows):
            if r == 1:
                pl.when(b == 2)(lambda: ring_second(0))
                pl.when(b == 5)(lambda: ring_third(0))

            @pl.when(b < blocks)
            def _():
                for g in range(GROUP):
                    peak = peaks[g, rows]
                    total = mass[g]
                    for t in range(KB // HD):
                        block = lg[g, rows, pl.ds(pl.multiple_of(HD + b * KB + t * HD, HD), HD)]
                        probs = jnp.exp(block - peak)
                        total = total + probs
                        ps[g * HALF : (g + 1) * HALF, t * HD : (t + 1) * HD] = probs.astype(jnp.bfloat16)
                    mass[g] = total
                block = v_buf[pl.ds(pl.multiple_of(b * KB, KB), KB), :]
                acc[...] += jnp.dot(ps[...], block, preferred_element_type=jnp.float32)

            return 0

        lax.fori_loop(0, 8, weigh, 0)
        inverse = [
            jnp.broadcast_to(1.0 / jnp.sum(mass[g], axis=1, keepdims=True), (HALF, HD))
            for g in range(GROUP)
        ]
        for h in range(GROUP):
            cols = slice(h * HD, (h + 1) * HD)
            total = mix_ref[h, 0] * (acc[:HALF, cols] * inverse[0])
            for g in range(1, GROUP):
                total = total + mix_ref[h, g] * (acc[g * HALF : (g + 1) * HALF, cols] * inverse[g])
            rms = jnp.sqrt(jnp.mean(total * total, axis=1, keepdims=True) + 1e-05)
            normed[:, cols] = (total / rms * gain_ref[:, cols]).astype(jnp.bfloat16)
        if r == 0:
            wo.last()
            wo.whole()

        def out_block(b, _, r=r):
            width = GROUP * HD
            source = pl.ds(pl.multiple_of(b * width, width), width)
            piece = jnp.dot(normed[...], wo_buf[source], preferred_element_type=jnp.float32)
            far, y, side = lax.div(b, 8), lax.rem(lax.div(b, 2), 4), lax.rem(b, 2)
            part[r, y, far, :, pl.ds(pl.multiple_of(side * ROWS, ROWS), ROWS)] = piece.astype(jnp.bfloat16)
            return 0

        lax.fori_loop(0, 16, out_block, 0)
        ring_first(r)

    ring_last(0)
    ring_second(1)
    ring_third(1)
    ring_last(1)
    for r in range(2):
        for event in range(5):
            ring_copy(r, event).wait_send()
    for each in (feats, wk, wv, wq, keys, values, wo):
        each.close()


def layer(*operands):
    smem = pl.BlockSpec(memory_space=pltpu.SMEM)
    vmem = pl.BlockSpec(memory_space=pltpu.VMEM)
    hbm = pl.BlockSpec(memory_space=pltpu.HBM)
    width = GROUP * HD
    half = lambda *dims: pltpu.VMEM(dims, jnp.bfloat16)
    full = lambda *dims: pltpu.VMEM(dims, jnp.float32)
    dma = pltpu.SemaphoreType.DMA
    return pl.pallas_call(
        layer_kernel,
        out_shape=jax.ShapeDtypeStruct((ROWS, width), jnp.bfloat16),
        in_specs=[hbm] * 5 + [smem] * 2 + [vmem] * 3,
        out_specs=vmem,
        scratch_shapes=[
            half(ROWS, TOKENS), half(TOKENS, width), half(TOKENS, width), half(TOKENS, width),
            half(HD + TOKENS + 16, width), half(TOKENS, width), half(16 * width, ROWS),
            half(3, ROWS, width), half(ROWS + 16, width), half(16, width),
            full(GROUP, ROWS + 8, HD), full(GROUP, KB + 32, HD),
            half(GROUP, ROWS, CK * HD), half(2, KB, CK * HD),
            full(GROUP, ROWS, HD + TOKENS), full(2 * GROUP, 2, HD + 8, HD),
            half(GROUP * HALF, KB), full(GROUP * HALF, width),
            full(GROUP, HALF, HD), full(GROUP, ROWS, HD), half(HALF, width),
            half(2, 4, 2, HALF, width),
            half(2, 2, 2, HALF // 2, width), half(2, 2, 2, HALF, width), half(2, 2, 2, HALF, width),
            half(2, HALF, width), half(2, HALF, width),
            dma((6, 16)), dma((6, 16)), dma((9,)), dma((9,)), dma((8,)), dma((2,)), dma((2, 5)), dma((2, 5)),
        ],
        compiler_params=pltpu.CompilerParams(
            collective_id=1, has_side_effects=True, vmem_limit_bytes=67043328
        ),
        name="layer",
    )(*operands)


def per_device(
    activations, positions, w_query, w_key, w_value, conv_kernel, head_mix, out_gain, w_out
):
    exponents = jnp.arange(HD // 2, dtype=jnp.float32) * (2.0 / HD)
    inverse = jnp.exp(-exponents * math.log(500000.0))
    angle = (positions.astype(jnp.float32) * 0.25)[:, None] * inverse[None, :]
    cosine = jnp.cos(angle)
    sine = jnp.sin(angle)
    return layer(
        activations, w_key, w_value, w_query, w_out, conv_kernel, head_mix,
        jnp.concatenate([cosine, cosine], 1), jnp.concatenate([-sine, sine], 1),
        out_gain.reshape(1, -1),
    )


def solution(mesh):
    return jax.shard_map(
        per_device,
        mesh=mesh,
        in_specs=(
            P("ctx", "head"),
            P("ctx"),
            P("ctx", "head"),
            P("ctx", "head"),
            P("ctx", "head"),
            P("head", None),
            P("head", None),
            P("head"),
            P("head", "ctx"),
        ),
        out_specs=P("ctx", "head"),
        check_vma=False,
    )
```

```python
import math

import jax
import jax.numpy as jnp
from jax import lax
from jax.experimental import pallas as pl
from jax.experimental.pallas import tpu as pltpu
from jax.sharding import PartitionSpec as P

HD = 128
GROUP = 4
CQ = 6
CK = 11
KB = 512
ROWS = 256
TOKENS = 4096
HALF = 128
BAND = 10


MESH = pl.DeviceIdType.MESH


class Places:
    def __init__(self):
        self.ctx = lax.axis_index("ctx")
        self.head = lax.axis_index("head")
        self.col = lax.div(self.ctx, 8)
        self.z = lax.rem(lax.div(self.ctx, 2), 4)
        self.core = lax.rem(self.ctx, 2)
        self.y = lax.rem(self.head, 4)
        self.far = lax.div(self.head, 4)

    def ctx_at(self, flip_col=False, dz=0, flip_core=False):
        col = 1 - self.col if flip_col else self.col
        core = 1 - self.core if flip_core else self.core
        return col * 8 + lax.rem(self.z + dz + 4, 4) * 2 + core

    def head_at(self, flip=False, dy=0):
        far = 1 - self.far if flip else self.far
        return far * 4 + lax.rem(self.y + dy + 4, 4)


def greet(targets):
    barrier = pltpu.get_barrier_semaphore()
    for target in targets:
        pl.semaphore_signal(barrier, inc=1, device_id=target, device_id_type=MESH)
    return lambda: pl.semaphore_wait(barrier, len(targets))


class Gather:
    def __init__(self, at, own, buf, rows, send, recv, base=0):
        self.at, self.own, self.buf, self.rows, self.send, self.recv = at, own, buf, rows, send, recv
        self.base = base
        self.sib = {"ctx": at.ctx_at(flip_core=True)}
        self.xn = {"ctx": at.ctx_at(flip_col=True)}
        self.up = {"ctx": at.ctx_at(dz=1)}
        self.down = {"ctx": at.ctx_at(dz=-1)}

    def slot(self, index, half=None):
        size = self.rows if half is None else self.rows // 2
        first = self.base + index * self.rows + (size if half == 1 else 0)
        return self.buf.at[pl.ds(pl.multiple_of(first, 128), size), :]

    def put(self, event, target, src, dst):
        copy = pltpu.make_async_remote_copy(
            src_ref=src, dst_ref=dst, send_sem=self.send.at[event], recv_sem=self.recv.at[event],
            device_id=target, device_id_type=MESH,
        )
        copy.start()

    def pass_on(self, event, target, index, half=None):
        piece = self.slot(index, half)
        self.put(event, target, piece, piece)

    def arrive(self, event, index, half=None):
        piece = self.slot(index, half)
        pltpu.make_async_remote_copy(
            src_ref=piece, dst_ref=piece, send_sem=self.send.at[event],
            recv_sem=self.recv.at[event], device_id=self.sib, device_id_type=MESH,
        ).wait_recv()

    def first(self):
        dst = self.slot(self.at.ctx)
        self.put(2, self.up, self.own, dst)
        self.put(3, self.down, self.own, dst)
        self.put(1, self.xn, self.own, dst)
        self.put(0, self.sib, self.own, dst)

    def second(self):
        at = self.at
        index = at.ctx_at(flip_col=True)
        self.arrive(1, index)
        self.pass_on(4, self.up, index)
        self.pass_on(5, self.down, index)
        self.pass_on(9, self.sib, index)
        index = at.ctx_at(dz=-1)
        self.arrive(2, index)
        self.pass_on(6, self.up, index, 0)
        self.pass_on(10, self.sib, index)
        index = at.ctx_at(dz=1)
        self.arrive(3, index)
        self.pass_on(7, self.down, index, 1)
        self.pass_on(11, self.sib, index)

    def third(self):
        at = self.at
        index = at.ctx_at(dz=2)
        self.arrive(6, index, 0)
        self.arrive(7, index, 1)
        self.pass_on(8, self.xn, index)
        self.pass_on(14, self.sib, index)
        for event, dz, on in ((4, -1, 12), (5, 1, 13)):
            index = at.ctx_at(flip_col=True, dz=dz)
            self.arrive(event, index)
            self.pass_on(on, self.sib, index)

    def last(self):
        at = self.at
        index = at.ctx_at(flip_col=True, dz=2)
        self.arrive(8, index)
        self.pass_on(15, self.sib, index)

    def whole(self):
        at = self.at
        for event, flip_col, dz in (
            (0, False, 0), (9, True, 0), (10, False, -1), (11, False, 1),
            (12, True, -1), (13, True, 1), (14, False, 2), (15, True, 2),
        ):
            self.arrive(event, at.ctx_at(flip_col=flip_col, dz=dz, flip_core=True))

    halves = (6, 7)
    events = 16

    def close(self):
        for event in range(self.events):
            piece = self.slot(0, 0 if event in self.halves else None)
            pltpu.make_async_remote_copy(
                src_ref=piece, dst_ref=piece, send_sem=self.send.at[event],
                recv_sem=self.recv.at[event], device_id=self.sib, device_id_type=MESH,
            ).wait_send()


class Features:
    def __init__(self, at, own, buf, send, recv):
        self.at, self.own, self.buf, self.send, self.recv = at, own, buf, send, recv
        self.partner = self.sib = {"head": at.head_at(flip=True)}
        self.up = {"head": at.head_at(dy=1)}
        self.down = {"head": at.head_at(dy=-1)}

    def slot(self, index, half=None):
        cols = pl.ds(pl.multiple_of(index * 512, 512), 512)
        if half is None:
            return self.buf.at[:, cols]
        return self.buf.at[pl.ds(half * (ROWS // 2), ROWS // 2), cols]

    put, pass_on = Gather.put, Gather.pass_on

    def arrive(self, event, index, half=None):
        piece = self.slot(index, half)
        pltpu.make_async_remote_copy(
            src_ref=piece, dst_ref=piece, send_sem=self.send.at[event],
            recv_sem=self.recv.at[event], device_id=self.partner, device_id_type=MESH,
        ).wait_recv()

    def first(self):
        dst = self.slot(self.at.head)
        self.put(0, self.partner, self.own, dst)
        self.put(1, self.up, self.own, dst)
        self.put(2, self.down, self.own, dst)

    def second(self):
        at = self.at
        index = at.head_at(flip=True)
        self.arrive(0, index)
        self.pass_on(3, self.up, index)
        self.pass_on(4, self.down, index)
        index = at.head_at(dy=-1)
        self.arrive(1, index)
        self.pass_on(5, self.up, index, 0)
        index = at.head_at(dy=1)
        self.arrive(2, index)
        self.pass_on(6, self.down, index, 1)

    def third(self):
        at = self.at
        index = at.head_at(flip=True, dy=-1)
        self.arrive(3, index)
        self.pass_on(7, self.up, index, 0)
        index = at.head_at(flip=True, dy=1)
        self.arrive(4, index)
        self.pass_on(8, self.down, index, 1)

    def whole(self):
        at = self.at
        for event, flip in ((5, False), (7, True)):
            index = at.head_at(flip=flip, dy=2)
            self.arrive(event, index, 0)
            self.arrive(event + 1, index, 1)

    halves = (5, 6, 7, 8)
    events = 9
    close = Gather.close


def dot_nt(left, right):
    return lax.dot_general(
        left, right, (((1,), (1,)), ((), ())), preferred_element_type=jnp.float32
    )


def layer_kernel(
    x_ref, wk_ref, wv_ref, wq_ref, wo_ref, kern_ref, mix_ref, cos_ref, sin_ref, gain_ref, o_ref,
    x_buf, w_buf, wv_buf, k_buf, v_buf, wo_buf, made, qx, rim_in,
    q32, k32, qt, kc, lg, band, acc, mass, peaks, normed, part,
    y_half, y_sum, y_full, give, got,
    send, recv, x_send, x_recv, here, rim_sems, r_send, r_recv,
):
    at = Places()
    place = at.ctx
    r0 = place * ROWS
    blocks = lax.div(place + 2, 2)
    scale = 1.0 / math.sqrt(HD)
    after = {"ctx": lax.rem(at.ctx + 1, 16)}
    met = greet(
        [{"ctx": at.ctx_at(flip_core=True)}, {"ctx": at.ctx_at(flip_col=True)}]
        + [{"ctx": at.ctx_at(dz=1)}, {"ctx": at.ctx_at(dz=-1)}]
        + [{"head": at.head_at(dy=1)}, {"head": at.head_at(dy=-1)}, {"head": at.head_at(flip=True)}]
        + [after, {"ctx": lax.rem(at.ctx + 15, 16)}]
    )

    def gather(t, own, buf, rows, base=0):
        return Gather(at, own, buf, rows, send.at[t], recv.at[t], base)

    feats = Features(at, x_ref, x_buf, x_send, x_recv)
    wk = gather(0, wk_ref, w_buf, ROWS)
    wv = gather(1, wv_ref, wv_buf, ROWS)
    wq = gather(2, wq_ref, w_buf, ROWS, TOKENS)
    keys = gather(3, None, k_buf, ROWS, HD)
    values = gather(4, None, v_buf, ROWS)
    wo = gather(5, wo_ref, wo_buf, 2 * ROWS)
    keys.own = keys.slot(at.ctx)
    values.own = values.slot(at.ctx)

    own = [
        pltpu.make_async_copy(x_ref, feats.slot(at.head), here.at[0]),
        pltpu.make_async_copy(wk_ref, wk.slot(at.ctx), here.at[1]),
        pltpu.make_async_copy(wq_ref, wq.slot(at.ctx), here.at[3]),
        pltpu.make_async_copy(wv_ref, wv.slot(at.ctx), here.at[2]),
        pltpu.make_async_copy(wo_ref, wo.slot(at.ctx), here.at[4]),
    ]
    for copy in own:
        copy.start()
    k_buf[:HD] = jnp.zeros((HD, GROUP * HD), jnp.bfloat16)
    k_buf[HD + TOKENS :] = jnp.zeros((16, GROUP * HD), jnp.bfloat16)

    met()
    wk.first()
    feats.first()

    def project(buf):
        return jnp.dot(x_buf[...], buf[:TOKENS], preferred_element_type=jnp.float32)

    def rotate(projected):
        turned = []
        for h in range(GROUP):
            piece = projected[:, h * HD : (h + 1) * HD]
            turned.append(piece * cos_ref[...] + pltpu.roll(piece, HD // 2, 1) * sin_ref[...])
        return jnp.concatenate(turned, 1)

    def keep(index, value, dst):
        made[index] = value.astype(jnp.bfloat16)
        copy = pltpu.make_async_copy(made.at[index], dst, here.at[5 + index])
        copy.start()
        copy.wait()

    wk.second()
    feats.second()
    wq.first()
    wk.third()
    feats.third()
    wq.second()
    wv.first()
    wk.last()
    for copy in own:
        copy.wait()
    feats.whole()
    wk.whole()
    keep(0, rotate(project(w_buf.at[:TOKENS])), keys.slot(at.ctx))
    wq.third()
    keys.first()
    wv.second()
    wq.last()
    wq.whole()
    keep(2, rotate(project(w_buf.at[TOKENS:])), qx.at[pl.ds(16, ROWS)])
    rim = pltpu.make_async_remote_copy(
        src_ref=qx.at[pl.ds(ROWS, 16)], dst_ref=rim_in,
        send_sem=rim_sems.at[0], recv_sem=rim_sems.at[1], device_id=after, device_id_type=MESH,
    )
    rim.start()
    keys.second()
    wv.third()
    wo.first()
    rim.wait()
    qx[:16] = jnp.where(place > 0, rim_in[...], jnp.zeros_like(rim_in))
    for h in range(GROUP):
        q32[h] = qx[:, h * HD : (h + 1) * HD].astype(jnp.float32)[8:] * scale

    def mix_lags(r, _):
        for h in range(GROUP):
            view = q32.at[h, pl.ds(pl.multiple_of(r * 16, 16), 24)]
            lags = [view[8 - a : 24 - a] for a in range(CQ)]
            for c in range(CK):
                total = kern_ref[h, c] * lags[0]
                for a in range(1, CQ):
                    total = total + kern_ref[h, a * CK + c] * lags[a]
                qt[h, pl.ds(pl.multiple_of(r * 16, 16), 16), c * HD : (c + 1) * HD] = total.astype(
                    jnp.bfloat16
                )
        return 0

    keys.third()
    lax.fori_loop(0, ROWS // 16, mix_lags, 0)
    wv.last()
    keys.last()
    wv.whole()
    keep(1, project(wv_buf), values.slot(at.ctx))
    values.first()
    wo.second()
    keys.whole()

    steps = {1: [values.second], 2: [wo.third], 4: [values.third], 6: [wo.last]}

    def block_logits(b, _):
        for when, actions in steps.items():

            @pl.when(b == when)
            def _(actions=actions):
                for action in actions:
                    action()

        @pl.when(b < blocks)
        def _():
            for h in range(GROUP):
                rows = k_buf[pl.ds(pl.multiple_of(HD - 16 + b * KB, 16), KB + 32), h * HD : (h + 1) * HD]
                k32[h] = rows.astype(jnp.float32)
                for c in range(CK):
                    start = 16 + CK // 2 - c
                    kc[h % 2, :, c * HD : (c + 1) * HD] = k32[h, start : start + KB].astype(jnp.bfloat16)
                lg[h, :, pl.ds(pl.multiple_of(HD + b * KB, HD), KB)] = dot_nt(qt[h], kc[h % 2])

        return 0

    lax.fori_loop(0, 8, block_logits, 0)
    values.last()

    for s in range(2):
        for h in range(GROUP):
            cols = slice(h * HD, (h + 1) * HD)
            near = k_buf[pl.ds(pl.multiple_of(r0 + s * HD, HD), 2 * HD), cols]
            scores = dot_nt(qx[s * HD : s * HD + HD + 16, cols], near)[8:] * scale
            apart = (
                lax.broadcasted_iota(jnp.int32, scores.shape, 0)
                - lax.broadcasted_iota(jnp.int32, scores.shape, 1)
                + (HD - 8)
            )
            kept = jnp.where((apart >= 0) & (apart <= 24), scores, 0.0)
            band[s * GROUP + h, 0] = kept[:, :HD]
            band[s * GROUP + h, 1] = kept[:, HD:]

    row_in = lax.broadcasted_iota(jnp.int32, (8, HD), 0)
    col_in = lax.broadcasted_iota(jnp.int32, (8, HD), 1)

    def taps(h, lags, width):
        total = None
        for c in range(CK):
            piece = kern_ref[h, c] * lags[0]
            for a in range(1, CQ):
                piece = piece + kern_ref[h, a * CK + c] * lags[a]
            shift = (c - CK // 2) % width
            piece = pltpu.roll(piece, shift, 1) if shift else piece
            total = piece if total is None else total + piece
        return total

    def two_tiles(k, _):
        for s in range(2):
            here_cols = pl.ds(pl.multiple_of(HD + r0 + s * HD, HD), HD)
            prior = pl.ds(pl.multiple_of(r0 + s * HD, HD), HD)
            for h in range(GROUP):
                views = [
                    band.at[s * GROUP + h, t, pl.ds(pl.multiple_of(8 * k, 8), 16)] for t in range(2)
                ]
                lags = [
                    jnp.concatenate([view[8 - a : 16 - a] for view in views], 1) for a in range(CQ)
                ]
                direct = taps(h, lags, 2 * HD)
                rows = pl.ds(pl.multiple_of(s * HD + 8 * k, 8), 8)
                apart = 8 * k + row_in - col_in
                lg[h, rows, prior] = jnp.where(
                    apart + HD >= BAND, lg[h, rows, prior], direct[:, :HD]
                )
                lg[h, rows, here_cols] = jnp.where(
                    apart >= BAND,
                    lg[h, rows, here_cols],
                    jnp.where(apart >= 0, direct[:, HD:], -jnp.inf),
                )
        return 0

    def one_tile(k, _):
        for s in range(2):
            here_cols = pl.ds(pl.multiple_of(HD + r0 + s * HD, HD), HD)
            for h in range(GROUP):
                view = band.at[s * GROUP + h, 1, pl.ds(pl.multiple_of(8 * k, 8), 16)]
                direct = taps(h, [view[8 - a : 16 - a] for a in range(CQ)], HD)
                rows = pl.ds(pl.multiple_of(s * HD + 8 * k, 8), 8)
                apart = 8 * k + row_in - col_in
                lg[h, rows, here_cols] = jnp.where(
                    apart >= BAND,
                    lg[h, rows, here_cols],
                    jnp.where(apart >= 0, direct, -jnp.inf),
                )
        return 0

    lax.fori_loop(0, 2, two_tiles, 0)
    lax.fori_loop(2, HD // 8, one_tile, 0)
    for h in range(GROUP):
        lg[h, :HD, pl.ds(pl.multiple_of(2 * HD + r0, HD), HD)] = jnp.full(
            (HD, HD), -jnp.inf, jnp.float32
        )

    @pl.when(lax.rem(place, 2) == 0)
    def _():
        for h in range(GROUP):
            lg[h, :, pl.ds(pl.multiple_of(3 * HD + r0, HD), ROWS)] = jnp.full(
                (ROWS, ROWS), -jnp.inf, jnp.float32
            )

    for g in range(GROUP):

        def peak_of(b, peak, g=g):
            block = lg[g, :, pl.ds(pl.multiple_of(HD + b * KB, HD), KB)]
            for t in range(KB // HD):
                peak = jnp.maximum(peak, block[:, t * HD : (t + 1) * HD])
            return peak

        peak = lax.fori_loop(0, blocks, peak_of, jnp.full((ROWS, HD), -jnp.inf, jnp.float32))
        peaks[g] = jnp.broadcast_to(jnp.max(peak, axis=1, keepdims=True), (ROWS, HD))

    wk.close()
    wq.close()
    mass[...] = jnp.zeros_like(mass)

    def raise_block(b, _):
        for g in range(GROUP):
            for r in range(2):
                rows = slice(r * HALF, (r + 1) * HALF)
                peak = peaks[g, rows]
                total = mass[g, rows]
                first = b * GROUP * ROWS + (r * GROUP + g) * HALF
                for t in range(KB // HD):
                    block = lg[g, rows, pl.ds(pl.multiple_of(HD + b * KB + t * HD, HD), HD)]
                    probs = jnp.exp(block - peak)
                    total = total + probs
                    w_buf[pl.ds(pl.multiple_of(first, HALF), HALF), t * HD : (t + 1) * HD] = probs.astype(
                        jnp.bfloat16
                    )
                mass[g, rows] = total
        return 0

    lax.fori_loop(0, blocks, raise_block, 0)
    values.whole()

    up = {"head": at.head_at(dy=1)}
    down = {"head": at.head_at(dy=-1)}
    partner = {"head": at.head_at(flip=True)}
    chunk = ROWS // 4
    quarter = chunk // 2
    y_up, y_down, y_far = (lax.rem(at.y + d, 4) for d in (1, 3, 2))

    def ring_copy(r, event):
        target, src, dst = (
            (up, part.at[y_far, :, pl.ds(r * chunk, quarter)], y_half.at[r, 0]),
            (down, part.at[y_far, :, pl.ds(r * chunk + quarter, quarter)], y_half.at[r, 1]),
            (up, y_sum.at[r, 0], y_full.at[r, 0]),
            (down, y_sum.at[r, 1], y_full.at[r, 1]),
            (partner, give.at[r], got.at[r]),
        )[event]
        return pltpu.make_async_remote_copy(
            src_ref=src, dst_ref=dst, send_sem=r_send.at[r, event], recv_sem=r_recv.at[r, event],
            device_id=target, device_id_type=MESH,
        )

    def add(left, right):
        return (left.astype(jnp.float32) + right.astype(jnp.float32)).astype(jnp.bfloat16)

    def ring_first(r):
        ring_copy(r, 0).start()
        ring_copy(r, 1).start()
        y_sum[r, 0, :, quarter:] = part[y_up, :, r * chunk + quarter : (r + 1) * chunk]
        y_sum[r, 1, :, :quarter] = part[y_down, :, r * chunk : r * chunk + quarter]

    def ring_second(r):
        ring_copy(r, 0).wait_recv()
        y_sum[r, 0, :, :quarter] = add(part[y_up, :, r * chunk : r * chunk + quarter], y_half[r, 0])
        ring_copy(r, 2).start()
        ring_copy(r, 1).wait_recv()
        y_sum[r, 1, :, quarter:] = add(part[y_down, :, r * chunk + quarter : (r + 1) * chunk], y_half[r, 1])
        ring_copy(r, 3).start()

    def ring_total(r, far):
        return (
            part[at.y, far, r * chunk : (r + 1) * chunk].astype(jnp.float32)
            + y_full[r, 0, far].astype(jnp.float32)
            + y_full[r, 1, far].astype(jnp.float32)
        )

    def ring_third(r):
        ring_copy(r, 2).wait_recv()
        ring_copy(r, 3).wait_recv()
        give[r] = ring_total(r, 1 - at.far).astype(jnp.bfloat16)
        ring_copy(r, 4).start()

    def ring_last(r):
        mine = ring_total(r, at.far)
        ring_copy(r, 4).wait_recv()
        total = mine + got[r].astype(jnp.float32)
        o_ref[r * chunk : (r + 1) * chunk] = total.astype(jnp.bfloat16)

    for r in range(2):
        rows = slice(r * HALF, (r + 1) * HALF)
        acc[...] = jnp.zeros_like(acc)

        def weigh(b, _, r=r):
            first = b * GROUP * ROWS + r * GROUP * HALF
            left = w_buf[pl.ds(pl.multiple_of(first, HALF), GROUP * HALF)]
            block = v_buf[pl.ds(pl.multiple_of(b * KB, KB), KB), :]
            acc[...] += jnp.dot(left, block, preferred_element_type=jnp.float32)
            return 0

        lax.fori_loop(0, blocks, weigh, 0)
        inverse = [
            jnp.broadcast_to(1.0 / jnp.sum(mass[g, rows], axis=1, keepdims=True), (HALF, HD))
            for g in range(GROUP)
        ]
        for h in range(GROUP):
            cols = slice(h * HD, (h + 1) * HD)
            total = mix_ref[h, 0] * (acc[:HALF, cols] * inverse[0])
            for g in range(1, GROUP):
                total = total + mix_ref[h, g] * (acc[g * HALF : (g + 1) * HALF, cols] * inverse[g])
            rms = jnp.sqrt(jnp.mean(total * total, axis=1, keepdims=True) + 1e-05)
            normed[rows, cols] = (total / rms * gain_ref[:, cols]).astype(jnp.bfloat16)

    wo.whole()

    def project_out(r):
        rows = slice(r * HALF, (r + 1) * HALF)

        def out_block(b, _):
            width = GROUP * HD
            source = pl.ds(pl.multiple_of(b * width, width), width)
            piece = jnp.dot(normed[rows], wo_buf[source], preferred_element_type=jnp.float32)
            far, y, side = lax.div(b, 8), lax.rem(lax.div(b, 2), 4), lax.rem(b, 2)
            part[y, far, rows, pl.ds(pl.multiple_of(side * ROWS, ROWS), ROWS)] = piece.astype(jnp.bfloat16)
            return 0

        lax.fori_loop(0, 16, out_block, 0)

    project_out(0)
    ring_first(0)
    ring_first(1)
    project_out(1)
    ring_first(2)
    ring_second(0)
    ring_first(3)
    ring_second(1)
    ring_third(0)
    ring_second(2)
    ring_third(1)
    ring_second(3)
    ring_third(2)
    ring_last(0)
    ring_last(1)
    ring_third(3)
    ring_last(2)
    ring_last(3)
    for r in range(4):
        for event in range(5):
            ring_copy(r, event).wait_send()
    for each in (feats, wv, keys, values, wo):
        each.close()


def layer(*operands):
    smem = pl.BlockSpec(memory_space=pltpu.SMEM)
    vmem = pl.BlockSpec(memory_space=pltpu.VMEM)
    hbm = pl.BlockSpec(memory_space=pltpu.HBM)
    width = GROUP * HD
    half = lambda *dims: pltpu.VMEM(dims, jnp.bfloat16)
    full = lambda *dims: pltpu.VMEM(dims, jnp.float32)
    dma = pltpu.SemaphoreType.DMA
    return pl.pallas_call(
        layer_kernel,
        out_shape=jax.ShapeDtypeStruct((ROWS, width), jnp.bfloat16),
        in_specs=[hbm] * 5 + [smem] * 2 + [vmem] * 3,
        out_specs=vmem,
        scratch_shapes=[
            half(ROWS, TOKENS), half(2 * TOKENS, width), half(TOKENS, width),
            half(HD + TOKENS + 16, width), half(TOKENS, width), half(16 * width, ROWS),
            half(3, ROWS, width), half(ROWS + 16, width), half(16, width),
            full(GROUP, ROWS + 8, HD), full(GROUP, KB + 32, HD),
            half(GROUP, ROWS, CK * HD), half(2, KB, CK * HD),
            full(GROUP, ROWS, HD + TOKENS), full(2 * GROUP, 2, HD + 8, HD),
            full(GROUP * HALF, width),
            full(GROUP, ROWS, HD), full(GROUP, ROWS, HD), half(ROWS, width),
            half(4, 2, ROWS, width),
            half(4, 2, 2, ROWS // 8, width), half(4, 2, 2, ROWS // 4, width), half(4, 2, 2, ROWS // 4, width),
            half(4, ROWS // 4, width), half(4, ROWS // 4, width),
            dma((6, 16)), dma((6, 16)), dma((9,)), dma((9,)), dma((8,)), dma((2,)), dma((4, 5)), dma((4, 5)),
        ],
        compiler_params=pltpu.CompilerParams(
            collective_id=1, has_side_effects=True, vmem_limit_bytes=67043328
        ),
        name="layer",
    )(*operands)


def per_device(
    activations, positions, w_query, w_key, w_value, conv_kernel, head_mix, out_gain, w_out
):
    exponents = jnp.arange(HD // 2, dtype=jnp.float32) * (2.0 / HD)
    inverse = jnp.exp(-exponents * math.log(500000.0))
    angle = (positions.astype(jnp.float32) * 0.25)[:, None] * inverse[None, :]
    cosine = jnp.cos(angle)
    sine = jnp.sin(angle)
    return layer(
        activations, w_key, w_value, w_query, w_out, conv_kernel, head_mix,
        jnp.concatenate([cosine, cosine], 1), jnp.concatenate([-sine, sine], 1),
        out_gain.reshape(1, -1),
    )


def solution(mesh):
    return jax.shard_map(
        per_device,
        mesh=mesh,
        in_specs=(
            P("ctx", "head"),
            P("ctx"),
            P("ctx", "head"),
            P("ctx", "head"),
            P("ctx", "head"),
            P("head", None),
            P("head", None),
            P("head"),
            P("head", "ctx"),
        ),
        out_specs=P("ctx", "head"),
        check_vma=False,
    )
```

```python
import math

import jax
import jax.numpy as jnp
from jax import lax
from jax.experimental import pallas as pl
from jax.experimental.pallas import tpu as pltpu
from jax.sharding import PartitionSpec as P

HD = 128
GROUP = 4
CQ = 6
CK = 11
KB = 512
ROWS = 256
TOKENS = 4096
HALF = 128
BAND = 10


MESH = pl.DeviceIdType.MESH


class Places:
    def __init__(self):
        self.ctx = lax.axis_index("ctx")
        self.head = lax.axis_index("head")
        self.col = lax.div(self.ctx, 8)
        self.z = lax.rem(lax.div(self.ctx, 2), 4)
        self.core = lax.rem(self.ctx, 2)
        self.y = lax.rem(self.head, 4)
        self.far = lax.div(self.head, 4)

    def ctx_at(self, flip_col=False, dz=0, flip_core=False):
        col = 1 - self.col if flip_col else self.col
        core = 1 - self.core if flip_core else self.core
        return col * 8 + lax.rem(self.z + dz + 4, 4) * 2 + core

    def head_at(self, flip=False, dy=0):
        far = 1 - self.far if flip else self.far
        return far * 4 + lax.rem(self.y + dy + 4, 4)


def greet(targets):
    barrier = pltpu.get_barrier_semaphore()
    for target in targets:
        pl.semaphore_signal(barrier, inc=1, device_id=target, device_id_type=MESH)
    return lambda: pl.semaphore_wait(barrier, len(targets))


class Gather:
    def __init__(self, at, own, buf, rows, send, recv, base=0):
        self.at, self.own, self.buf, self.rows, self.send, self.recv = at, own, buf, rows, send, recv
        self.base = base
        self.sib = {"ctx": at.ctx_at(flip_core=True)}
        self.xn = {"ctx": at.ctx_at(flip_col=True)}
        self.up = {"ctx": at.ctx_at(dz=1)}
        self.down = {"ctx": at.ctx_at(dz=-1)}

    def slot(self, index, half=None):
        size = self.rows if half is None else self.rows // 2
        first = self.base + index * self.rows + (size if half == 1 else 0)
        return self.buf.at[pl.ds(pl.multiple_of(first, 128), size), :]

    def put(self, event, target, src, dst):
        copy = pltpu.make_async_remote_copy(
            src_ref=src, dst_ref=dst, send_sem=self.send.at[event], recv_sem=self.recv.at[event],
            device_id=target, device_id_type=MESH,
        )
        copy.start()

    def pass_on(self, event, target, index, half=None):
        piece = self.slot(index, half)
        self.put(event, target, piece, piece)

    def arrive(self, event, index, half=None):
        piece = self.slot(index, half)
        pltpu.make_async_remote_copy(
            src_ref=piece, dst_ref=piece, send_sem=self.send.at[event],
            recv_sem=self.recv.at[event], device_id=self.sib, device_id_type=MESH,
        ).wait_recv()

    def first(self):
        dst = self.slot(self.at.ctx)
        self.put(2, self.up, self.own, dst)
        self.put(3, self.down, self.own, dst)
        self.put(1, self.xn, self.own, dst)
        self.put(0, self.sib, self.own, dst)

    def second(self):
        at = self.at
        index = at.ctx_at(flip_col=True)
        self.arrive(1, index)
        self.pass_on(4, self.up, index)
        self.pass_on(5, self.down, index)
        self.pass_on(9, self.sib, index)
        index = at.ctx_at(dz=-1)
        self.arrive(2, index)
        self.pass_on(6, self.up, index, 0)
        self.pass_on(10, self.sib, index)
        index = at.ctx_at(dz=1)
        self.arrive(3, index)
        self.pass_on(7, self.down, index, 1)
        self.pass_on(11, self.sib, index)

    def third(self):
        at = self.at
        index = at.ctx_at(dz=2)
        self.arrive(6, index, 0)
        self.arrive(7, index, 1)
        self.pass_on(8, self.xn, index)
        self.pass_on(14, self.sib, index)
        for event, dz, on in ((4, -1, 12), (5, 1, 13)):
            index = at.ctx_at(flip_col=True, dz=dz)
            self.arrive(event, index)
            self.pass_on(on, self.sib, index)

    def last(self):
        at = self.at
        index = at.ctx_at(flip_col=True, dz=2)
        self.arrive(8, index)
        self.pass_on(15, self.sib, index)

    def whole(self):
        at = self.at
        for event, flip_col, dz in (
            (0, False, 0), (9, True, 0), (10, False, -1), (11, False, 1),
            (12, True, -1), (13, True, 1), (14, False, 2), (15, True, 2),
        ):
            self.arrive(event, at.ctx_at(flip_col=flip_col, dz=dz, flip_core=True))

    halves = (6, 7)
    events = 16

    def close(self):
        for event in range(self.events):
            piece = self.slot(0, 0 if event in self.halves else None)
            pltpu.make_async_remote_copy(
                src_ref=piece, dst_ref=piece, send_sem=self.send.at[event],
                recv_sem=self.recv.at[event], device_id=self.sib, device_id_type=MESH,
            ).wait_send()


class Features:
    def __init__(self, at, own, buf, send, recv):
        self.at, self.own, self.buf, self.send, self.recv = at, own, buf, send, recv
        self.partner = self.sib = {"head": at.head_at(flip=True)}
        self.up = {"head": at.head_at(dy=1)}
        self.down = {"head": at.head_at(dy=-1)}

    def slot(self, index, half=None):
        cols = pl.ds(pl.multiple_of(index * 512, 512), 512)
        if half is None:
            return self.buf.at[:, cols]
        return self.buf.at[pl.ds(half * (ROWS // 2), ROWS // 2), cols]

    put, pass_on = Gather.put, Gather.pass_on

    def arrive(self, event, index, half=None):
        piece = self.slot(index, half)
        pltpu.make_async_remote_copy(
            src_ref=piece, dst_ref=piece, send_sem=self.send.at[event],
            recv_sem=self.recv.at[event], device_id=self.partner, device_id_type=MESH,
        ).wait_recv()

    def first(self):
        dst = self.slot(self.at.head)
        self.put(0, self.partner, self.own, dst)
        self.put(1, self.up, self.own, dst)
        self.put(2, self.down, self.own, dst)

    def second(self):
        at = self.at
        index = at.head_at(flip=True)
        self.arrive(0, index)
        self.pass_on(3, self.up, index)
        self.pass_on(4, self.down, index)
        index = at.head_at(dy=-1)
        self.arrive(1, index)
        self.pass_on(5, self.up, index, 0)
        index = at.head_at(dy=1)
        self.arrive(2, index)
        self.pass_on(6, self.down, index, 1)

    def third(self):
        at = self.at
        index = at.head_at(flip=True, dy=-1)
        self.arrive(3, index)
        self.pass_on(7, self.up, index, 0)
        index = at.head_at(flip=True, dy=1)
        self.arrive(4, index)
        self.pass_on(8, self.down, index, 1)

    def whole(self):
        at = self.at
        for event, flip in ((5, False), (7, True)):
            index = at.head_at(flip=flip, dy=2)
            self.arrive(event, index, 0)
            self.arrive(event + 1, index, 1)

    halves = (5, 6, 7, 8)
    events = 9
    close = Gather.close


def dot_nt(left, right):
    return lax.dot_general(
        left, right, (((1,), (1,)), ((), ())), preferred_element_type=jnp.float32
    )


def layer_kernel(
    x_ref, wk_ref, wv_ref, wq_ref, wo_ref, kern_ref, mix_ref, cos_ref, sin_ref, gain_ref, o_ref,
    x_buf, w_buf, wv_buf, k_buf, v_buf, wo_buf, made, qx, rim_in,
    q32, k32, qt, kc, lg, band, acc, mass, peaks, normed, part,
    y_half, y_sum, y_full, give, got,
    send, recv, x_send, x_recv, here, rim_sems, r_send, r_recv,
):
    at = Places()
    place = at.ctx
    r0 = place * ROWS
    blocks = lax.div(place + 2, 2)
    scale = 1.0 / math.sqrt(HD)
    after = {"ctx": lax.rem(at.ctx + 1, 16)}
    met = greet(
        [{"ctx": at.ctx_at(flip_core=True)}, {"ctx": at.ctx_at(flip_col=True)}]
        + [{"ctx": at.ctx_at(dz=1)}, {"ctx": at.ctx_at(dz=-1)}]
        + [{"head": at.head_at(dy=1)}, {"head": at.head_at(dy=-1)}, {"head": at.head_at(flip=True)}]
        + [after, {"ctx": lax.rem(at.ctx + 15, 16)}]
    )

    def gather(t, own, buf, rows, base=0):
        return Gather(at, own, buf, rows, send.at[t], recv.at[t], base)

    feats = Features(at, x_ref, x_buf, x_send, x_recv)
    wk = gather(0, wk_ref, w_buf, ROWS)
    wv = gather(1, wv_ref, wv_buf, ROWS)
    wq = gather(2, wq_ref, w_buf, ROWS, TOKENS)
    keys = gather(3, None, k_buf, ROWS, HD)
    values = gather(4, None, v_buf, ROWS)
    wo = gather(5, wo_ref, wo_buf, 2 * ROWS)
    keys.own = keys.slot(at.ctx)
    values.own = values.slot(at.ctx)

    own = [
        pltpu.make_async_copy(x_ref, feats.slot(at.head), here.at[0]),
        pltpu.make_async_copy(wk_ref, wk.slot(at.ctx), here.at[1]),
        pltpu.make_async_copy(wq_ref, wq.slot(at.ctx), here.at[3]),
        pltpu.make_async_copy(wv_ref, wv.slot(at.ctx), here.at[2]),
        pltpu.make_async_copy(wo_ref, wo.slot(at.ctx), here.at[4]),
    ]
    for copy in own:
        copy.start()
    k_buf[:HD] = jnp.zeros((HD, GROUP * HD), jnp.bfloat16)
    k_buf[HD + TOKENS :] = jnp.zeros((16, GROUP * HD), jnp.bfloat16)

    met()
    wk.first()
    feats.first()

    def project(buf):
        return jnp.dot(x_buf[...], buf[:TOKENS], preferred_element_type=jnp.float32)

    def rotate(projected):
        turned = []
        for h in range(GROUP):
            piece = projected[:, h * HD : (h + 1) * HD]
            turned.append(piece * cos_ref[...] + pltpu.roll(piece, HD // 2, 1) * sin_ref[...])
        return jnp.concatenate(turned, 1)

    def keep(index, value, dst):
        made[index] = value.astype(jnp.bfloat16)
        copy = pltpu.make_async_copy(made.at[index], dst, here.at[5 + index])
        copy.start()
        copy.wait()

    wk.second()
    feats.second()
    wq.first()
    wk.third()
    feats.third()
    wq.second()
    wv.first()
    wk.last()
    for copy in own:
        copy.wait()
    feats.whole()
    wk.whole()
    keep(0, rotate(project(w_buf.at[:TOKENS])), keys.slot(at.ctx))
    wq.third()
    keys.first()
    wv.second()
    wq.last()
    wq.whole()
    keep(2, rotate(project(w_buf.at[TOKENS:])), qx.at[pl.ds(16, ROWS)])
    rim = pltpu.make_async_remote_copy(
        src_ref=qx.at[pl.ds(ROWS, 16)], dst_ref=rim_in,
        send_sem=rim_sems.at[0], recv_sem=rim_sems.at[1], device_id=after, device_id_type=MESH,
    )
    rim.start()
    keys.second()
    wv.third()
    wo.first()
    rim.wait()
    qx[:16] = jnp.where(place > 0, rim_in[...], jnp.zeros_like(rim_in))
    for h in range(GROUP):
        q32[h] = qx[:, h * HD : (h + 1) * HD].astype(jnp.float32)[8:] * scale

    def mix_lags(r, _):
        for h in range(GROUP):
            view = q32.at[h, pl.ds(pl.multiple_of(r * 16, 16), 24)]
            lags = [view[8 - a : 24 - a] for a in range(CQ)]
            for c in range(CK):
                total = kern_ref[h, c] * lags[0]
                for a in range(1, CQ):
                    total = total + kern_ref[h, a * CK + c] * lags[a]
                qt[h, pl.ds(pl.multiple_of(r * 16, 16), 16), c * HD : (c + 1) * HD] = total.astype(
                    jnp.bfloat16
                )
        return 0

    keys.third()
    lax.fori_loop(0, ROWS // 16, mix_lags, 0)
    wv.last()
    keys.last()
    wv.whole()
    keep(1, project(wv_buf), values.slot(at.ctx))
    values.first()
    wo.second()
    keys.whole()

    steps = {2: [values.second], 5: [wo.third]}

    def block_logits(b, _):
        for when, actions in steps.items():

            @pl.when(b == when)
            def _(actions=actions):
                for action in actions:
                    action()

        @pl.when(b < blocks)
        def _():
            for h in range(GROUP):
                rows = k_buf[pl.ds(pl.multiple_of(HD - 16 + b * KB, 16), KB + 32), h * HD : (h + 1) * HD]
                k32[h] = rows.astype(jnp.float32)
                for c in range(CK):
                    start = 16 + CK // 2 - c
                    kc[h % 2, :, c * HD : (c + 1) * HD] = k32[h, start : start + KB].astype(jnp.bfloat16)
                lg[h, :, pl.ds(pl.multiple_of(HD + b * KB, HD), KB)] = dot_nt(qt[h], kc[h % 2])

        return 0

    lax.fori_loop(0, 8, block_logits, 0)
    values.third()

    for s in range(2):
        for h in range(GROUP):
            cols = slice(h * HD, (h + 1) * HD)
            near = k_buf[pl.ds(pl.multiple_of(r0 + s * HD, HD), 2 * HD), cols]
            scores = dot_nt(qx[s * HD : s * HD + HD + 16, cols], near)[8:] * scale
            apart = (
                lax.broadcasted_iota(jnp.int32, scores.shape, 0)
                - lax.broadcasted_iota(jnp.int32, scores.shape, 1)
                + (HD - 8)
            )
            kept = jnp.where((apart >= 0) & (apart <= 24), scores, 0.0)
            band[s * GROUP + h, 0] = kept[:, :HD]
            band[s * GROUP + h, 1] = kept[:, HD:]

    row_in = lax.broadcasted_iota(jnp.int32, (8, HD), 0)
    col_in = lax.broadcasted_iota(jnp.int32, (8, HD), 1)

    def taps(h, lags, width):
        total = None
        for c in range(CK):
            piece = kern_ref[h, c] * lags[0]
            for a in range(1, CQ):
                piece = piece + kern_ref[h, a * CK + c] * lags[a]
            shift = (c - CK // 2) % width
            piece = pltpu.roll(piece, shift, 1) if shift else piece
            total = piece if total is None else total + piece
        return total

    def two_tiles(k, _):
        for s in range(2):
            here_cols = pl.ds(pl.multiple_of(HD + r0 + s * HD, HD), HD)
            prior = pl.ds(pl.multiple_of(r0 + s * HD, HD), HD)
            for h in range(GROUP):
                views = [
                    band.at[s * GROUP + h, t, pl.ds(pl.multiple_of(8 * k, 8), 16)] for t in range(2)
                ]
                lags = [
                    jnp.concatenate([view[8 - a : 16 - a] for view in views], 1) for a in range(CQ)
                ]
                direct = taps(h, lags, 2 * HD)
                rows = pl.ds(pl.multiple_of(s * HD + 8 * k, 8), 8)
                apart = 8 * k + row_in - col_in
                lg[h, rows, prior] = jnp.where(
                    apart + HD >= BAND, lg[h, rows, prior], direct[:, :HD]
                )
                lg[h, rows, here_cols] = jnp.where(
                    apart >= BAND,
                    lg[h, rows, here_cols],
                    jnp.where(apart >= 0, direct[:, HD:], -jnp.inf),
                )
        return 0

    def one_tile(k, _):
        for s in range(2):
            here_cols = pl.ds(pl.multiple_of(HD + r0 + s * HD, HD), HD)
            for h in range(GROUP):
                view = band.at[s * GROUP + h, 1, pl.ds(pl.multiple_of(8 * k, 8), 16)]
                direct = taps(h, [view[8 - a : 16 - a] for a in range(CQ)], HD)
                rows = pl.ds(pl.multiple_of(s * HD + 8 * k, 8), 8)
                apart = 8 * k + row_in - col_in
                lg[h, rows, here_cols] = jnp.where(
                    apart >= BAND,
                    lg[h, rows, here_cols],
                    jnp.where(apart >= 0, direct, -jnp.inf),
                )
        return 0

    lax.fori_loop(0, 2, two_tiles, 0)
    lax.fori_loop(2, HD // 8, one_tile, 0)
    for h in range(GROUP):
        lg[h, :HD, pl.ds(pl.multiple_of(2 * HD + r0, HD), HD)] = jnp.full(
            (HD, HD), -jnp.inf, jnp.float32
        )

    @pl.when(lax.rem(place, 2) == 0)
    def _():
        for h in range(GROUP):
            lg[h, :, pl.ds(pl.multiple_of(3 * HD + r0, HD), ROWS)] = jnp.full(
                (ROWS, ROWS), -jnp.inf, jnp.float32
            )

    values.last()
    for g in range(GROUP):

        def peak_of(b, peak, g=g):
            block = lg[g, :, pl.ds(pl.multiple_of(HD + b * KB, HD), KB)]
            for t in range(KB // HD):
                peak = jnp.maximum(peak, block[:, t * HD : (t + 1) * HD])
            return peak

        peak = lax.fori_loop(0, blocks, peak_of, jnp.full((ROWS, HD), -jnp.inf, jnp.float32))
        peaks[g] = jnp.broadcast_to(jnp.max(peak, axis=1, keepdims=True), (ROWS, HD))

    wk.close()
    wq.close()
    mass[...] = jnp.zeros_like(mass)

    def raise_block(b, _):
        for g in range(GROUP):
            for r in range(2):
                rows = slice(r * HALF, (r + 1) * HALF)
                peak = peaks[g, rows]
                total = mass[g, rows]
                first = b * GROUP * ROWS + (r * GROUP + g) * HALF
                for t in range(KB // HD):
                    block = lg[g, rows, pl.ds(pl.multiple_of(HD + b * KB + t * HD, HD), HD)]
                    probs = jnp.exp(block - peak)
                    total = total + probs
                    w_buf[pl.ds(pl.multiple_of(first, HALF), HALF), t * HD : (t + 1) * HD] = probs.astype(
                        jnp.bfloat16
                    )
                mass[g, rows] = total
        return 0

    lax.fori_loop(0, blocks, raise_block, 0)
    wo.last()
    values.whole()

    up = {"head": at.head_at(dy=1)}
    down = {"head": at.head_at(dy=-1)}
    partner = {"head": at.head_at(flip=True)}
    chunk = ROWS // 4
    quarter = chunk // 2
    y_up, y_down, y_far = (lax.rem(at.y + d, 4) for d in (1, 3, 2))

    def ring_copy(r, event):
        target, src, dst = (
            (up, part.at[y_far, :, pl.ds(r * chunk, quarter)], y_half.at[r, 0]),
            (down, part.at[y_far, :, pl.ds(r * chunk + quarter, quarter)], y_half.at[r, 1]),
            (up, y_sum.at[r, 0], y_full.at[r, 0]),
            (down, y_sum.at[r, 1], y_full.at[r, 1]),
            (partner, give.at[r], got.at[r]),
        )[event]
        return pltpu.make_async_remote_copy(
            src_ref=src, dst_ref=dst, send_sem=r_send.at[r, event], recv_sem=r_recv.at[r, event],
            device_id=target, device_id_type=MESH,
        )

    def add(left, right):
        return (left.astype(jnp.float32) + right.astype(jnp.float32)).astype(jnp.bfloat16)

    def ring_first(r):
        ring_copy(r, 0).start()
        ring_copy(r, 1).start()

    def ring_second(r):
        y_sum[r, 0, :, quarter:] = part[y_up, :, r * chunk + quarter : (r + 1) * chunk]
        y_sum[r, 1, :, :quarter] = part[y_down, :, r * chunk : r * chunk + quarter]
        ring_copy(r, 0).wait_recv()
        y_sum[r, 0, :, :quarter] = add(part[y_up, :, r * chunk : r * chunk + quarter], y_half[r, 0])
        ring_copy(r, 2).start()
        ring_copy(r, 1).wait_recv()
        y_sum[r, 1, :, quarter:] = add(part[y_down, :, r * chunk + quarter : (r + 1) * chunk], y_half[r, 1])
        ring_copy(r, 3).start()

    def ring_total(r, far):
        return (
            part[at.y, far, r * chunk : (r + 1) * chunk].astype(jnp.float32)
            + y_full[r, 0, far].astype(jnp.float32)
            + y_full[r, 1, far].astype(jnp.float32)
        )

    def ring_third(r):
        ring_copy(r, 2).wait_recv()
        ring_copy(r, 3).wait_recv()
        give[r] = ring_total(r, 1 - at.far).astype(jnp.bfloat16)
        ring_copy(r, 4).start()

    def ring_last(r):
        mine = ring_total(r, at.far)
        ring_copy(r, 4).wait_recv()
        total = mine + got[r].astype(jnp.float32)
        o_ref[r * chunk : (r + 1) * chunk] = total.astype(jnp.bfloat16)

    for r in range(2):
        rows = slice(r * HALF, (r + 1) * HALF)
        acc[...] = jnp.zeros_like(acc)

        def weigh(b, _, r=r):
            first = b * GROUP * ROWS + r * GROUP * HALF
            left = w_buf[pl.ds(pl.multiple_of(first, HALF), GROUP * HALF)]
            block = v_buf[pl.ds(pl.multiple_of(b * KB, KB), KB), :]
            acc[...] += jnp.dot(left, block, preferred_element_type=jnp.float32)
            return 0

        lax.fori_loop(0, blocks, weigh, 0)
        inverse = [
            jnp.broadcast_to(1.0 / jnp.sum(mass[g, rows], axis=1, keepdims=True), (HALF, HD))
            for g in range(GROUP)
        ]
        for h in range(GROUP):
            cols = slice(h * HD, (h + 1) * HD)
            total = mix_ref[h, 0] * (acc[:HALF, cols] * inverse[0])
            for g in range(1, GROUP):
                total = total + mix_ref[h, g] * (acc[g * HALF : (g + 1) * HALF, cols] * inverse[g])
            rms = jnp.sqrt(jnp.mean(total * total, axis=1, keepdims=True) + 1e-05)
            normed[rows, cols] = (total / rms * gain_ref[:, cols]).astype(jnp.bfloat16)

    wo.whole()

    def project_out(step):
        y = lax.rem(at.y + step, 4)
        for far in range(2):
            for side in range(2):
                first = (far * 8 + y * 2 + side) * GROUP * HD
                source = pl.ds(pl.multiple_of(first, GROUP * HD), GROUP * HD)
                piece = jnp.dot(normed[...], wo_buf[source], preferred_element_type=jnp.float32)
                part[y, far, :, side * ROWS : (side + 1) * ROWS] = piece.astype(jnp.bfloat16)

    project_out(2)
    for r in range(4):
        ring_first(r)
    project_out(1)
    project_out(3)
    for r in range(4):
        ring_second(r)
    project_out(0)
    ring_third(0)
    ring_third(1)
    ring_third(2)
    ring_last(0)
    ring_third(3)
    ring_last(1)
    ring_last(2)
    ring_last(3)
    for r in range(4):
        for event in range(5):
            ring_copy(r, event).wait_send()
    for each in (feats, wv, keys, values, wo):
        each.close()


def layer(*operands):
    smem = pl.BlockSpec(memory_space=pltpu.SMEM)
    vmem = pl.BlockSpec(memory_space=pltpu.VMEM)
    hbm = pl.BlockSpec(memory_space=pltpu.HBM)
    width = GROUP * HD
    half = lambda *dims: pltpu.VMEM(dims, jnp.bfloat16)
    full = lambda *dims: pltpu.VMEM(dims, jnp.float32)
    dma = pltpu.SemaphoreType.DMA
    return pl.pallas_call(
        layer_kernel,
        out_shape=jax.ShapeDtypeStruct((ROWS, width), jnp.bfloat16),
        in_specs=[hbm] * 5 + [smem] * 2 + [vmem] * 3,
        out_specs=vmem,
        scratch_shapes=[
            half(ROWS, TOKENS), half(2 * TOKENS, width), half(TOKENS, width),
            half(HD + TOKENS + 16, width), half(TOKENS, width), half(16 * width, ROWS),
            half(3, ROWS, width), half(ROWS + 16, width), half(16, width),
            full(GROUP, ROWS + 8, HD), full(GROUP, KB + 32, HD),
            half(GROUP, ROWS, CK * HD), half(2, KB, CK * HD),
            full(GROUP, ROWS, HD + TOKENS), full(2 * GROUP, 2, HD + 8, HD),
            full(GROUP * HALF, width),
            full(GROUP, ROWS, HD), full(GROUP, ROWS, HD), half(ROWS, width),
            half(4, 2, ROWS, width),
            half(4, 2, 2, ROWS // 8, width), half(4, 2, 2, ROWS // 4, width), half(4, 2, 2, ROWS // 4, width),
            half(4, ROWS // 4, width), half(4, ROWS // 4, width),
            dma((6, 16)), dma((6, 16)), dma((9,)), dma((9,)), dma((8,)), dma((2,)), dma((4, 5)), dma((4, 5)),
        ],
        compiler_params=pltpu.CompilerParams(
            collective_id=1, has_side_effects=True, vmem_limit_bytes=67043328
        ),
        name="layer",
    )(*operands)


def per_device(
    activations, positions, w_query, w_key, w_value, conv_kernel, head_mix, out_gain, w_out
):
    exponents = jnp.arange(HD // 2, dtype=jnp.float32) * (2.0 / HD)
    inverse = jnp.exp(-exponents * math.log(500000.0))
    angle = (positions.astype(jnp.float32) * 0.25)[:, None] * inverse[None, :]
    cosine = jnp.cos(angle)
    sine = jnp.sin(angle)
    return layer(
        activations, w_key, w_value, w_query, w_out, conv_kernel, head_mix,
        jnp.concatenate([cosine, cosine], 1), jnp.concatenate([-sine, sine], 1),
        out_gain.reshape(1, -1),
    )


def solution(mesh):
    return jax.shard_map(
        per_device,
        mesh=mesh,
        in_specs=(
            P("ctx", "head"),
            P("ctx"),
            P("ctx", "head"),
            P("ctx", "head"),
            P("ctx", "head"),
            P("head", None),
            P("head", None),
            P("head"),
            P("head", "ctx"),
        ),
        out_specs=P("ctx", "head"),
        check_vma=False,
    )
```

```python
import math

import jax
import jax.numpy as jnp
from jax import lax
from jax.experimental import pallas as pl
from jax.experimental.pallas import tpu as pltpu
from jax.sharding import PartitionSpec as P

HD = 128
GROUP = 4
CQ = 6
CK = 11
KB = 512
ROWS = 256
TOKENS = 4096
HALF = 128
BAND = 10


MESH = pl.DeviceIdType.MESH


class Places:
    def __init__(self):
        self.ctx = lax.axis_index("ctx")
        self.head = lax.axis_index("head")
        self.col = lax.div(self.ctx, 8)
        self.z = lax.rem(lax.div(self.ctx, 2), 4)
        self.core = lax.rem(self.ctx, 2)
        self.y = lax.rem(self.head, 4)
        self.far = lax.div(self.head, 4)

    def ctx_at(self, flip_col=False, dz=0, flip_core=False):
        col = 1 - self.col if flip_col else self.col
        core = 1 - self.core if flip_core else self.core
        return col * 8 + lax.rem(self.z + dz + 4, 4) * 2 + core

    def head_at(self, flip=False, dy=0):
        far = 1 - self.far if flip else self.far
        return far * 4 + lax.rem(self.y + dy + 4, 4)


def greet(targets):
    barrier = pltpu.get_barrier_semaphore()
    for target in targets:
        pl.semaphore_signal(barrier, inc=1, device_id=target, device_id_type=MESH)
    return lambda: pl.semaphore_wait(barrier, len(targets))


class Gather:
    def __init__(self, at, own, buf, rows, send, recv, base=0):
        self.at, self.own, self.buf, self.rows, self.send, self.recv = at, own, buf, rows, send, recv
        self.base = base
        self.sib = {"ctx": at.ctx_at(flip_core=True)}
        self.xn = {"ctx": at.ctx_at(flip_col=True)}
        self.up = {"ctx": at.ctx_at(dz=1)}
        self.down = {"ctx": at.ctx_at(dz=-1)}

    def slot(self, index, half=None):
        short = self.rows * 3 // 16
        at, size = {
            None: (0, self.rows), 0: (0, self.rows // 2), 1: (self.rows // 2, self.rows // 2),
            2: (0, self.rows - short), 3: (self.rows - short, short),
        }[half]
        first = self.base + index * self.rows + at
        return self.buf.at[pl.ds(pl.multiple_of(first, 16), size), :]

    def put(self, event, target, src, dst):
        copy = pltpu.make_async_remote_copy(
            src_ref=src, dst_ref=dst, send_sem=self.send, recv_sem=self.recv.at[event],
            device_id=target, device_id_type=MESH,
        )
        copy.start()

    def pass_on(self, event, target, index, half=None):
        piece = self.slot(index, half)
        self.put(event, target, piece, piece)

    def arrive(self, event, index, half=None):
        piece = self.slot(index, half)
        pltpu.make_async_remote_copy(
            src_ref=piece, dst_ref=piece, send_sem=self.send,
            recv_sem=self.recv.at[event], device_id=self.sib, device_id_type=MESH,
        ).wait_recv()

    def first(self):
        dst = self.slot(self.at.ctx)
        self.put(2, self.up, self.own, dst)
        self.put(3, self.down, self.own, dst)
        self.put(1, self.xn, self.own, dst)
        self.put(0, self.sib, self.own, dst)

    def second(self):
        at = self.at
        index = at.ctx_at(flip_col=True)
        self.arrive(1, index)
        self.pass_on(4, self.up, index, 2)
        self.pass_on(5, self.down, index, 2)
        self.pass_on(9, self.sib, index)
        index = at.ctx_at(dz=-1)
        self.arrive(2, index)
        self.pass_on(6, self.up, index, 0)
        self.pass_on(16, self.xn, index, 3)
        self.pass_on(10, self.sib, index)
        index = at.ctx_at(dz=1)
        self.arrive(3, index)
        self.pass_on(7, self.down, index, 1)
        self.pass_on(17, self.xn, index, 3)
        self.pass_on(11, self.sib, index)

    def third(self):
        at = self.at
        index = at.ctx_at(dz=2)
        self.arrive(6, index, 0)
        self.arrive(7, index, 1)
        self.pass_on(8, self.xn, index)
        self.pass_on(14, self.sib, index)
        for event, dz, on in ((4, -1, 12), (5, 1, 13)):
            index = at.ctx_at(flip_col=True, dz=dz)
            self.arrive(event, index, 2)
            self.arrive(event + 12, index, 3)
            self.pass_on(on, self.sib, index)

    def last(self):
        at = self.at
        index = at.ctx_at(flip_col=True, dz=2)
        self.arrive(8, index)
        self.pass_on(15, self.sib, index)

    def from_core(self, pieces):
        for event, flip_col, dz in pieces:
            self.arrive(event, self.at.ctx_at(flip_col=flip_col, dz=dz, flip_core=True))

    def near(self):
        self.from_core(((0, False, 0), (10, False, -1), (12, True, -1)))

    def rest(self):
        self.from_core(((9, True, 0), (11, False, 1), (13, True, 1), (14, False, 2), (15, True, 2)))

    def whole(self):
        self.near()
        self.rest()

    def close(self):
        sent = self.buf.at[pl.ds(self.base, 15 * self.rows), :]
        pltpu.make_async_remote_copy(
            src_ref=sent, dst_ref=sent, send_sem=self.send, recv_sem=self.recv.at[0],
            device_id=self.sib, device_id_type=MESH,
        ).wait_send()


class Features:
    def __init__(self, at, own, buf, send, recv):
        self.at, self.own, self.buf, self.send, self.recv = at, own, buf, send, recv
        self.partner = self.sib = {"head": at.head_at(flip=True)}
        self.up = {"head": at.head_at(dy=1)}
        self.down = {"head": at.head_at(dy=-1)}

    def slot(self, index, half=None):
        cols = pl.ds(pl.multiple_of(index * 512, 512), 512)
        if half is None:
            return self.buf.at[:, cols]
        return self.buf.at[pl.ds(half * (ROWS // 2), ROWS // 2), cols]

    put, pass_on = Gather.put, Gather.pass_on

    def arrive(self, event, index, half=None):
        piece = self.slot(index, half)
        pltpu.make_async_remote_copy(
            src_ref=piece, dst_ref=piece, send_sem=self.send,
            recv_sem=self.recv.at[event], device_id=self.partner, device_id_type=MESH,
        ).wait_recv()

    def first(self):
        dst = self.slot(self.at.head)
        self.put(0, self.partner, self.own, dst)
        self.put(1, self.up, self.own, dst)
        self.put(2, self.down, self.own, dst)

    def second(self):
        at = self.at
        index = at.head_at(flip=True)
        self.arrive(0, index)
        self.pass_on(3, self.up, index)
        self.pass_on(4, self.down, index)
        index = at.head_at(dy=-1)
        self.arrive(1, index)
        self.pass_on(5, self.up, index, 0)
        index = at.head_at(dy=1)
        self.arrive(2, index)
        self.pass_on(6, self.down, index, 1)

    def third(self):
        at = self.at
        index = at.head_at(flip=True, dy=-1)
        self.arrive(3, index)
        self.pass_on(7, self.up, index, 0)
        index = at.head_at(flip=True, dy=1)
        self.arrive(4, index)
        self.pass_on(8, self.down, index, 1)

    def whole(self):
        at = self.at
        for event, flip in ((5, False), (7, True)):
            index = at.head_at(flip=flip, dy=2)
            self.arrive(event, index, 0)
            self.arrive(event + 1, index, 1)

    def close(self):
        sent = self.buf.at[:, : 7 * 512]
        pltpu.make_async_remote_copy(
            src_ref=sent, dst_ref=sent, send_sem=self.send, recv_sem=self.recv.at[0],
            device_id=self.partner, device_id_type=MESH,
        ).wait_send()


def dot_nt(left, right):
    return lax.dot_general(
        left, right, (((1,), (1,)), ((), ())), preferred_element_type=jnp.float32
    )


def layer_kernel(
    x_ref, wk_ref, wv_ref, wq_ref, wo_ref, kern_ref, mix_ref, cos_ref, sin_ref, gain_ref, o_ref,
    x_buf, w_buf, wv_buf, k_buf, v_buf, wo_buf, made, qx, rim_in,
    q32, k32, qt, kc, lg, band, acc, mass, peaks, normed, part,
    y_half, y_sum, y_full, give, got,
    send, recv, x_send, x_recv, here, rim_sems, r_send, r_recv,
):
    at = Places()
    place = at.ctx
    r0 = place * ROWS
    blocks = lax.div(place + 2, 2)
    scale = 1.0 / math.sqrt(HD)
    after = {"ctx": lax.rem(at.ctx + 1, 16)}
    met = greet(
        [{"ctx": at.ctx_at(flip_core=True)}, {"ctx": at.ctx_at(flip_col=True)}]
        + [{"ctx": at.ctx_at(dz=1)}, {"ctx": at.ctx_at(dz=-1)}]
        + [{"head": at.head_at(dy=1)}, {"head": at.head_at(dy=-1)}, {"head": at.head_at(flip=True)}]
        + [after, {"ctx": lax.rem(at.ctx + 15, 16)}]
    )

    def gather(t, own, buf, rows, base=0):
        return Gather(at, own, buf, rows, send.at[t], recv.at[t], base)

    feats = Features(at, x_ref, x_buf, x_send.at[0], x_recv)
    wk = gather(0, wk_ref, w_buf, ROWS)
    wv = gather(1, wv_ref, wv_buf, ROWS)
    wq = gather(2, wq_ref, w_buf, ROWS, TOKENS)
    keys = gather(3, None, k_buf, ROWS, HD)
    values = gather(4, None, v_buf, ROWS)
    wo = gather(5, wo_ref, wo_buf, 2 * ROWS)
    keys.own = keys.slot(at.ctx)
    values.own = values.slot(at.ctx)

    own = [
        pltpu.make_async_copy(x_ref, feats.slot(at.head), here.at[0]),
        pltpu.make_async_copy(wk_ref, wk.slot(at.ctx), here.at[1]),
        pltpu.make_async_copy(wq_ref, wq.slot(at.ctx), here.at[3]),
        pltpu.make_async_copy(wv_ref, wv.slot(at.ctx), here.at[2]),
        pltpu.make_async_copy(wo_ref, wo.slot(at.ctx), here.at[4]),
    ]
    for copy in own:
        copy.start()
    k_buf[:HD] = jnp.zeros((HD, GROUP * HD), jnp.bfloat16)
    k_buf[HD + TOKENS :] = jnp.zeros((16, GROUP * HD), jnp.bfloat16)

    met()
    wk.first()
    feats.first()

    def project(buf):
        return jnp.dot(x_buf[...], buf[:TOKENS], preferred_element_type=jnp.float32)

    def rotate(projected):
        turned = []
        for h in range(GROUP):
            piece = projected[:, h * HD : (h + 1) * HD]
            turned.append(piece * cos_ref[...] + pltpu.roll(piece, HD // 2, 1) * sin_ref[...])
        return jnp.concatenate(turned, 1)

    def keep(index, value, dst):
        made[index] = value.astype(jnp.bfloat16)
        copy = pltpu.make_async_copy(made.at[index], dst, here.at[5 + index])
        copy.start()
        copy.wait()

    wk.second()
    wq.first()
    feats.second()
    wk.third()
    feats.third()
    wq.second()
    wv.first()
    wk.last()
    for copy in own:
        copy.wait()
    feats.whole()
    wk.whole()
    keep(0, rotate(project(w_buf.at[:TOKENS])), keys.slot(at.ctx))
    wq.third()
    keys.first()
    wv.second()
    wq.last()
    wq.whole()
    keep(2, rotate(project(w_buf.at[TOKENS:])), qx.at[pl.ds(16, ROWS)])
    rim = pltpu.make_async_remote_copy(
        src_ref=qx.at[pl.ds(ROWS, 16)], dst_ref=rim_in,
        send_sem=rim_sems.at[0], recv_sem=rim_sems.at[1], device_id=after, device_id_type=MESH,
    )
    rim.start()
    keys.second()
    wv.third()
    wo.first()
    rim.wait()
    qx[:16] = jnp.where(place > 0, rim_in[...], jnp.zeros_like(rim_in))
    for h in range(GROUP):
        q32[h] = qx[:, h * HD : (h + 1) * HD].astype(jnp.float32)[8:] * scale

    def mix_lags(r, _):
        for h in range(GROUP):
            view = q32.at[h, pl.ds(pl.multiple_of(r * 16, 16), 24)]
            lags = [view[8 - a : 24 - a] for a in range(CQ)]
            for c in range(CK):
                total = kern_ref[h, c] * lags[0]
                for a in range(1, CQ):
                    total = total + kern_ref[h, a * CK + c] * lags[a]
                qt[h, pl.ds(pl.multiple_of(r * 16, 16), 16), c * HD : (c + 1) * HD] = total.astype(
                    jnp.bfloat16
                )
        return 0

    keys.third()
    lax.fori_loop(0, ROWS // 16, mix_lags, 0)
    wv.last()
    keys.last()
    wv.whole()
    keep(1, project(wv_buf), values.slot(at.ctx))
    values.first()
    wo.second()
    keys.near()
    for s in range(2):
        for h in range(GROUP):
            cols = slice(h * HD, (h + 1) * HD)
            near = k_buf[pl.ds(pl.multiple_of(r0 + s * HD, HD), 2 * HD), cols]
            scores = dot_nt(qx[s * HD : s * HD + HD + 16, cols], near)[8:] * scale
            apart = (
                lax.broadcasted_iota(jnp.int32, scores.shape, 0)
                - lax.broadcasted_iota(jnp.int32, scores.shape, 1)
                + (HD - 8)
            )
            kept = jnp.where((apart >= 0) & (apart <= 24), scores, 0.0)
            band[s * GROUP + h, 0] = kept[:, :HD]
            band[s * GROUP + h, 1] = kept[:, HD:]

    def taps(h, lags, width):
        total = None
        for c in range(CK):
            piece = kern_ref[h, c] * lags[0]
            for a in range(1, CQ):
                piece = piece + kern_ref[h, a * CK + c] * lags[a]
            shift = (c - CK // 2) % width
            piece = pltpu.roll(piece, shift, 1) if shift else piece
            total = piece if total is None else total + piece
        return total

    def two_tiles(k, _):
        rows = pl.ds(pl.multiple_of(8 * k, 8), 8)
        for s in range(2):
            for h in range(GROUP):
                views = [
                    band.at[s * GROUP + h, t, pl.ds(pl.multiple_of(8 * k, 8), 16)] for t in range(2)
                ]
                lags = [
                    jnp.concatenate([view[8 - a : 16 - a] for view in views], 1) for a in range(CQ)
                ]
                direct = taps(h, lags, 2 * HD)
                band[s * GROUP + h, 0, rows] = direct[:, :HD]
                band[s * GROUP + h, 1, rows] = direct[:, HD:]
        return 0

    def one_tile(k, _):
        rows = pl.ds(pl.multiple_of(8 * k, 8), 8)
        for s in range(2):
            for h in range(GROUP):
                view = band.at[s * GROUP + h, 1, pl.ds(pl.multiple_of(8 * k, 8), 16)]
                band[s * GROUP + h, 1, rows] = taps(h, [view[8 - a : 16 - a] for a in range(CQ)], HD)
        return 0

    lax.fori_loop(0, 2, two_tiles, 0)
    lax.fori_loop(2, HD // 8, one_tile, 0)
    keys.rest()

    steps = {2: [values.second], 5: [wo.third]}

    def block_logits(b, _):
        for when, actions in steps.items():

            @pl.when(b == when)
            def _(actions=actions):
                for action in actions:
                    action()

        @pl.when(b < blocks)
        def _():
            for h in range(GROUP):
                rows = k_buf[pl.ds(pl.multiple_of(HD - 16 + b * KB, 16), KB + 32), h * HD : (h + 1) * HD]
                k32[h] = rows.astype(jnp.float32)
                for c in range(CK):
                    start = 16 + CK // 2 - c
                    kc[h % 2, :, c * HD : (c + 1) * HD] = k32[h, start : start + KB].astype(jnp.bfloat16)
                logits = dot_nt(qt[h], kc[h % 2])
                lg[h, :, pl.ds(pl.multiple_of(HD + b * KB, HD), KB)] = logits
                peak = logits[:, :HD]
                for t in range(1, KB // HD):
                    peak = jnp.maximum(peak, logits[:, t * HD : (t + 1) * HD])
                peaks[h] = jnp.maximum(peaks[h], jnp.where(b < blocks - 2, peak, -jnp.inf))

        return 0

    peaks[...] = jnp.full_like(peaks, -jnp.inf)
    lax.fori_loop(0, 8, block_logits, 0)
    values.third()

    apart = lax.broadcasted_iota(jnp.int32, (HD, HD), 0) - lax.broadcasted_iota(jnp.int32, (HD, HD), 1)
    for s in range(2):
        here_cols = pl.ds(pl.multiple_of(HD + r0 + s * HD, HD), HD)
        prior = pl.ds(pl.multiple_of(r0 + s * HD, HD), HD)
        for h in range(GROUP):
            rows = slice(s * HD, (s + 1) * HD)
            lg[h, rows, here_cols] = jnp.where(
                apart >= BAND,
                lg[h, rows, here_cols],
                jnp.where(apart >= 0, band[s * GROUP + h, 1, :HD], -jnp.inf),
            )
            rows = slice(s * HD, s * HD + 16)
            lg[h, rows, prior] = jnp.where(
                apart[:16] + HD >= BAND, lg[h, rows, prior], band[s * GROUP + h, 0, :16]
            )

    for h in range(GROUP):
        lg[h, :HD, pl.ds(pl.multiple_of(2 * HD + r0, HD), HD)] = jnp.full(
            (HD, HD), -jnp.inf, jnp.float32
        )

    @pl.when(lax.rem(place, 2) == 0)
    def _():
        for h in range(GROUP):
            lg[h, :, pl.ds(pl.multiple_of(3 * HD + r0, HD), ROWS)] = jnp.full(
                (ROWS, ROWS), -jnp.inf, jnp.float32
            )

    values.last()
    for g in range(GROUP):

        def peak_of(b, peak, g=g):
            block = lg[g, :, pl.ds(pl.multiple_of(HD + b * KB, HD), KB)]
            for t in range(KB // HD):
                peak = jnp.maximum(peak, block[:, t * HD : (t + 1) * HD])
            return peak

        peak = lax.fori_loop(jnp.maximum(blocks - 2, 0), blocks, peak_of, peaks[g])
        peaks[g] = jnp.broadcast_to(jnp.max(peak, axis=1, keepdims=True), (ROWS, HD))

    wk.close()
    wq.close()
    mass[...] = jnp.zeros_like(mass)

    def raise_block(b, _):
        for g in range(GROUP):
            for r in range(2):
                rows = slice(r * HALF, (r + 1) * HALF)
                peak = peaks[g, rows]
                total = mass[g, rows]
                first = b * GROUP * ROWS + (r * GROUP + g) * HALF
                for t in range(KB // HD):
                    block = lg[g, rows, pl.ds(pl.multiple_of(HD + b * KB + t * HD, HD), HD)]
                    probs = jnp.exp(block - peak)
                    total = total + probs
                    w_buf[pl.ds(pl.multiple_of(first, HALF), HALF), t * HD : (t + 1) * HD] = probs.astype(
                        jnp.bfloat16
                    )
                mass[g, rows] = total
        return 0

    lax.fori_loop(0, blocks, raise_block, 0)
    wo.last()
    values.whole()

    up = {"head": at.head_at(dy=1)}
    down = {"head": at.head_at(dy=-1)}
    partner = {"head": at.head_at(flip=True)}
    chunk = ROWS // 4
    quarter = chunk // 2
    y_up, y_down, y_far = (lax.rem(at.y + d, 4) for d in (1, 3, 2))

    def ring_copy(r, event):
        target, src, dst = (
            (up, part.at[y_far, :, pl.ds(r * chunk, quarter)], y_half.at[r, 0]),
            (down, part.at[y_far, :, pl.ds(r * chunk + quarter, quarter)], y_half.at[r, 1]),
            (up, y_sum.at[r, 0], y_full.at[r, 0]),
            (down, y_sum.at[r, 1], y_full.at[r, 1]),
            (partner, give.at[r], got.at[r]),
        )[event]
        return pltpu.make_async_remote_copy(
            src_ref=src, dst_ref=dst, send_sem=r_send.at[r, event], recv_sem=r_recv.at[r, event],
            device_id=target, device_id_type=MESH,
        )

    def add(left, right):
        return (left.astype(jnp.float32) + right.astype(jnp.float32)).astype(jnp.bfloat16)

    def ring_first(r):
        ring_copy(r, 0).start()
        ring_copy(r, 1).start()

    def ring_second(r):
        y_sum[r, 0, :, quarter:] = part[y_up, :, r * chunk + quarter : (r + 1) * chunk]
        y_sum[r, 1, :, :quarter] = part[y_down, :, r * chunk : r * chunk + quarter]
        ring_copy(r, 0).wait_recv()
        y_sum[r, 0, :, :quarter] = add(part[y_up, :, r * chunk : r * chunk + quarter], y_half[r, 0])
        ring_copy(r, 2).start()
        ring_copy(r, 1).wait_recv()
        y_sum[r, 1, :, quarter:] = add(part[y_down, :, r * chunk + quarter : (r + 1) * chunk], y_half[r, 1])
        ring_copy(r, 3).start()

    def ring_total(r, far):
        return (
            part[at.y, far, r * chunk : (r + 1) * chunk].astype(jnp.float32)
            + y_full[r, 0, far].astype(jnp.float32)
            + y_full[r, 1, far].astype(jnp.float32)
        )

    def ring_third(r):
        ring_copy(r, 2).wait_recv()
        ring_copy(r, 3).wait_recv()
        give[r] = ring_total(r, 1 - at.far).astype(jnp.bfloat16)
        ring_copy(r, 4).start()

    def ring_last(r):
        mine = ring_total(r, at.far)
        ring_copy(r, 4).wait_recv()
        total = mine + got[r].astype(jnp.float32)
        o_ref[r * chunk : (r + 1) * chunk] = total.astype(jnp.bfloat16)

    for r in range(2):
        rows = slice(r * HALF, (r + 1) * HALF)
        acc[...] = jnp.zeros_like(acc)

        def weigh(b, _, r=r):
            first = b * GROUP * ROWS + r * GROUP * HALF
            left = w_buf[pl.ds(pl.multiple_of(first, HALF), GROUP * HALF)]
            block = v_buf[pl.ds(pl.multiple_of(b * KB, KB), KB), :]
            acc[...] += jnp.dot(left, block, preferred_element_type=jnp.float32)
            return 0

        lax.fori_loop(0, blocks, weigh, 0)
        inverse = [
            jnp.broadcast_to(1.0 / jnp.sum(mass[g, rows], axis=1, keepdims=True), (HALF, HD))
            for g in range(GROUP)
        ]
        for h in range(GROUP):
            cols = slice(h * HD, (h + 1) * HD)
            total = mix_ref[h, 0] * (acc[:HALF, cols] * inverse[0])
            for g in range(1, GROUP):
                total = total + mix_ref[h, g] * (acc[g * HALF : (g + 1) * HALF, cols] * inverse[g])
            rms = jnp.sqrt(jnp.mean(total * total, axis=1, keepdims=True) + 1e-05)
            normed[rows, cols] = (total / rms * gain_ref[:, cols]).astype(jnp.bfloat16)

    wo.whole()

    def project_out(step):
        y = lax.rem(at.y + step, 4)
        for far in range(2):
            for side in range(2):
                first = (far * 8 + y * 2 + side) * GROUP * HD
                source = pl.ds(pl.multiple_of(first, GROUP * HD), GROUP * HD)
                piece = jnp.dot(normed[...], wo_buf[source], preferred_element_type=jnp.float32)
                part[y, far, :, side * ROWS : (side + 1) * ROWS] = piece.astype(jnp.bfloat16)

    project_out(2)
    for r in range(4):
        ring_first(r)
    project_out(1)
    project_out(3)
    for r in range(4):
        ring_second(r)
    project_out(0)
    ring_third(0)
    ring_third(1)
    ring_third(2)
    ring_last(0)
    ring_third(3)
    ring_last(1)
    ring_last(2)
    ring_last(3)
    for r in range(4):
        for event in range(5):
            ring_copy(r, event).wait_send()
    for each in (feats, wv, keys, values, wo):
        each.close()


def layer(*operands):
    smem = pl.BlockSpec(memory_space=pltpu.SMEM)
    vmem = pl.BlockSpec(memory_space=pltpu.VMEM)
    hbm = pl.BlockSpec(memory_space=pltpu.HBM)
    width = GROUP * HD
    half = lambda *dims: pltpu.VMEM(dims, jnp.bfloat16)
    full = lambda *dims: pltpu.VMEM(dims, jnp.float32)
    dma = pltpu.SemaphoreType.DMA
    return pl.pallas_call(
        layer_kernel,
        out_shape=jax.ShapeDtypeStruct((ROWS, width), jnp.bfloat16),
        in_specs=[hbm] * 5 + [smem] * 2 + [vmem] * 3,
        out_specs=vmem,
        scratch_shapes=[
            half(ROWS, TOKENS), half(2 * TOKENS, width), half(TOKENS, width),
            half(HD + TOKENS + 16, width), half(TOKENS, width), half(16 * width, ROWS),
            half(3, ROWS, width), half(ROWS + 16, width), half(16, width),
            full(GROUP, ROWS + 8, HD), full(GROUP, KB + 32, HD),
            half(GROUP, ROWS, CK * HD), half(2, KB, CK * HD),
            full(GROUP, ROWS, HD + TOKENS), full(2 * GROUP, 2, HD + 8, HD),
            full(GROUP * HALF, width),
            full(GROUP, ROWS, HD), full(GROUP, ROWS, HD), half(ROWS, width),
            half(4, 2, ROWS, width),
            half(4, 2, 2, ROWS // 8, width), half(4, 2, 2, ROWS // 4, width), half(4, 2, 2, ROWS // 4, width),
            half(4, ROWS // 4, width), half(4, ROWS // 4, width),
            dma((6,)), dma((6, 18)), dma((1,)), dma((9,)), dma((8,)), dma((2,)), dma((4, 5)), dma((4, 5)),
        ],
        compiler_params=pltpu.CompilerParams(
            collective_id=1, has_side_effects=True, vmem_limit_bytes=67043328
        ),
        name="layer",
    )(*operands)


def per_device(
    activations, positions, w_query, w_key, w_value, conv_kernel, head_mix, out_gain, w_out
):
    exponents = jnp.arange(HD // 2, dtype=jnp.float32) * (2.0 / HD)
    inverse = jnp.exp(-exponents * math.log(500000.0))
    angle = (positions.astype(jnp.float32) * 0.25)[:, None] * inverse[None, :]
    cosine = jnp.cos(angle)
    sine = jnp.sin(angle)
    return layer(
        activations, w_key, w_value, w_query, w_out, conv_kernel, head_mix,
        jnp.concatenate([cosine, cosine], 1), jnp.concatenate([-sine, sine], 1),
        out_gain.reshape(1, -1),
    )


def solution(mesh):
    return jax.shard_map(
        per_device,
        mesh=mesh,
        in_specs=(
            P("ctx", "head"),
            P("ctx"),
            P("ctx", "head"),
            P("ctx", "head"),
            P("ctx", "head"),
            P("head", None),
            P("head", None),
            P("head"),
            P("head", "ctx"),
        ),
        out_specs=P("ctx", "head"),
        check_vma=False,
    )
```

```python
import math

import jax
import jax.numpy as jnp
from jax import lax
from jax.experimental import pallas as pl
from jax.experimental.pallas import tpu as pltpu
from jax.sharding import PartitionSpec as P

HD = 128
GROUP = 4
CQ = 6
CK = 11
KB = 512
ROWS = 256
TOKENS = 4096
HALF = 128
BAND = 10


MESH = pl.DeviceIdType.MESH


class Places:
    def __init__(self):
        self.ctx = lax.axis_index("ctx")
        self.head = lax.axis_index("head")
        self.col = lax.div(self.ctx, 8)
        self.z = lax.rem(lax.div(self.ctx, 2), 4)
        self.core = lax.rem(self.ctx, 2)
        self.y = lax.rem(self.head, 4)
        self.far = lax.div(self.head, 4)

    def ctx_at(self, flip_col=False, dz=0, flip_core=False):
        col = 1 - self.col if flip_col else self.col
        core = 1 - self.core if flip_core else self.core
        return col * 8 + lax.rem(self.z + dz + 4, 4) * 2 + core

    def head_at(self, flip=False, dy=0):
        far = 1 - self.far if flip else self.far
        return far * 4 + lax.rem(self.y + dy + 4, 4)


def greet(targets):
    barrier = pltpu.get_barrier_semaphore()
    for target in targets:
        pl.semaphore_signal(barrier, inc=1, device_id=target, device_id_type=MESH)
    return lambda: pl.semaphore_wait(barrier, len(targets))


class Gather:
    def __init__(self, at, own, buf, rows, send, recv, base=0):
        self.at, self.own, self.buf, self.rows, self.send, self.recv = at, own, buf, rows, send, recv
        self.base = base
        self.sib = {"ctx": at.ctx_at(flip_core=True)}
        self.xn = {"ctx": at.ctx_at(flip_col=True)}
        self.up = {"ctx": at.ctx_at(dz=1)}
        self.down = {"ctx": at.ctx_at(dz=-1)}

    def slot(self, index, half=None):
        short = self.rows * 3 // 16
        at, size = {
            None: (0, self.rows), 0: (0, self.rows // 2), 1: (self.rows // 2, self.rows // 2),
            2: (0, self.rows - short), 3: (self.rows - short, short),
        }[half]
        first = self.base + index * self.rows + at
        return self.buf.at[pl.ds(pl.multiple_of(first, 16), size), :]

    def put(self, event, target, src, dst):
        copy = pltpu.make_async_remote_copy(
            src_ref=src, dst_ref=dst, send_sem=self.send, recv_sem=self.recv.at[event],
            device_id=target, device_id_type=MESH,
        )
        copy.start()

    def pass_on(self, event, target, index, half=None):
        piece = self.slot(index, half)
        self.put(event, target, piece, piece)

    def arrive(self, event, index, half=None):
        piece = self.slot(index, half)
        pltpu.make_async_remote_copy(
            src_ref=piece, dst_ref=piece, send_sem=self.send,
            recv_sem=self.recv.at[event], device_id=self.sib, device_id_type=MESH,
        ).wait_recv()

    def first(self):
        dst = self.slot(self.at.ctx)
        self.put(2, self.up, self.own, dst)
        self.put(3, self.down, self.own, dst)
        self.put(1, self.xn, self.own, dst)
        self.put(0, self.sib, self.own, dst)

    def second(self):
        at = self.at
        index = at.ctx_at(flip_col=True)
        self.arrive(1, index)
        self.pass_on(4, self.up, index, 2)
        self.pass_on(5, self.down, index, 2)
        self.pass_on(9, self.sib, index)
        index = at.ctx_at(dz=-1)
        self.arrive(2, index)
        self.pass_on(6, self.up, index, 0)
        self.pass_on(16, self.xn, index, 3)
        self.pass_on(10, self.sib, index)
        index = at.ctx_at(dz=1)
        self.arrive(3, index)
        self.pass_on(7, self.down, index, 1)
        self.pass_on(17, self.xn, index, 3)
        self.pass_on(11, self.sib, index)

    def third(self):
        at = self.at
        index = at.ctx_at(dz=2)
        self.arrive(6, index, 0)
        self.arrive(7, index, 1)
        self.pass_on(8, self.xn, index)
        self.pass_on(14, self.sib, index)
        for event, dz, on in ((4, -1, 12), (5, 1, 13)):
            index = at.ctx_at(flip_col=True, dz=dz)
            self.arrive(event, index, 2)
            self.arrive(event + 12, index, 3)
            self.pass_on(on, self.sib, index)

    def last(self):
        at = self.at
        index = at.ctx_at(flip_col=True, dz=2)
        self.arrive(8, index)
        self.pass_on(15, self.sib, index)

    def from_core(self, pieces):
        for event, flip_col, dz in pieces:
            self.arrive(event, self.at.ctx_at(flip_col=flip_col, dz=dz, flip_core=True))

    def near(self):
        self.from_core(((0, False, 0), (10, False, -1), (12, True, -1)))

    def rest(self):
        self.from_core(((9, True, 0), (11, False, 1), (13, True, 1), (14, False, 2), (15, True, 2)))

    def whole(self):
        self.near()
        self.rest()

    def close(self):
        sent = self.buf.at[pl.ds(self.base, 15 * self.rows), :]
        pltpu.make_async_remote_copy(
            src_ref=sent, dst_ref=sent, send_sem=self.send, recv_sem=self.recv.at[0],
            device_id=self.sib, device_id_type=MESH,
        ).wait_send()


class Features:
    def __init__(self, at, own, buf, send, recv):
        self.at, self.own, self.buf, self.send, self.recv = at, own, buf, send, recv
        self.partner = self.sib = {"head": at.head_at(flip=True)}
        self.up = {"head": at.head_at(dy=1)}
        self.down = {"head": at.head_at(dy=-1)}

    def slot(self, index, half=None):
        cols = pl.ds(pl.multiple_of(index * 512, 512), 512)
        if half is None:
            return self.buf.at[:, cols]
        return self.buf.at[pl.ds(half * (ROWS // 2), ROWS // 2), cols]

    put, pass_on = Gather.put, Gather.pass_on

    def arrive(self, event, index, half=None):
        piece = self.slot(index, half)
        pltpu.make_async_remote_copy(
            src_ref=piece, dst_ref=piece, send_sem=self.send,
            recv_sem=self.recv.at[event], device_id=self.partner, device_id_type=MESH,
        ).wait_recv()

    def first(self):
        dst = self.slot(self.at.head)
        self.put(0, self.partner, self.own, dst)
        self.put(1, self.up, self.own, dst)
        self.put(2, self.down, self.own, dst)

    def second(self):
        at = self.at
        index = at.head_at(flip=True)
        self.arrive(0, index)
        self.pass_on(3, self.up, index)
        self.pass_on(4, self.down, index)
        index = at.head_at(dy=-1)
        self.arrive(1, index)
        self.pass_on(5, self.up, index, 0)
        index = at.head_at(dy=1)
        self.arrive(2, index)
        self.pass_on(6, self.down, index, 1)

    def third(self):
        at = self.at
        index = at.head_at(flip=True, dy=-1)
        self.arrive(3, index)
        self.pass_on(7, self.up, index, 0)
        index = at.head_at(flip=True, dy=1)
        self.arrive(4, index)
        self.pass_on(8, self.down, index, 1)

    def whole(self):
        at = self.at
        for event, flip in ((5, False), (7, True)):
            index = at.head_at(flip=flip, dy=2)
            self.arrive(event, index, 0)
            self.arrive(event + 1, index, 1)

    def close(self):
        sent = self.buf.at[:, : 7 * 512]
        pltpu.make_async_remote_copy(
            src_ref=sent, dst_ref=sent, send_sem=self.send, recv_sem=self.recv.at[0],
            device_id=self.partner, device_id_type=MESH,
        ).wait_send()


def dot_nt(left, right):
    return lax.dot_general(
        left, right, (((1,), (1,)), ((), ())), preferred_element_type=jnp.float32
    )


def layer_kernel(
    x_ref, wk_ref, wv_ref, wq_ref, wo_ref, kern_ref, mix_ref, pos_ref, gain_ref, o_ref,
    cos_ref, sin_ref, x_buf, w_buf, wv_buf, k_buf, v_buf, wo_buf, made, qx, rim_in,
    q32, k32, qt, kc, lg, band, acc, mass, peaks, normed, part,
    y_half, y_sum, y_full, give, got,
    send, recv, x_send, x_recv, here, rim_sems, r_send, r_recv,
):
    at = Places()
    place = at.ctx
    r0 = place * ROWS
    blocks = lax.div(place + 2, 2)
    scale = 1.0 / math.sqrt(HD)
    after = {"ctx": lax.rem(at.ctx + 1, 16)}
    met = greet(
        [{"ctx": at.ctx_at(flip_core=True)}, {"ctx": at.ctx_at(flip_col=True)}]
        + [{"ctx": at.ctx_at(dz=1)}, {"ctx": at.ctx_at(dz=-1)}]
        + [{"head": at.head_at(dy=1)}, {"head": at.head_at(dy=-1)}, {"head": at.head_at(flip=True)}]
        + [after, {"ctx": lax.rem(at.ctx + 15, 16)}]
    )

    def gather(t, own, buf, rows, base=0):
        return Gather(at, own, buf, rows, send.at[t], recv.at[t], base)

    feats = Features(at, x_ref, x_buf, x_send.at[0], x_recv)
    wk = gather(0, wk_ref, w_buf, ROWS)
    wv = gather(1, wv_ref, wv_buf, ROWS)
    wq = gather(2, wq_ref, w_buf, ROWS, TOKENS)
    keys = gather(3, None, k_buf, ROWS, HD)
    values = gather(4, None, v_buf, ROWS)
    wo = gather(5, wo_ref, wo_buf, 2 * ROWS)
    keys.own = keys.slot(at.ctx)
    values.own = values.slot(at.ctx)

    own = [
        pltpu.make_async_copy(x_ref, feats.slot(at.head), here.at[0]),
        pltpu.make_async_copy(wk_ref, wk.slot(at.ctx), here.at[1]),
        pltpu.make_async_copy(wq_ref, wq.slot(at.ctx), here.at[3]),
        pltpu.make_async_copy(wv_ref, wv.slot(at.ctx), here.at[2]),
        pltpu.make_async_copy(wo_ref, wo.slot(at.ctx), here.at[4]),
    ]
    for copy in own:
        copy.start()
    k_buf[:HD] = jnp.zeros((HD, GROUP * HD), jnp.bfloat16)
    k_buf[HD + TOKENS :] = jnp.zeros((16, GROUP * HD), jnp.bfloat16)

    met()
    wk.first()
    feats.first()

    lane = lax.broadcasted_iota(jnp.int32, (HD, HD), 1)
    lower = lane < HD // 2
    exponents = jnp.where(lower, lane, lane - HD // 2).astype(jnp.float32) * (2.0 / HD)
    inverse_rate = jnp.exp(-exponents * math.log(500000.0))
    for t in range(ROWS // HD):
        along = jnp.broadcast_to(pos_ref[t : t + 1].astype(jnp.float32) * 0.25, (HD, HD))
        angle = jnp.transpose(along) * inverse_rate
        sine = jnp.sin(angle)
        cos_ref[t * HD : (t + 1) * HD] = jnp.cos(angle)
        sin_ref[t * HD : (t + 1) * HD] = jnp.where(lower, -sine, sine)

    def project(buf):
        return jnp.dot(x_buf[...], buf[:TOKENS], preferred_element_type=jnp.float32)

    def rotate(projected):
        turned = []
        for h in range(GROUP):
            piece = projected[:, h * HD : (h + 1) * HD]
            turned.append(piece * cos_ref[...] + pltpu.roll(piece, HD // 2, 1) * sin_ref[...])
        return jnp.concatenate(turned, 1)

    def keep(index, value, dst):
        made[index] = value.astype(jnp.bfloat16)
        copy = pltpu.make_async_copy(made.at[index], dst, here.at[5 + index])
        copy.start()
        copy.wait()

    wk.second()
    wq.first()
    feats.second()
    wk.third()
    feats.third()
    wq.second()
    wv.first()
    wk.last()
    for copy in own:
        copy.wait()
    feats.whole()
    wk.whole()
    keep(0, rotate(project(w_buf.at[:TOKENS])), keys.slot(at.ctx))
    wq.third()
    keys.first()
    wv.second()
    wq.last()
    wq.whole()
    keep(2, rotate(project(w_buf.at[TOKENS:])), qx.at[pl.ds(16, ROWS)])
    rim = pltpu.make_async_remote_copy(
        src_ref=qx.at[pl.ds(ROWS, 16)], dst_ref=rim_in,
        send_sem=rim_sems.at[0], recv_sem=rim_sems.at[1], device_id=after, device_id_type=MESH,
    )
    rim.start()
    keys.second()
    wv.third()
    wo.first()
    rim.wait()
    qx[:16] = jnp.where(place > 0, rim_in[...], jnp.zeros_like(rim_in))
    for h in range(GROUP):
        q32[h] = qx[:, h * HD : (h + 1) * HD].astype(jnp.float32)[8:] * scale

    def mix_lags(r, _):
        for h in range(GROUP):
            view = q32.at[h, pl.ds(pl.multiple_of(r * 16, 16), 24)]
            lags = [view[8 - a : 24 - a] for a in range(CQ)]
            for c in range(CK):
                total = kern_ref[h, c] * lags[0]
                for a in range(1, CQ):
                    total = total + kern_ref[h, a * CK + c] * lags[a]
                qt[h, pl.ds(pl.multiple_of(r * 16, 16), 16), c * HD : (c + 1) * HD] = total.astype(
                    jnp.bfloat16
                )
        return 0

    keys.third()
    lax.fori_loop(0, ROWS // 16, mix_lags, 0)
    wv.last()
    keys.last()
    wv.whole()
    keep(1, project(wv_buf), values.slot(at.ctx))
    values.first()
    wo.second()
    keys.near()
    for s in range(2):
        for h in range(GROUP):
            cols = slice(h * HD, (h + 1) * HD)
            near = k_buf[pl.ds(pl.multiple_of(r0 + s * HD, HD), 2 * HD), cols]
            scores = dot_nt(qx[s * HD : s * HD + HD + 16, cols], near)[8:] * scale
            apart = (
                lax.broadcasted_iota(jnp.int32, scores.shape, 0)
                - lax.broadcasted_iota(jnp.int32, scores.shape, 1)
                + (HD - 8)
            )
            kept = jnp.where((apart >= 0) & (apart <= 24), scores, 0.0)
            band[s * GROUP + h, 0] = kept[:, :HD]
            band[s * GROUP + h, 1] = kept[:, HD:]

    def taps(h, lags, width):
        total = None
        for c in range(CK):
            piece = kern_ref[h, c] * lags[0]
            for a in range(1, CQ):
                piece = piece + kern_ref[h, a * CK + c] * lags[a]
            shift = (c - CK // 2) % width
            piece = pltpu.roll(piece, shift, 1) if shift else piece
            total = piece if total is None else total + piece
        return total

    def two_tiles(k, _):
        rows = pl.ds(pl.multiple_of(8 * k, 8), 8)
        for s in range(2):
            for h in range(GROUP):
                views = [
                    band.at[s * GROUP + h, t, pl.ds(pl.multiple_of(8 * k, 8), 16)] for t in range(2)
                ]
                lags = [
                    jnp.concatenate([view[8 - a : 16 - a] for view in views], 1) for a in range(CQ)
                ]
                direct = taps(h, lags, 2 * HD)
                band[s * GROUP + h, 0, rows] = direct[:, :HD]
                band[s * GROUP + h, 1, rows] = direct[:, HD:]
        return 0

    def one_tile(k, _):
        rows = pl.ds(pl.multiple_of(8 * k, 8), 8)
        for s in range(2):
            for h in range(GROUP):
                view = band.at[s * GROUP + h, 1, pl.ds(pl.multiple_of(8 * k, 8), 16)]
                band[s * GROUP + h, 1, rows] = taps(h, [view[8 - a : 16 - a] for a in range(CQ)], HD)
        return 0

    lax.fori_loop(0, 2, two_tiles, 0)
    lax.fori_loop(2, HD // 8, one_tile, 0)
    keys.rest()

    steps = {2: [values.second], 5: [wo.third]}

    def block_logits(b, _):
        for when, actions in steps.items():

            @pl.when(b == when)
            def _(actions=actions):
                for action in actions:
                    action()

        @pl.when(b < blocks)
        def _():
            for h in range(GROUP):
                rows = k_buf[pl.ds(pl.multiple_of(HD - 16 + b * KB, 16), KB + 32), h * HD : (h + 1) * HD]
                k32[h] = rows.astype(jnp.float32)
                for c in range(CK):
                    start = 16 + CK // 2 - c
                    kc[h % 2, :, c * HD : (c + 1) * HD] = k32[h, start : start + KB].astype(jnp.bfloat16)
                logits = dot_nt(qt[h], kc[h % 2])
                lg[h, :, pl.ds(pl.multiple_of(HD + b * KB, HD), KB)] = logits
                peak = logits[:, :HD]
                for t in range(1, KB // HD):
                    peak = jnp.maximum(peak, logits[:, t * HD : (t + 1) * HD])
                peaks[h] = jnp.maximum(peaks[h], jnp.where(b < blocks - 2, peak, -jnp.inf))

        return 0

    peaks[...] = jnp.full_like(peaks, -jnp.inf)
    lax.fori_loop(0, 8, block_logits, 0)
    values.third()

    apart = lax.broadcasted_iota(jnp.int32, (HD, HD), 0) - lax.broadcasted_iota(jnp.int32, (HD, HD), 1)
    for s in range(2):
        here_cols = pl.ds(pl.multiple_of(HD + r0 + s * HD, HD), HD)
        prior = pl.ds(pl.multiple_of(r0 + s * HD, HD), HD)
        for h in range(GROUP):
            rows = slice(s * HD, (s + 1) * HD)
            lg[h, rows, here_cols] = jnp.where(
                apart >= BAND,
                lg[h, rows, here_cols],
                jnp.where(apart >= 0, band[s * GROUP + h, 1, :HD], -jnp.inf),
            )
            rows = slice(s * HD, s * HD + 16)
            lg[h, rows, prior] = jnp.where(
                apart[:16] + HD >= BAND, lg[h, rows, prior], band[s * GROUP + h, 0, :16]
            )

    for h in range(GROUP):
        lg[h, :HD, pl.ds(pl.multiple_of(2 * HD + r0, HD), HD)] = jnp.full(
            (HD, HD), -jnp.inf, jnp.float32
        )

    @pl.when(lax.rem(place, 2) == 0)
    def _():
        for h in range(GROUP):
            lg[h, :, pl.ds(pl.multiple_of(3 * HD + r0, HD), ROWS)] = jnp.full(
                (ROWS, ROWS), -jnp.inf, jnp.float32
            )

    values.last()
    for g in range(GROUP):

        def peak_of(b, peak, g=g):
            block = lg[g, :, pl.ds(pl.multiple_of(HD + b * KB, HD), KB)]
            for t in range(KB // HD):
                peak = jnp.maximum(peak, block[:, t * HD : (t + 1) * HD])
            return peak

        peak = lax.fori_loop(jnp.maximum(blocks - 2, 0), blocks, peak_of, peaks[g])
        peaks[g] = jnp.broadcast_to(jnp.max(peak, axis=1, keepdims=True), (ROWS, HD))

    wk.close()
    wq.close()
    mass[...] = jnp.zeros_like(mass)

    def raise_block(b, _):
        for g in range(GROUP):
            for r in range(2):
                rows = slice(r * HALF, (r + 1) * HALF)
                peak = peaks[g, rows]
                total = mass[g, rows]
                first = b * GROUP * ROWS + (r * GROUP + g) * HALF
                for t in range(KB // HD):
                    block = lg[g, rows, pl.ds(pl.multiple_of(HD + b * KB + t * HD, HD), HD)]
                    probs = jnp.exp(block - peak)
                    total = total + probs
                    w_buf[pl.ds(pl.multiple_of(first, HALF), HALF), t * HD : (t + 1) * HD] = probs.astype(
                        jnp.bfloat16
                    )
                mass[g, rows] = total
        return 0

    lax.fori_loop(0, blocks, raise_block, 0)
    wo.last()
    values.whole()

    up = {"head": at.head_at(dy=1)}
    down = {"head": at.head_at(dy=-1)}
    partner = {"head": at.head_at(flip=True)}
    chunk = ROWS // 4
    quarter = chunk // 2
    y_up, y_down, y_far = (lax.rem(at.y + d, 4) for d in (1, 3, 2))

    def ring_copy(r, event):
        target, src, dst = (
            (up, part.at[y_far, :, pl.ds(r * chunk, quarter)], y_half.at[r, 0]),
            (down, part.at[y_far, :, pl.ds(r * chunk + quarter, quarter)], y_half.at[r, 1]),
            (up, y_sum.at[r, 0], y_full.at[r, 0]),
            (down, y_sum.at[r, 1], y_full.at[r, 1]),
            (partner, give.at[r], got.at[r]),
        )[event]
        return pltpu.make_async_remote_copy(
            src_ref=src, dst_ref=dst, send_sem=r_send.at[r, event], recv_sem=r_recv.at[r, event],
            device_id=target, device_id_type=MESH,
        )

    def add(left, right):
        return (left.astype(jnp.float32) + right.astype(jnp.float32)).astype(jnp.bfloat16)

    def ring_first(r):
        ring_copy(r, 0).start()
        ring_copy(r, 1).start()

    def ring_second(r):
        y_sum[r, 0, :, quarter:] = part[y_up, :, r * chunk + quarter : (r + 1) * chunk]
        y_sum[r, 1, :, :quarter] = part[y_down, :, r * chunk : r * chunk + quarter]
        ring_copy(r, 0).wait_recv()
        y_sum[r, 0, :, :quarter] = add(part[y_up, :, r * chunk : r * chunk + quarter], y_half[r, 0])
        ring_copy(r, 2).start()
        ring_copy(r, 1).wait_recv()
        y_sum[r, 1, :, quarter:] = add(part[y_down, :, r * chunk + quarter : (r + 1) * chunk], y_half[r, 1])
        ring_copy(r, 3).start()

    def ring_total(r, far):
        return (
            part[at.y, far, r * chunk : (r + 1) * chunk].astype(jnp.float32)
            + y_full[r, 0, far].astype(jnp.float32)
            + y_full[r, 1, far].astype(jnp.float32)
        )

    def ring_third(r):
        ring_copy(r, 2).wait_recv()
        ring_copy(r, 3).wait_recv()
        give[r] = ring_total(r, 1 - at.far).astype(jnp.bfloat16)
        ring_copy(r, 4).start()

    def ring_last(r):
        mine = ring_total(r, at.far)
        ring_copy(r, 4).wait_recv()
        total = mine + got[r].astype(jnp.float32)
        o_ref[r * chunk : (r + 1) * chunk] = total.astype(jnp.bfloat16)

    for r in range(2):
        rows = slice(r * HALF, (r + 1) * HALF)
        acc[...] = jnp.zeros_like(acc)

        def weigh(b, _, r=r):
            first = b * GROUP * ROWS + r * GROUP * HALF
            left = w_buf[pl.ds(pl.multiple_of(first, HALF), GROUP * HALF)]
            block = v_buf[pl.ds(pl.multiple_of(b * KB, KB), KB), :]
            acc[...] += jnp.dot(left, block, preferred_element_type=jnp.float32)
            return 0

        lax.fori_loop(0, blocks, weigh, 0)
        inverse = [
            jnp.broadcast_to(1.0 / jnp.sum(mass[g, rows], axis=1, keepdims=True), (HALF, HD))
            for g in range(GROUP)
        ]
        for h in range(GROUP):
            cols = slice(h * HD, (h + 1) * HD)
            total = mix_ref[h, 0] * (acc[:HALF, cols] * inverse[0])
            for g in range(1, GROUP):
                total = total + mix_ref[h, g] * (acc[g * HALF : (g + 1) * HALF, cols] * inverse[g])
            rms = jnp.sqrt(jnp.mean(total * total, axis=1, keepdims=True) + 1e-05)
            normed[rows, cols] = (total / rms * gain_ref[:, cols]).astype(jnp.bfloat16)

    wo.whole()

    def project_out(step):
        y = lax.rem(at.y + step, 4)
        for far in range(2):
            for side in range(2):
                first = (far * 8 + y * 2 + side) * GROUP * HD
                source = pl.ds(pl.multiple_of(first, GROUP * HD), GROUP * HD)
                piece = jnp.dot(normed[...], wo_buf[source], preferred_element_type=jnp.float32)
                part[y, far, :, side * ROWS : (side + 1) * ROWS] = piece.astype(jnp.bfloat16)

    project_out(2)
    for r in range(4):
        ring_first(r)
    project_out(1)
    project_out(3)
    for r in range(4):
        ring_second(r)
    project_out(0)
    ring_third(0)
    ring_third(1)
    ring_third(2)
    ring_last(0)
    ring_third(3)
    ring_last(1)
    ring_last(2)
    ring_last(3)
    for r in range(4):
        for event in range(5):
            ring_copy(r, event).wait_send()
    for each in (feats, wv, keys, values, wo):
        each.close()


def layer(*operands):
    smem = pl.BlockSpec(memory_space=pltpu.SMEM)
    vmem = pl.BlockSpec(memory_space=pltpu.VMEM)
    hbm = pl.BlockSpec(memory_space=pltpu.HBM)
    width = GROUP * HD
    half = lambda *dims: pltpu.VMEM(dims, jnp.bfloat16)
    full = lambda *dims: pltpu.VMEM(dims, jnp.float32)
    dma = pltpu.SemaphoreType.DMA
    return pl.pallas_call(
        layer_kernel,
        out_shape=jax.ShapeDtypeStruct((ROWS, width), jnp.bfloat16),
        in_specs=[hbm] * 5 + [smem] * 2 + [vmem] * 2,
        out_specs=vmem,
        scratch_shapes=[
            full(ROWS, HD), full(ROWS, HD),
            half(ROWS, TOKENS), half(2 * TOKENS, width), half(TOKENS, width),
            half(HD + TOKENS + 16, width), half(TOKENS, width), half(16 * width, ROWS),
            half(3, ROWS, width), half(ROWS + 16, width), half(16, width),
            full(GROUP, ROWS + 8, HD), full(GROUP, KB + 32, HD),
            half(GROUP, ROWS, CK * HD), half(2, KB, CK * HD),
            full(GROUP, ROWS, HD + TOKENS), full(2 * GROUP, 2, HD + 8, HD),
            full(GROUP * HALF, width),
            full(GROUP, ROWS, HD), full(GROUP, ROWS, HD), half(ROWS, width),
            half(4, 2, ROWS, width),
            half(4, 2, 2, ROWS // 8, width), half(4, 2, 2, ROWS // 4, width), half(4, 2, 2, ROWS // 4, width),
            half(4, ROWS // 4, width), half(4, ROWS // 4, width),
            dma((6,)), dma((6, 18)), dma((1,)), dma((9,)), dma((8,)), dma((2,)), dma((4, 5)), dma((4, 5)),
        ],
        compiler_params=pltpu.CompilerParams(
            collective_id=1, has_side_effects=True, vmem_limit_bytes=67043328
        ),
        name="layer",
    )(*operands)


def per_device(
    activations, positions, w_query, w_key, w_value, conv_kernel, head_mix, out_gain, w_out
):
    return layer(
        activations, w_key, w_value, w_query, w_out, conv_kernel, head_mix,
        positions.reshape(ROWS // HD, HD), out_gain.reshape(1, -1),
    )


def solution(mesh):
    return jax.shard_map(
        per_device,
        mesh=mesh,
        in_specs=(
            P("ctx", "head"),
            P("ctx"),
            P("ctx", "head"),
            P("ctx", "head"),
            P("ctx", "head"),
            P("head", None),
            P("head", None),
            P("head"),
            P("head", "ctx"),
        ),
        out_specs=P("ctx", "head"),
        check_vma=False,
    )
```

```python
import math

import jax
import jax.numpy as jnp
from jax import lax
from jax.experimental import pallas as pl
from jax.experimental.pallas import tpu as pltpu
from jax.sharding import PartitionSpec as P

HD = 128
GROUP = 4
CQ = 6
CK = 11
KB = 512
ROWS = 256
TOKENS = 4096
HALF = 128
BAND = 10


MESH = pl.DeviceIdType.MESH


class Places:
    def __init__(self):
        self.ctx = lax.axis_index("ctx")
        self.head = lax.axis_index("head")
        self.col = lax.div(self.ctx, 8)
        self.z = lax.rem(lax.div(self.ctx, 2), 4)
        self.core = lax.rem(self.ctx, 2)
        self.y = lax.rem(self.head, 4)
        self.far = lax.div(self.head, 4)

    def ctx_at(self, flip_col=False, dz=0, flip_core=False):
        col = 1 - self.col if flip_col else self.col
        core = 1 - self.core if flip_core else self.core
        return col * 8 + lax.rem(self.z + dz + 4, 4) * 2 + core

    def head_at(self, flip=False, dy=0):
        far = 1 - self.far if flip else self.far
        return far * 4 + lax.rem(self.y + dy + 4, 4)


def greet(targets):
    barrier = pltpu.get_barrier_semaphore()
    for target in targets:
        pl.semaphore_signal(barrier, inc=1, device_id=target, device_id_type=MESH)
    return lambda: pl.semaphore_wait(barrier, len(targets))


class Gather:
    def __init__(self, at, own, buf, rows, send, recv, base=0):
        self.at, self.own, self.buf, self.rows, self.send, self.recv = at, own, buf, rows, send, recv
        self.base = base
        self.sib = {"ctx": at.ctx_at(flip_core=True)}
        self.xn = {"ctx": at.ctx_at(flip_col=True)}
        self.up = {"ctx": at.ctx_at(dz=1)}
        self.down = {"ctx": at.ctx_at(dz=-1)}

    def slot(self, index, half=None):
        short = self.rows * 3 // 16
        at, size = {
            None: (0, self.rows), 0: (0, self.rows // 2), 1: (self.rows // 2, self.rows // 2),
            2: (0, self.rows - short), 3: (self.rows - short, short),
        }[half]
        first = self.base + index * self.rows + at
        return self.buf.at[pl.ds(pl.multiple_of(first, 16), size), :]

    def put(self, event, target, src, dst):
        copy = pltpu.make_async_remote_copy(
            src_ref=src, dst_ref=dst, send_sem=self.send, recv_sem=self.recv.at[event],
            device_id=target, device_id_type=MESH,
        )
        copy.start()

    def pass_on(self, event, target, index, half=None):
        piece = self.slot(index, half)
        self.put(event, target, piece, piece)

    def arrive(self, event, index, half=None):
        piece = self.slot(index, half)
        pltpu.make_async_remote_copy(
            src_ref=piece, dst_ref=piece, send_sem=self.send,
            recv_sem=self.recv.at[event], device_id=self.sib, device_id_type=MESH,
        ).wait_recv()

    def first(self):
        dst = self.slot(self.at.ctx)
        self.put(2, self.up, self.own, dst)
        self.put(3, self.down, self.own, dst)
        self.put(1, self.xn, self.own, dst)
        self.put(0, self.sib, self.own, dst)

    def second(self):
        at = self.at
        index = at.ctx_at(flip_col=True)
        self.arrive(1, index)
        self.pass_on(4, self.up, index, 2)
        self.pass_on(5, self.down, index, 2)
        self.pass_on(9, self.sib, index)
        index = at.ctx_at(dz=-1)
        self.arrive(2, index)
        self.pass_on(6, self.up, index, 0)
        self.pass_on(16, self.xn, index, 3)
        self.pass_on(10, self.sib, index)
        index = at.ctx_at(dz=1)
        self.arrive(3, index)
        self.pass_on(7, self.down, index, 1)
        self.pass_on(17, self.xn, index, 3)
        self.pass_on(11, self.sib, index)

    def third(self):
        at = self.at
        index = at.ctx_at(dz=2)
        self.arrive(6, index, 0)
        self.arrive(7, index, 1)
        self.pass_on(8, self.xn, index)
        self.pass_on(14, self.sib, index)
        for event, dz, on in ((4, -1, 12), (5, 1, 13)):
            index = at.ctx_at(flip_col=True, dz=dz)
            self.arrive(event, index, 2)
            self.arrive(event + 12, index, 3)
            self.pass_on(on, self.sib, index)

    def last(self):
        at = self.at
        index = at.ctx_at(flip_col=True, dz=2)
        self.arrive(8, index)
        self.pass_on(15, self.sib, index)

    def from_core(self, pieces):
        for event, flip_col, dz in pieces:
            self.arrive(event, self.at.ctx_at(flip_col=flip_col, dz=dz, flip_core=True))

    def near(self):
        self.from_core(((0, False, 0), (10, False, -1), (12, True, -1)))

    def rest(self):
        self.from_core(((9, True, 0), (11, False, 1), (13, True, 1), (14, False, 2), (15, True, 2)))

    def whole(self):
        self.near()
        self.rest()

    def close(self):
        sent = self.buf.at[pl.ds(self.base, 15 * self.rows), :]
        pltpu.make_async_remote_copy(
            src_ref=sent, dst_ref=sent, send_sem=self.send, recv_sem=self.recv.at[0],
            device_id=self.sib, device_id_type=MESH,
        ).wait_send()


class Features:
    def __init__(self, at, own, buf, send, recv):
        self.at, self.own, self.buf, self.send, self.recv = at, own, buf, send, recv
        self.partner = self.sib = {"head": at.head_at(flip=True)}
        self.up = {"head": at.head_at(dy=1)}
        self.down = {"head": at.head_at(dy=-1)}

    def slot(self, index, half=None):
        cols = pl.ds(pl.multiple_of(index * 512, 512), 512)
        if half is None:
            return self.buf.at[:, cols]
        return self.buf.at[pl.ds(half * (ROWS // 2), ROWS // 2), cols]

    put, pass_on = Gather.put, Gather.pass_on

    def arrive(self, event, index, half=None):
        piece = self.slot(index, half)
        pltpu.make_async_remote_copy(
            src_ref=piece, dst_ref=piece, send_sem=self.send,
            recv_sem=self.recv.at[event], device_id=self.partner, device_id_type=MESH,
        ).wait_recv()

    def first(self):
        dst = self.slot(self.at.head)
        self.put(0, self.partner, self.own, dst)
        self.put(1, self.up, self.own, dst)
        self.put(2, self.down, self.own, dst)

    def second(self):
        at = self.at
        index = at.head_at(flip=True)
        self.arrive(0, index)
        self.pass_on(3, self.up, index)
        self.pass_on(4, self.down, index)
        index = at.head_at(dy=-1)
        self.arrive(1, index)
        self.pass_on(5, self.up, index, 0)
        index = at.head_at(dy=1)
        self.arrive(2, index)
        self.pass_on(6, self.down, index, 1)

    def third(self):
        at = self.at
        index = at.head_at(flip=True, dy=-1)
        self.arrive(3, index)
        self.pass_on(7, self.up, index, 0)
        index = at.head_at(flip=True, dy=1)
        self.arrive(4, index)
        self.pass_on(8, self.down, index, 1)

    def whole(self):
        at = self.at
        for event, flip in ((5, False), (7, True)):
            index = at.head_at(flip=flip, dy=2)
            self.arrive(event, index, 0)
            self.arrive(event + 1, index, 1)

    def close(self):
        sent = self.buf.at[:, : 7 * 512]
        pltpu.make_async_remote_copy(
            src_ref=sent, dst_ref=sent, send_sem=self.send, recv_sem=self.recv.at[0],
            device_id=self.partner, device_id_type=MESH,
        ).wait_send()


def dot_nt(left, right):
    return lax.dot_general(
        left, right, (((1,), (1,)), ((), ())), preferred_element_type=jnp.float32
    )


def layer_kernel(
    x_ref, wk_ref, wv_ref, wq_ref, wo_ref, kern_ref, mix_ref, pos_ref, gain_ref, o_ref,
    cos_ref, sin_ref, x_buf, w_buf, wv_buf, k_buf, v_buf, wo_buf, made, qx, rim_in,
    q32, k32, qt, kc, lg, band, acc, mass, peaks, normed, part,
    y_half, y_sum, y_full, give, got,
    send, recv, x_send, x_recv, here, rim_sems, r_send, r_recv,
):
    at = Places()
    place = at.ctx
    r0 = place * ROWS
    blocks = lax.div(place + 2, 2)
    scale = 1.0 / math.sqrt(HD)
    after = {"ctx": lax.rem(at.ctx + 1, 16)}
    met = greet(
        [{"ctx": at.ctx_at(flip_core=True)}, {"ctx": at.ctx_at(flip_col=True)}]
        + [{"ctx": at.ctx_at(dz=1)}, {"ctx": at.ctx_at(dz=-1)}]
        + [{"head": at.head_at(dy=1)}, {"head": at.head_at(dy=-1)}, {"head": at.head_at(flip=True)}]
        + [after, {"ctx": lax.rem(at.ctx + 15, 16)}]
    )

    def gather(t, own, buf, rows, base=0):
        return Gather(at, own, buf, rows, send.at[t], recv.at[t], base)

    feats = Features(at, x_ref, x_buf, x_send.at[0], x_recv)
    wk = gather(0, wk_ref, w_buf, ROWS)
    wv = gather(1, wv_ref, wv_buf, ROWS)
    wq = gather(2, wq_ref, w_buf, ROWS, TOKENS)
    keys = gather(3, None, k_buf, ROWS, HD)
    values = gather(4, None, v_buf, ROWS)
    wo = gather(5, wo_ref, wo_buf, 2 * ROWS)
    keys.own = keys.slot(at.ctx)
    values.own = values.slot(at.ctx)

    own = [
        pltpu.make_async_copy(x_ref, feats.slot(at.head), here.at[0]),
        pltpu.make_async_copy(wk_ref, wk.slot(at.ctx), here.at[1]),
        pltpu.make_async_copy(wq_ref, wq.slot(at.ctx), here.at[3]),
        pltpu.make_async_copy(wv_ref, wv.slot(at.ctx), here.at[2]),
        pltpu.make_async_copy(wo_ref, wo.slot(at.ctx), here.at[4]),
    ]
    for copy in own:
        copy.start()
    k_buf[:HD] = jnp.zeros((HD, GROUP * HD), jnp.bfloat16)
    k_buf[HD + TOKENS :] = jnp.zeros((16, GROUP * HD), jnp.bfloat16)

    met()
    wk.first()
    feats.first()

    lane = lax.broadcasted_iota(jnp.int32, (HD, HD), 1)
    lower = lane < HD // 2
    exponents = jnp.where(lower, lane, lane - HD // 2).astype(jnp.float32) * (2.0 / HD)
    inverse_rate = jnp.exp(-exponents * math.log(500000.0))
    for t in range(ROWS // HD):
        along = jnp.broadcast_to(pos_ref[t : t + 1].astype(jnp.float32) * 0.25, (HD, HD))
        angle = jnp.transpose(along) * inverse_rate
        sine = jnp.sin(angle)
        cos_ref[t * HD : (t + 1) * HD] = jnp.cos(angle)
        sin_ref[t * HD : (t + 1) * HD] = jnp.where(lower, -sine, sine)

    def project(buf):
        return jnp.dot(x_buf[...], buf[:TOKENS], preferred_element_type=jnp.float32)

    def rotate(projected):
        turned = []
        for h in range(GROUP):
            piece = projected[:, h * HD : (h + 1) * HD]
            turned.append(piece * cos_ref[...] + pltpu.roll(piece, HD // 2, 1) * sin_ref[...])
        return jnp.concatenate(turned, 1)

    def keep(index, value, dst):
        made[index] = value.astype(jnp.bfloat16)
        copy = pltpu.make_async_copy(made.at[index], dst, here.at[5 + index])
        copy.start()
        copy.wait()

    wk.second()
    wq.first()
    feats.second()
    wk.third()
    feats.third()
    wq.second()
    wv.first()
    wk.last()
    for copy in own:
        copy.wait()
    feats.whole()
    wk.whole()
    keep(0, rotate(project(w_buf.at[:TOKENS])), keys.slot(at.ctx))
    wq.third()
    keys.first()
    wv.second()
    wq.last()
    wq.whole()
    keep(2, rotate(project(w_buf.at[TOKENS:])), qx.at[pl.ds(16, ROWS)])
    rim = pltpu.make_async_remote_copy(
        src_ref=qx.at[pl.ds(ROWS, 16)], dst_ref=rim_in,
        send_sem=rim_sems.at[0], recv_sem=rim_sems.at[1], device_id=after, device_id_type=MESH,
    )
    rim.start()
    keys.second()
    wv.third()
    wo.first()
    rim.wait()
    qx[:16] = jnp.where(place > 0, rim_in[...], jnp.zeros_like(rim_in))
    for h in range(GROUP):
        q32[h] = qx[:, h * HD : (h + 1) * HD].astype(jnp.float32)[8:] * scale

    def mix_lags(r, _):
        for h in range(GROUP):
            view = q32.at[h, pl.ds(pl.multiple_of(r * 16, 16), 24)]
            lags = [view[8 - a : 24 - a] for a in range(CQ)]
            for c in range(CK):
                total = kern_ref[h, c] * lags[0]
                for a in range(1, CQ):
                    total = total + kern_ref[h, a * CK + c] * lags[a]
                qt[h, pl.ds(pl.multiple_of(r * 16, 16), 16), c * HD : (c + 1) * HD] = total.astype(
                    jnp.bfloat16
                )
        return 0

    keys.third()
    lax.fori_loop(0, ROWS // 16, mix_lags, 0)
    wv.last()
    keys.last()
    wv.whole()
    keep(1, project(wv_buf), values.slot(at.ctx))
    values.first()
    wo.second()
    keys.near()
    for s in range(2):
        for h in range(GROUP):
            cols = slice(h * HD, (h + 1) * HD)
            near = k_buf[pl.ds(pl.multiple_of(r0 + s * HD, HD), 2 * HD), cols]
            scores = dot_nt(qx[s * HD : s * HD + HD + 16, cols], near)[8:] * scale
            apart = (
                lax.broadcasted_iota(jnp.int32, scores.shape, 0)
                - lax.broadcasted_iota(jnp.int32, scores.shape, 1)
                + (HD - 8)
            )
            kept = jnp.where((apart >= 0) & (apart <= 24), scores, 0.0)
            band[s * GROUP + h, 0] = kept[:, :HD]
            band[s * GROUP + h, 1] = kept[:, HD:]

    def taps(h, lags, width):
        total = None
        for c in range(CK):
            piece = kern_ref[h, c] * lags[0]
            for a in range(1, CQ):
                piece = piece + kern_ref[h, a * CK + c] * lags[a]
            shift = (c - CK // 2) % width
            piece = pltpu.roll(piece, shift, 1) if shift else piece
            total = piece if total is None else total + piece
        return total

    def two_tiles(k, _):
        rows = pl.ds(pl.multiple_of(8 * k, 8), 8)
        for s in range(2):
            for h in range(GROUP):
                views = [
                    band.at[s * GROUP + h, t, pl.ds(pl.multiple_of(8 * k, 8), 16)] for t in range(2)
                ]
                lags = [
                    jnp.concatenate([view[8 - a : 16 - a] for view in views], 1) for a in range(CQ)
                ]
                direct = taps(h, lags, 2 * HD)
                band[s * GROUP + h, 0, rows] = direct[:, :HD]
                band[s * GROUP + h, 1, rows] = direct[:, HD:]
        return 0

    def one_tile(k, _):
        rows = pl.ds(pl.multiple_of(8 * k, 8), 8)
        for s in range(2):
            for h in range(GROUP):
                view = band.at[s * GROUP + h, 1, pl.ds(pl.multiple_of(8 * k, 8), 16)]
                band[s * GROUP + h, 1, rows] = taps(h, [view[8 - a : 16 - a] for a in range(CQ)], HD)
        return 0

    lax.fori_loop(0, 2, two_tiles, 0)
    lax.fori_loop(2, HD // 8, one_tile, 0)
    keys.rest()

    steps = {2: [values.second], 4: [wo.third], 7: [values.third]}

    def block_logits(b, _):
        for when, actions in steps.items():

            @pl.when(b == when)
            def _(actions=actions):
                for action in actions:
                    action()

        @pl.when(b < blocks)
        def _():
            for h in range(GROUP):
                rows = k_buf[pl.ds(pl.multiple_of(HD - 16 + b * KB, 16), KB + 32), h * HD : (h + 1) * HD]
                k32[h] = rows.astype(jnp.float32)
                for c in range(CK):
                    start = 16 + CK // 2 - c
                    kc[h % 2, :, c * HD : (c + 1) * HD] = k32[h, start : start + KB].astype(jnp.bfloat16)
                logits = dot_nt(qt[h], kc[h % 2])
                lg[h, :, pl.ds(pl.multiple_of(HD + b * KB, HD), KB)] = logits
                peak = logits[:, :HD]
                for t in range(1, KB // HD):
                    peak = jnp.maximum(peak, logits[:, t * HD : (t + 1) * HD])
                peaks[h] = jnp.maximum(peaks[h], jnp.where(b < blocks - 2, peak, -jnp.inf))

        return 0

    peaks[...] = jnp.full_like(peaks, -jnp.inf)
    lax.fori_loop(0, 8, block_logits, 0)

    apart = lax.broadcasted_iota(jnp.int32, (HD, HD), 0) - lax.broadcasted_iota(jnp.int32, (HD, HD), 1)
    for s in range(2):
        here_cols = pl.ds(pl.multiple_of(HD + r0 + s * HD, HD), HD)
        prior = pl.ds(pl.multiple_of(r0 + s * HD, HD), HD)
        for h in range(GROUP):
            rows = slice(s * HD, (s + 1) * HD)
            lg[h, rows, here_cols] = jnp.where(
                apart >= BAND,
                lg[h, rows, here_cols],
                jnp.where(apart >= 0, band[s * GROUP + h, 1, :HD], -jnp.inf),
            )
            rows = slice(s * HD, s * HD + 16)
            lg[h, rows, prior] = jnp.where(
                apart[:16] + HD >= BAND, lg[h, rows, prior], band[s * GROUP + h, 0, :16]
            )

    for h in range(GROUP):
        lg[h, :HD, pl.ds(pl.multiple_of(2 * HD + r0, HD), HD)] = jnp.full(
            (HD, HD), -jnp.inf, jnp.float32
        )

    @pl.when(lax.rem(place, 2) == 0)
    def _():
        for h in range(GROUP):
            lg[h, :, pl.ds(pl.multiple_of(3 * HD + r0, HD), ROWS)] = jnp.full(
                (ROWS, ROWS), -jnp.inf, jnp.float32
            )

    values.last()
    for g in range(GROUP):

        def peak_of(b, peak, g=g):
            block = lg[g, :, pl.ds(pl.multiple_of(HD + b * KB, HD), KB)]
            for t in range(KB // HD):
                peak = jnp.maximum(peak, block[:, t * HD : (t + 1) * HD])
            return peak

        peak = lax.fori_loop(jnp.maximum(blocks - 2, 0), blocks, peak_of, peaks[g])
        peaks[g] = jnp.broadcast_to(jnp.max(peak, axis=1, keepdims=True), (ROWS, HD))

    wk.close()
    wq.close()
    mass[...] = jnp.zeros_like(mass)

    def raise_block(b, _):
        for g in range(GROUP):
            for r in range(2):
                rows = slice(r * HALF, (r + 1) * HALF)
                peak = peaks[g, rows]
                total = mass[g, rows]
                first = b * GROUP * ROWS + (r * GROUP + g) * HALF
                for t in range(KB // HD):
                    block = lg[g, rows, pl.ds(pl.multiple_of(HD + b * KB + t * HD, HD), HD)]
                    probs = jnp.exp(block - peak)
                    total = total + probs
                    w_buf[pl.ds(pl.multiple_of(first, HALF), HALF), t * HD : (t + 1) * HD] = probs.astype(
                        jnp.bfloat16
                    )
                mass[g, rows] = total
        return 0

    lax.fori_loop(0, blocks, raise_block, 0)
    wo.last()
    values.whole()

    up = {"head": at.head_at(dy=1)}
    down = {"head": at.head_at(dy=-1)}
    partner = {"head": at.head_at(flip=True)}
    chunk = ROWS // 4
    quarter = chunk // 2
    y_up, y_down, y_far = (lax.rem(at.y + d, 4) for d in (1, 3, 2))

    def ring_copy(r, event):
        target, src, dst = (
            (up, part.at[y_far, :, pl.ds(r * chunk, quarter)], y_half.at[r, 0]),
            (down, part.at[y_far, :, pl.ds(r * chunk + quarter, quarter)], y_half.at[r, 1]),
            (up, y_sum.at[r, 0], y_full.at[r, 0]),
            (down, y_sum.at[r, 1], y_full.at[r, 1]),
            (partner, give.at[r], got.at[r]),
        )[event]
        return pltpu.make_async_remote_copy(
            src_ref=src, dst_ref=dst, send_sem=r_send.at[r, event], recv_sem=r_recv.at[r, event],
            device_id=target, device_id_type=MESH,
        )

    def add(left, right):
        return (left.astype(jnp.float32) + right.astype(jnp.float32)).astype(jnp.bfloat16)

    def ring_first(r):
        ring_copy(r, 0).start()
        ring_copy(r, 1).start()

    def ring_second(r):
        y_sum[r, 0, :, quarter:] = part[y_up, :, r * chunk + quarter : (r + 1) * chunk]
        y_sum[r, 1, :, :quarter] = part[y_down, :, r * chunk : r * chunk + quarter]
        ring_copy(r, 0).wait_recv()
        y_sum[r, 0, :, :quarter] = add(part[y_up, :, r * chunk : r * chunk + quarter], y_half[r, 0])
        ring_copy(r, 2).start()
        ring_copy(r, 1).wait_recv()
        y_sum[r, 1, :, quarter:] = add(part[y_down, :, r * chunk + quarter : (r + 1) * chunk], y_half[r, 1])
        ring_copy(r, 3).start()

    def ring_total(r, far):
        return (
            part[at.y, far, r * chunk : (r + 1) * chunk].astype(jnp.float32)
            + y_full[r, 0, far].astype(jnp.float32)
            + y_full[r, 1, far].astype(jnp.float32)
        )

    def ring_third(r):
        ring_copy(r, 2).wait_recv()
        ring_copy(r, 3).wait_recv()
        give[r] = ring_total(r, 1 - at.far).astype(jnp.bfloat16)
        ring_copy(r, 4).start()

    def ring_last(r):
        mine = ring_total(r, at.far)
        ring_copy(r, 4).wait_recv()
        total = mine + got[r].astype(jnp.float32)
        o_ref[r * chunk : (r + 1) * chunk] = total.astype(jnp.bfloat16)

    acc[...] = jnp.zeros_like(acc)

    def weigh(b, _):
        left = w_buf[pl.ds(pl.multiple_of(b * GROUP * ROWS, GROUP * ROWS), GROUP * ROWS)]
        block = v_buf[pl.ds(pl.multiple_of(b * KB, KB), KB), :]
        acc[...] += jnp.dot(left, block, preferred_element_type=jnp.float32)
        return 0

    lax.fori_loop(0, blocks, weigh, 0)
    for r in range(2):
        rows = slice(r * HALF, (r + 1) * HALF)
        base = r * GROUP * HALF
        inverse = [
            jnp.broadcast_to(1.0 / jnp.sum(mass[g, rows], axis=1, keepdims=True), (HALF, HD))
            for g in range(GROUP)
        ]
        for h in range(GROUP):
            cols = slice(h * HD, (h + 1) * HD)
            total = mix_ref[h, 0] * (acc[base : base + HALF, cols] * inverse[0])
            for g in range(1, GROUP):
                total = total + mix_ref[h, g] * (acc[base + g * HALF : base + (g + 1) * HALF, cols] * inverse[g])
            rms = jnp.sqrt(jnp.mean(total * total, axis=1, keepdims=True) + 1e-05)
            normed[rows, cols] = (total / rms * gain_ref[:, cols]).astype(jnp.bfloat16)

    wo.whole()

    def project_out(step):
        y = lax.rem(at.y + step, 4)
        for far in range(2):
            for side in range(2):
                first = (far * 8 + y * 2 + side) * GROUP * HD
                source = pl.ds(pl.multiple_of(first, GROUP * HD), GROUP * HD)
                piece = jnp.dot(normed[...], wo_buf[source], preferred_element_type=jnp.float32)
                part[y, far, :, side * ROWS : (side + 1) * ROWS] = piece.astype(jnp.bfloat16)

    project_out(2)
    for r in range(4):
        ring_first(r)
    project_out(1)
    project_out(3)
    for r in range(4):
        ring_second(r)
    project_out(0)
    ring_third(0)
    ring_third(1)
    ring_third(2)
    ring_last(0)
    ring_third(3)
    ring_last(1)
    ring_last(2)
    ring_last(3)
    for r in range(4):
        for event in range(5):
            ring_copy(r, event).wait_send()
    for each in (feats, wv, keys, values, wo):
        each.close()


def layer(*operands):
    smem = pl.BlockSpec(memory_space=pltpu.SMEM)
    vmem = pl.BlockSpec(memory_space=pltpu.VMEM)
    hbm = pl.BlockSpec(memory_space=pltpu.HBM)
    width = GROUP * HD
    half = lambda *dims: pltpu.VMEM(dims, jnp.bfloat16)
    full = lambda *dims: pltpu.VMEM(dims, jnp.float32)
    dma = pltpu.SemaphoreType.DMA
    return pl.pallas_call(
        layer_kernel,
        out_shape=jax.ShapeDtypeStruct((ROWS, width), jnp.bfloat16),
        in_specs=[hbm] * 5 + [smem] * 2 + [vmem] * 2,
        out_specs=vmem,
        scratch_shapes=[
            full(ROWS, HD), full(ROWS, HD),
            half(ROWS, TOKENS), half(2 * TOKENS, width), half(TOKENS, width),
            half(HD + TOKENS + 16, width), half(TOKENS, width), half(16 * width, ROWS),
            half(3, ROWS, width), half(ROWS + 16, width), half(16, width),
            full(GROUP, ROWS + 8, HD), full(GROUP, KB + 32, HD),
            half(GROUP, ROWS, CK * HD), half(2, KB, CK * HD),
            full(GROUP, ROWS, HD + TOKENS), full(2 * GROUP, 2, HD + 8, HD),
            full(GROUP * ROWS, width),
            full(GROUP, ROWS, HD), full(GROUP, ROWS, HD), half(ROWS, width),
            half(4, 2, ROWS, width),
            half(4, 2, 2, ROWS // 8, width), half(4, 2, 2, ROWS // 4, width), half(4, 2, 2, ROWS // 4, width),
            half(4, ROWS // 4, width), half(4, ROWS // 4, width),
            dma((6,)), dma((6, 18)), dma((1,)), dma((9,)), dma((8,)), dma((2,)), dma((4, 5)), dma((4, 5)),
        ],
        compiler_params=pltpu.CompilerParams(
            collective_id=1, has_side_effects=True, vmem_limit_bytes=67043328
        ),
        name="layer",
    )(*operands)


def per_device(
    activations, positions, w_query, w_key, w_value, conv_kernel, head_mix, out_gain, w_out
):
    return layer(
        activations, w_key, w_value, w_query, w_out, conv_kernel, head_mix,
        positions.reshape(ROWS // HD, HD), out_gain.reshape(1, -1),
    )


def solution(mesh):
    return jax.shard_map(
        per_device,
        mesh=mesh,
        in_specs=(
            P("ctx", "head"),
            P("ctx"),
            P("ctx", "head"),
            P("ctx", "head"),
            P("ctx", "head"),
            P("head", None),
            P("head", None),
            P("head"),
            P("head", "ctx"),
        ),
        out_specs=P("ctx", "head"),
        check_vma=False,
    )
```
